32 devices in a mesh: fsdp: 8 (over z, x), tensor: 4 (over y, core).
Axes of the slice: x: 2, y: 2, z: 4, core: 2. Of those that a mesh axis runs over, the one named last changes fastest.
Arguments:
- inputs: bfloat16 [16384, 1024], P(('fsdp', 'tensor')), may hold values from -6 to 6
- segments: int32 [16384], P('fsdp'), may hold values from 0 to 303, as said below
- cotangent: bfloat16 [16384, 1024], P(('fsdp', 'tensor')), may hold values from -6 to 6
- attention_gain: float32 [1024], P(('fsdp', 'tensor')), may hold values from 0.5 to 1.5
- attention_shift: float32 [1024], P(('fsdp', 'tensor')), may hold values from -1.8 to 1.8
- feedforward_gain: float32 [1024], P(('fsdp', 'tensor')), may hold values from 0.5 to 1.5
- feedforward_shift: float32 [1024], P(('fsdp', 'tensor')), may hold values from -1.8 to 1.8
- project_weight: bfloat16 [1024, 3072], P('fsdp', 'tensor'), may hold values from -0.1875 to 0.1875
- project_bias: bfloat16 [3072], P(('tensor', 'fsdp')), may hold values from -3 to 3
- dense_weight: bfloat16 [1024, 1024], P(('tensor', 'fsdp')), may hold values from -0.75 to 0.75
- dense_bias: float32 [1024], P(('fsdp', 'tensor')), may hold values from -1.8 to 1.8
- expand_weight: bfloat16 [1024, 4096], P('fsdp', 'tensor'), may hold values from -0.1875 to 0.1875
- expand_bias: bfloat16 [4096], P(('tensor', 'fsdp')), may hold values from -3 to 3
- shrink_weight: bfloat16 [4096, 1024], P(('tensor', 'fsdp')), may hold values from -0.09375 to 0.09375
- shrink_bias: float32 [1024], P(('fsdp', 'tensor')), may hold values from -1.8 to 1.8
Outputs:
- output: bfloat16 [16384, 1024], P(('fsdp', 'tensor'))
- inputs_gradient: bfloat16 [16384, 1024], P(('fsdp', 'tensor'))
- attention_gain_gradient: float32 [1024], P(('fsdp', 'tensor'))
- attention_shift_gradient: float32 [1024], P(('fsdp', 'tensor'))
- feedforward_gain_gradient: float32 [1024], P(('fsdp', 'tensor'))
- feedforward_shift_gradient: float32 [1024], P(('fsdp', 'tensor'))
- project_weight_gradient: float32 [1024, 3072], P('fsdp', 'tensor')
- project_bias_gradient: float32 [3072], P(('tensor', 'fsdp'))
- dense_weight_gradient: float32 [1024, 1024], P(('tensor', 'fsdp'))
- dense_bias_gradient: float32 [1024], P(('fsdp', 'tensor'))
- expand_weight_gradient: float32 [1024, 4096], P('fsdp', 'tensor')
- expand_bias_gradient: float32 [4096], P(('tensor', 'fsdp'))
- shrink_weight_gradient: float32 [4096, 1024], P(('tensor', 'fsdp'))
- shrink_bias_gradient: float32 [1024], P(('fsdp', 'tensor'))
The draws below stay inside these ranges and needn't reach their ends.
Inputs may be any that keep to these rules, and one draw needn't show every extreme that they name: `segments`: within each aligned run of 1024 tokens (one sequence) the nonzero segment numbers never fall and occur in no other run; 0 marks padding, which stands only at the end of a run.
All inputs are finite; a program needn't handle non-finite values.
Results may differ from the reference program's by a relative error of at most 0.012.
Values may be sent and summed in bfloat16 or wider, within the bound.
No kernel may reach another device: no remote copies, remote signals or barrier semaphores. Data moves between devices by JAX's collectives and lax.ppermute only.
A program may use at most 192 MiB of HBM per device.

```python
import math
import jax
import jax.numpy as jnp
from jax import lax

D = 1024
H = 16
HD = 64
ROT = 16
FF = 4096
SEQ_LEN = 1024
TOKENS = 16384


def draw_segments(key, part):
    number = TOKENS // SEQ_LEN
    shortest = max(1, SEQ_LEN // 17)
    longest = max(shortest + 1, SEQ_LEN * 25 // 32)
    most_documents = SEQ_LEN // shortest + 1
    pad_limit = max(1, SEQ_LEN // 20)
    lengths = jax.random.randint(jax.random.fold_in(key, 11), (number, most_documents), shortest, longest + 1)
    ends = jnp.cumsum(lengths, axis=1)
    padding = jax.random.randint(jax.random.fold_in(key, 12), (number, 1), 1, pad_limit + 1)
    places = jnp.arange(SEQ_LEN, dtype=jnp.int32)
    document = jnp.sum((places[None, :, None] >= ends[:, None, :]).astype(jnp.int32), axis=2)
    living = places[None, :] < SEQ_LEN - padding
    last_document = jnp.max(jnp.where(living, document, 0), axis=1, keepdims=True)
    offsets = jnp.arange(number, dtype=jnp.int32)[:, None] * (most_documents + 1)
    numbered = offsets + most_documents - (last_document - document)
    return jnp.where(living, numbered, 0).reshape(TOKENS).astype(jnp.int32)


def spiked(drawn, own_key, source, target, parts, factor):
    owner, partner = [(jnp.arange(drawn.shape[dim]) // (drawn.shape[dim] // parts)).reshape([-1 if axis == dim else 1 for axis in range(drawn.ndim)]) for dim in (source, target)]
    chosen = jax.random.permutation(own_key, parts)[partner]
    strong = (owner == chosen) | (owner == (partner + parts // 2) % parts)
    return jnp.where(strong, factor * drawn, drawn)


def levels(key, shape, pieces, least, largest):
    level = 1.0
    for axis_at, shards_of in pieces:
        heights = jax.random.uniform(jax.random.fold_in(jax.random.fold_in(key, 6), axis_at), (shards_of,), jnp.float32, least / len(pieces), largest / len(pieces))
        level = level * jnp.repeat(jnp.exp(heights), shape[axis_at] // shards_of).reshape((-1,) + (1,) * (len(shape) - 1 - axis_at))
    return level


def scatter_about(stream_key, dims, scale, bound, shards=(), kind=jnp.bfloat16):
    entries = scale * jax.random.normal(stream_key, dims, jnp.float32)
    if shards:
        entries = entries * levels(stream_key, dims, shards, -0.22, 0.18)
    return jnp.clip(entries, -bound, bound).astype(kind)


def bell_draw_with(own_key, extent, scale, bound, split, heavy, kind=jnp.bfloat16):
    values = scale * jax.random.normal(own_key, extent, jnp.float32)
    if split:
        values = values * levels(own_key, extent, split, -0.22, 0.18)
    return jnp.clip(spiked(values, jax.random.fold_in(own_key, 3), *heavy), -bound, bound).astype(kind)


def setup_inputs(seed: int = 0) -> dict:
    key_of = jax.random.split(jax.random.key(seed), 16)
    inputs = bell_draw_with(key_of[0], (TOKENS, D), 1.0, 6.0, ((0, 32),), (0, 1, 32, 2.75))
    segments = draw_segments(jax.random.fold_in(key_of[15], 71), 0)
    cotangent = scatter_about(key_of[2], (TOKENS, D), 1.0, 6.0, ((0, 32),))
    attention_gain = jnp.clip(1.0 + 0.1 * jax.random.normal(key_of[3], (D,), jnp.float32), 0.5, 1.5)
    attention_shift = scatter_about(key_of[4], (D,), 0.3, 1.8, ((0, 32),), jnp.float32)
    feedforward_gain = jnp.clip(1.0 + 0.1 * jax.random.normal(key_of[5], (D,), jnp.float32), 0.5, 1.5)
    feedforward_shift = scatter_about(key_of[6], (D,), 0.3, 1.8, ((0, 32),), jnp.float32)
    project_weight = scatter_about(key_of[7], (D, 3 * D), D ** -0.5, 0.1875, ((0, 8), (1, 4)))
    project_bias = scatter_about(key_of[8], (3 * D,), 0.5, 3.0, ((0, 32),))
    dense_weight = scatter_about(key_of[9], (D, D), (D // 16) ** -0.5, 0.75, ((0, 32),))
    dense_bias = scatter_about(key_of[10], (D,), 0.3, 1.8, ((0, 32),), jnp.float32)
    expand_weight = scatter_about(key_of[11], (D, FF), D ** -0.5, 0.1875, ((0, 8), (1, 4)))
    expand_bias = scatter_about(key_of[12], (FF,), 0.5, 3.0, ((0, 32),))
    shrink_weight = scatter_about(key_of[13], (FF, D), FF ** -0.5, 0.09375, ((0, 32),))
    shrink_bias = scatter_about(key_of[14], (D,), 0.3, 1.8, ((0, 32),), jnp.float32)
    return {"inputs": inputs, "segments": segments, "cotangent": cotangent, "attention_gain": attention_gain, "attention_shift": attention_shift, "feedforward_gain": feedforward_gain, "feedforward_shift": feedforward_shift, "project_weight": project_weight, "project_bias": project_bias, "dense_weight": dense_weight, "dense_bias": dense_bias, "expand_weight": expand_weight, "expand_bias": expand_bias, "shrink_weight": shrink_weight, "shrink_bias": shrink_bias}


EPS = 1e-05
NEGATIVE = -1e+30

@jax.custom_vjp
def low(v):
    return lax.optimization_barrier(v.astype(jnp.bfloat16)).astype(jnp.float32)

@jax.custom_vjp
def low_back(v):
    return v

def low_keep(v):
    return (low(v), None)

def low_pass(kept, grad):
    return (grad,)

def back_keep(v):
    return (v, None)

def back_low(kept, grad):
    return (low(grad),)
low.defvjp(low_keep, low_pass)
low_back.defvjp(back_keep, back_low)

def matmul(left, right):
    return jnp.dot(left, right, precision=lax.Precision.HIGHEST)

def layer_norm(values, gain, shift):
    centre = values - lax.optimization_barrier(jnp.mean(values, axis=-1, keepdims=True))
    spread = lax.optimization_barrier(jnp.mean(centre * centre, axis=-1, keepdims=True))
    return centre * lax.rsqrt(spread + EPS) * gain + shift

def rotary_tables(positions):
    half = ROT // 2
    rates = jnp.exp(jnp.arange(half, dtype=jnp.int32).astype(jnp.float32) * (-2.0 * math.log(10000.0) / ROT))
    angles = positions.astype(jnp.float32)[:, None] * rates[None, :]
    cosine = jnp.concatenate([jnp.cos(angles), jnp.cos(angles)], axis=1)[:, None, :]
    sine = jnp.concatenate([jnp.sin(angles), jnp.sin(angles)], axis=1)[:, None, :]
    return (cosine, sine)

def rotate(vectors, cosine, sine):
    half = ROT // 2
    turned = vectors[..., :ROT]
    swapped = jnp.concatenate([-turned[..., half:], turned[..., :half]], axis=-1)
    return jnp.concatenate([turned * cosine + swapped * sine, vectors[..., ROT:]], axis=-1)

def allowed_mask(labels):
    index = jnp.arange(labels.shape[0], dtype=jnp.int32)
    causal = index[None, :] <= index[:, None]
    same = labels[:, None] == labels[None, :]
    alone = (labels[:, None] != 0) | (index[None, :] == index[:, None])
    return causal & same & alone

def reference(inputs, segments, cotangent, attention_gain, attention_shift, feedforward_gain, feedforward_shift, project_weight, project_bias, dense_weight, dense_bias, expand_weight, expand_bias, shrink_weight, shrink_bias):
    number = TOKENS // SEQ_LEN
    positions = jnp.arange(TOKENS, dtype=jnp.int32) % SEQ_LEN
    cosine, sine = rotary_tables(positions)
    labels = segments.reshape(number, SEQ_LEN)
    scale = 1.0 / math.sqrt(HD)

    def attend(block):
        query, keys, values, marks = block
        scores = low_back(jnp.einsum('qhd,khd->hqk', query, keys, precision=lax.Precision.HIGHEST) * scale)
        scores = jnp.where(allowed_mask(marks)[None], scores, NEGATIVE)
        top = lax.optimization_barrier(jnp.max(scores, axis=-1, keepdims=True))
        probs = jnp.exp(scores - top)
        probs = probs / lax.optimization_barrier(jnp.sum(probs, axis=-1, keepdims=True))
        return jnp.einsum('hqk,khd->qhd', low(probs), values, precision=lax.Precision.HIGHEST)

    def shaped(array):
        return array.reshape(number, SEQ_LEN, H, HD)

    def forward(tokens, gain_one, shift_one, gain_two, shift_two, weight_project, bias_project, weight_dense, bias_dense, weight_expand, bias_expand, weight_shrink, bias_shrink):
        normed_one = low(layer_norm(tokens, gain_one, shift_one))
        normed_two = low(layer_norm(tokens, gain_two, shift_two))
        projected = low_back(matmul(normed_one, weight_project) + bias_project).reshape(TOKENS, H, 3, HD)
        query = low(rotate(projected[:, :, 0], cosine, sine))
        keys = low(rotate(projected[:, :, 1], cosine, sine))
        values = low(projected[:, :, 2])
        mixed = lax.map(jax.checkpoint(attend), (shaped(query), shaped(keys), shaped(values), labels))
        mixed = low(low_back(mixed.reshape(TOKENS, D)))
        hidden = low_back(matmul(normed_two, weight_expand) + bias_expand)
        active = low(jax.nn.gelu(hidden, approximate=False))
        branch = low_back(matmul(mixed, weight_dense) + matmul(active, weight_shrink))
        return tokens + branch + bias_dense + bias_shrink
    floats = [array.astype(jnp.float32) for array in (inputs, attention_gain, attention_shift, feedforward_gain, feedforward_shift, project_weight, project_bias, dense_weight, dense_bias, expand_weight, expand_bias, shrink_weight, shrink_bias)]
    result, pullback = jax.vjp(forward, *floats)
    keep = (segments != 0).astype(jnp.float32)[:, None]
    grads = pullback(cotangent.astype(jnp.float32) * keep)
    return (result.astype(jnp.bfloat16), grads[0].astype(jnp.bfloat16), grads[1], grads[2], grads[3], grads[4], grads[5], grads[6], grads[7], grads[8], grads[9], grads[10], grads[11], grads[12])
```

```python
import math

import jax
import jax.numpy as jnp
from jax import lax
from jax.experimental import pallas as pl
from jax.experimental.pallas import tpu as pltpu
from jax.sharding import PartitionSpec as P

HD = 64
ROT = 16
SEQ_LEN = 1024
EPS = 1e-05
NEGATIVE = -1e30
QB = 256
VMEM_BYTES = 60 * 1024 * 1024
def nt(a,b): return lax.dot_general(a,b,(((1,),(1,)),((),())),preferred_element_type=jnp.float32)
def nn(a,b): return lax.dot_general(a,b,(((1,),(0,)),((),())),preferred_element_type=jnp.float32)

def attention_kernel(x_ref,c_ref,w_ref,b_ref,d_ref,lrow_ref,lcol_ref,cos_ref,up_ref,dn_ref,
                     mixed_ref,pg_ref, q_s,k_s,v_s,g_s,kt_s,vt_s,gt_s,pt_s,dst_s,ot_s,dqt_s,dk_s,dv_s):
    S=x_ref.shape[0]; width=d_ref.shape[0]; pairs=width//128; nb=S//QB
    scale=1.0/math.sqrt(HD)
    cos=cos_ref[...]; up=up_ref[...]; dn=dn_ref[...]
    def rot(u):
        return u*cos + pltpu.roll(u,8,axis=1)*up + pltpu.roll(u,120,axis=1)*dn
    def rot_back(w):
        return w*cos + pltpu.roll(w*up,120,axis=1) + pltpu.roll(w*dn,8,axis=1)
    xv=x_ref[...]
    gv=nt(c_ref[...],d_ref[...])
    for p in range(pairs):
        lo=p*128
        g=gv[:,lo:lo+128]
        g_s[:,lo:lo+128]=g.astype(jnp.bfloat16)
        q=nn(xv,w_ref[:,lo:lo+128])+b_ref[:,lo:lo+128]
        q_s[:,lo:lo+128]=(rot(q).astype(jnp.bfloat16).astype(jnp.float32)*scale).astype(jnp.bfloat16)
        k=nn(xv,w_ref[:,width+lo:width+lo+128])+b_ref[:,width+lo:width+lo+128]
        k_s[:,lo:lo+128]=rot(k).astype(jnp.bfloat16)
        v=nn(xv,w_ref[:,2*width+lo:2*width+lo+128])+b_ref[:,2*width+lo:2*width+lo+128]
        v_s[:,lo:lo+128]=v.astype(jnp.bfloat16)
    lane=lax.broadcasted_iota(jnp.int32,(1,128),1)
    krow=lax.broadcasted_iota(jnp.int32,(QB,QB),0); qcol=lax.broadcasted_iota(jnp.int32,(QB,QB),1)
    tri=krow<=qcol
    for p in range(pairs):
        lo=p*128
        sl=slice(lo,lo+128)
        kt_s[...]=k_s[:,sl].T
        vt_s[...]=v_s[:,sl].T
        gt_s[...]=g_s[:,sl].astype(jnp.float32).T
        for a in range(2):
            half=(lane>=64*a)&(lane<64*a+64)
            hs=slice(64*a,64*a+64)
            for i in range(nb):
                L=(i+1)*QB
                rows=slice(i*QB,L)
                zero=jnp.zeros((),jnp.bfloat16)
                qm=jnp.where(half,q_s[rows,sl],zero)
                gm=jnp.where(half,g_s[rows,sl],zero)
                s=nt(k_s[0:L,sl],qm)
                same=lcol_ref[0:L,:]==lrow_ref[:,rows]
                pieces=[]
                if i: pieces.append(jnp.where(same[:L-QB],s[:L-QB],NEGATIVE))
                pieces.append(jnp.where(same[L-QB:]&tri,s[L-QB:],NEGATIVE))
                s=jnp.concatenate(pieces,axis=0) if i else pieces[0]
                m=jnp.max(s,axis=0,keepdims=True)
                e=jnp.exp(s-m)
                l=jnp.sum(e,axis=0,keepdims=True)
                pr=e*(1.0/l)
                pb=pr.astype(jnp.bfloat16)
                pt_s[0:L,rows]=pb
                ot=nn(vt_s[hs,0:L],pb)
                ot_s[hs,rows]=ot
                dp=nt(v_s[0:L,sl],gm)
                D=jnp.sum(gt_s[hs,rows]*ot,axis=0,keepdims=True)
                ds=(pr*(dp-D)).astype(jnp.bfloat16)
                dst_s[0:L,rows]=ds
                dqt_s[hs,rows]=nn(kt_s[hs,0:L],ds)*scale
            for j in range(nb):
                rows=slice(j*QB,S); out=slice(j*QB,(j+1)*QB)
                qm=jnp.where(half,q_s[rows,sl],zero)
                gm=jnp.where(half,g_s[rows,sl],zero)
                dk=nn(dst_s[out,rows],qm); dv=nn(pt_s[out,rows],gm)
                if a==0:
                    dk_s[out,:]=dk; dv_s[out,:]=dv
                else:
                    dk_s[out,:]+=dk; dv_s[out,:]+=dv
        mixed_ref[:,sl]=ot_s[...].T.astype(jnp.bfloat16)
        pg_ref[:,lo:lo+128]=rot_back(dqt_s[...].T).astype(jnp.bfloat16)
        pg_ref[:,width+lo:width+lo+128]=rot_back(dk_s[...]).astype(jnp.bfloat16)
        pg_ref[:,2*width+lo:2*width+lo+128]=dv_s[...].astype(jnp.bfloat16)

def rotary_rows():
    half=ROT//2
    pos=jnp.arange(SEQ_LEN,dtype=jnp.int32).astype(jnp.float32)
    rates=jnp.exp(jnp.arange(half,dtype=jnp.int32).astype(jnp.float32)*(-2.0*math.log(10000.0)/ROT))
    ang=pos[:,None]*rates[None,:]
    c,s=jnp.cos(ang),jnp.sin(ang)
    one=jnp.ones((SEQ_LEN,HD-ROT),jnp.float32); z8=jnp.zeros((SEQ_LEN,half),jnp.float32); zr=jnp.zeros((SEQ_LEN,HD-ROT),jnp.float32)
    cos=jnp.concatenate([c,c,one]*2,axis=1)
    up=jnp.concatenate([z8,s,zr]*2,axis=1)
    dn=jnp.concatenate([-s,z8,zr]*2,axis=1)
    return cos,up,dn

def attention(xhat,ct,w,b,dense,labels):
    n,S=labels.shape; width=dense.shape[0]; D=xhat.shape[1]
    idx=jnp.arange(S,dtype=jnp.int32)[None,:]
    marks=jnp.where(labels!=0,labels,-1-idx)
    lrow=marks[:,None,:]; lcol=marks[:,:,None]
    cos,up,dn=rotary_rows()
    full=lambda shape: pl.BlockSpec(shape,lambda s:tuple(0 for _ in shape))
    bf=jnp.bfloat16; f32=jnp.float32
    return pl.pallas_call(
        attention_kernel,
        grid=(n,),
        in_specs=[pl.BlockSpec((S,D),lambda s:(s,0)),pl.BlockSpec((S,D),lambda s:(s,0)),
                  full(w.shape),full(b.shape),full(dense.shape),
                  pl.BlockSpec((None,1,S),lambda s:(s,0,0)),pl.BlockSpec((None,S,1),lambda s:(s,0,0)),
                  full(cos.shape),full(cos.shape),full(cos.shape)],
        out_specs=[pl.BlockSpec((S,width),lambda s:(s,0)),pl.BlockSpec((S,3*width),lambda s:(s,0))],
        out_shape=[jax.ShapeDtypeStruct((n*S,width),bf),jax.ShapeDtypeStruct((n*S,3*width),bf)],
        scratch_shapes=[pltpu.VMEM((S,width),bf)]*4+[pltpu.VMEM((128,S),bf)]*2+[pltpu.VMEM((128,S),f32)]
            +[pltpu.VMEM((S,S),bf)]*2+[pltpu.VMEM((128,S),f32)]*2+[pltpu.VMEM((S,128),f32)]*2,
        compiler_params=pltpu.CompilerParams(vmem_limit_bytes=VMEM_BYTES),
        name="attention",
    )(xhat,ct,w,b,dense,lrow,lcol,cos,up,dn)


def exchange(value, axis, size, offset):
    return lax.ppermute(value, axis, [(i, i ^ offset) for i in range(size)])


def sum_over(value, axis, size):
    offset = 1
    while offset < size:
        value = value + exchange(value, axis, size, offset)
        offset *= 2
    return value


def slots(value, index, size):
    row = lax.broadcasted_iota(jnp.int32, (size, 1), 0)
    return jnp.where(row == index, value[None, :], 0.0)


def gather_blocks(block, size):
    far = [block] + [exchange(block, "fsdp", size, 2 * m) for m in range(1, size // 2)]
    blocks = []
    for piece in far:
        blocks += [piece, exchange(piece, "fsdp", size, 1)]
    return blocks


def join_kernel(place_ref, *refs):
    out_ref = refs[-1]
    for k in range(len(refs) - 1):
        rows = refs[k].shape[0]
        start = pl.multiple_of(lax.bitwise_xor(place_ref[0], k) * rows, rows)
        out_ref[pl.ds(start, rows), :] = refs[k][...]


def join_scaled_kernel(place_ref, *refs):
    gain_ref, shift_ref, out_ref, bias_ref = refs[-4:]
    total = None
    for k in range(len(refs) - 4):
        rows = refs[k].shape[0]
        start = pl.multiple_of(lax.bitwise_xor(place_ref[0], k) * rows, rows)
        weight = refs[k][...].astype(jnp.float32)
        part = jnp.sum(weight * shift_ref[pl.ds(start, rows), :], axis=0, keepdims=True)
        total = part if total is None else total + part
        out_ref[pl.ds(start, rows), :] = (weight * gain_ref[pl.ds(start, rows), :]).astype(
            jnp.bfloat16
        )
    bias_ref[...] = total


def join(place, blocks):
    rows, columns = blocks[0].shape
    whole = pl.BlockSpec(memory_space=pltpu.VMEM)
    return pl.pallas_call(
        join_kernel,
        in_specs=[pl.BlockSpec(memory_space=pltpu.SMEM)] + [whole] * len(blocks),
        out_specs=whole,
        out_shape=jax.ShapeDtypeStruct((rows * len(blocks), columns), jnp.bfloat16),
        compiler_params=pltpu.CompilerParams(vmem_limit_bytes=VMEM_BYTES),
        name="join",
    )(place, *blocks)


def join_scaled(place, blocks, gain, shift):
    rows, columns = blocks[0].shape
    whole = pl.BlockSpec(memory_space=pltpu.VMEM)
    return pl.pallas_call(
        join_scaled_kernel,
        in_specs=[pl.BlockSpec(memory_space=pltpu.SMEM)] + [whole] * (len(blocks) + 2),
        out_specs=[whole, whole],
        out_shape=[
            jax.ShapeDtypeStruct((rows * len(blocks), columns), jnp.bfloat16),
            jax.ShapeDtypeStruct((1, columns), jnp.float32),
        ],
        compiler_params=pltpu.CompilerParams(vmem_limit_bytes=VMEM_BYTES),
        name="join_scaled",
    )(place, *blocks, gain[:, None], shift[:, None])


def grads_kernel(place_ref, left_ref, right_ref, near_ref, own_ref):
    product = lax.dot_general(
        left_ref[...],
        right_ref[...],
        (((0,), (0,)), ((), ())),
        preferred_element_type=jnp.float32,
    )
    rows = product.shape[0] // 2
    low, high = product[:rows], product[rows:]
    swap = (place_ref[0] & 1) == 1
    own_ref[...] = jnp.where(swap, high, low).astype(jnp.bfloat16)
    near_ref[...] = jnp.where(swap, low, high).astype(jnp.bfloat16)


def paired_grads(place, left, right, size):
    tokens, rows = left.shape
    columns = right.shape[1]
    pairs = size // 2
    block = rows // size
    return pl.pallas_call(
        grads_kernel,
        grid_spec=pltpu.PrefetchScalarGridSpec(
            num_scalar_prefetch=1,
            grid=(pairs,),
            in_specs=[
                pl.BlockSpec(
                    (tokens, 2 * block),
                    lambda m, place: (
                        0,
                        lax.bitwise_xor(lax.shift_right_logical(place[0], 1), m),
                    ),
                ),
                pl.BlockSpec((tokens, columns), lambda m, place: (0, 0)),
            ],
            out_specs=[pl.BlockSpec((None, block, columns), lambda m, place: (m, 0, 0))] * 2,
        ),
        out_shape=[jax.ShapeDtypeStruct((pairs, block, columns), jnp.bfloat16)] * 2,
        compiler_params=pltpu.CompilerParams(vmem_limit_bytes=VMEM_BYTES),
        name="grads",
    )(place, left, right)


def contract_rows(left, right):
    return lax.dot_general(
        left, right, (((0,), (0,)), ((), ())), preferred_element_type=jnp.float32
    )


def scatter_pairs(near, own, size):
    arrived = exchange(near, "fsdp", size, 1)
    total = own[0].astype(jnp.float32) + arrived[0].astype(jnp.float32)
    for m in range(1, size // 2):
        part = (own[m].astype(jnp.float32) + arrived[m].astype(jnp.float32)).astype(jnp.bfloat16)
        total = total + exchange(part, "fsdp", size, 2 * m).astype(jnp.float32)
    return total


def scattered_grads(place, left, right, size):
    rows = left.shape[1]
    block = rows // size
    if size == 8 and block % 128 == 0:
        near, own = paired_grads(place, left, right, size)
        return scatter_pairs(near, own, size)
    product = contract_rows(left, right)
    if size != 8:
        return lax.psum_scatter(product, "fsdp", scatter_dimension=0, tiled=True)
    parts = product.astype(jnp.bfloat16).reshape(size, block, right.shape[1])
    index = place[0]

    def take(k):
        return lax.dynamic_index_in_dim(parts, lax.bitwise_xor(index, k), 0, keepdims=False)

    near = jnp.stack([take(2 * m + 1) for m in range(size // 2)])
    own = [take(2 * m) for m in range(size // 2)]
    return scatter_pairs(near, own, size)


def gather_rows(place, block, size):
    if size == 8:
        return join(place, gather_blocks(block, size))
    return lax.all_gather(block, "fsdp", axis=0, tiled=True)


def gather_scaled(place, block, gain, shift, size):
    if size == 8:
        return join_scaled(place, gather_blocks(block, size), gain, shift)
    weight = lax.all_gather(block, "fsdp", axis=0, tiled=True).astype(jnp.float32)
    return (weight * gain[:, None]).astype(jnp.bfloat16), jnp.sum(
        weight * shift[:, None], axis=0, keepdims=True
    )


def sequence_rows(value, core):
    other = exchange(value, "tensor", 4, 2)
    pieces = []
    for part in (value, other):
        partner = exchange(part, "tensor", 4, 1)
        pieces.append(jnp.where(core == 0, part, partner))
        pieces.append(jnp.where(core == 0, partner, part))
    return jnp.concatenate(pieces, axis=0)


def owner_rows(value, core, rows):
    def half(start, which):
        return lax.dynamic_slice_in_dim(value, start + which * rows, rows, 0)

    far = exchange(half(2 * rows, 1 - core), "tensor", 4, 1)
    near = exchange(half(0, 1 - core), "tensor", 4, 1)
    far = (half(2 * rows, core).astype(jnp.float32) + far.astype(jnp.float32)).astype(jnp.bfloat16)
    far = exchange(far, "tensor", 4, 2)
    return (
        half(0, core).astype(jnp.float32) + near.astype(jnp.float32) + far.astype(jnp.float32)
    )


def normalise(features):
    centre = features - jnp.mean(features, axis=-1, keepdims=True)
    rate = lax.rsqrt(jnp.mean(centre * centre, axis=-1, keepdims=True) + EPS)
    return centre * rate, rate


def by_part(array):
    shape = array.shape
    array = array.reshape(shape[:-1] + (shape[-1] // (3 * HD), 3, HD))
    return jnp.swapaxes(array, -3, -2).reshape(shape)


def by_head(array):
    shape = array.shape
    array = array.reshape(shape[:-1] + (3, shape[-1] // (3 * HD), HD))
    return jnp.swapaxes(array, -3, -2).reshape(shape)


def local(
    inputs,
    segments,
    cotangent,
    attention_gain,
    attention_shift,
    feedforward_gain,
    feedforward_shift,
    project_weight,
    project_bias,
    dense_weight,
    dense_bias,
    expand_weight,
    expand_bias,
    shrink_weight,
    shrink_bias,
):
    f32, bf16 = jnp.float32, jnp.bfloat16
    size = lax.axis_size("fsdp")
    across = lax.axis_size("tensor")
    rows, width = inputs.shape
    assert across == 4 and 2 * rows == SEQ_LEN and segments.shape[0] == 2 * SEQ_LEN
    index = lax.axis_index("fsdp")
    rank = lax.axis_index("tensor")
    core = rank % 2
    chip = rank // 2
    place = index.astype(jnp.int32)[None]
    block = width // size

    features = inputs.astype(f32)
    normed_own, rate = normalise(features)
    own_labels = lax.dynamic_slice_in_dim(segments, rank * rows, rows, 0)
    upstream = cotangent.astype(f32) * (own_labels != 0).astype(f32)[:, None]

    small = jnp.concatenate(
        [
            attention_gain,
            attention_shift,
            feedforward_gain,
            feedforward_shift,
            dense_bias + shrink_bias,
        ]
    )
    piece = small.shape[0] // 5
    small = sum_over(slots(small, rank, across), "tensor", across)
    own_vectors = jnp.swapaxes(small.reshape(across, 5, piece), 0, 1).reshape(5, block)
    counts = (5 * block, project_bias.shape[0], expand_bias.shape[0])
    packed = jnp.concatenate(
        [own_vectors.reshape(-1), project_bias.astype(f32), expand_bias.astype(f32)]
    )
    packed = sum_over(slots(packed, index, size), "fsdp", size)
    vectors = jnp.swapaxes(packed[:, : counts[0]].reshape(size, 5, block), 0, 1).reshape(5, width)
    project_offset = by_part(packed[:, counts[0] : counts[0] + counts[1]].reshape(-1))
    expand_offset = packed[:, counts[0] + counts[1] :].reshape(-1)
    gain_one, shift_one, gain_two, shift_two, out_bias = vectors

    normed = sequence_rows(normed_own.astype(bf16), core)
    expand_local, expand_extra = gather_scaled(place, expand_weight, gain_two, shift_two, size)
    branch_grad = sequence_rows(upstream.astype(bf16), core)
    shrink_local = gather_rows(place, shrink_weight, size)
    project_local, project_extra = gather_scaled(
        place, by_part(project_weight), gain_one, shift_one, size
    )
    dense_local = gather_rows(place, dense_weight, size)

    hidden = jnp.dot(normed, expand_local, preferred_element_type=f32) + (
        expand_offset[None, :] + expand_extra
    )
    phi = 0.5 * (1.0 + lax.erf(hidden * (1.0 / math.sqrt(2.0))))
    active = (hidden * phi).astype(bf16)
    slope = phi + hidden * (jnp.exp(-0.5 * hidden * hidden) * (1.0 / math.sqrt(2.0 * math.pi)))
    shrink_sum = scattered_grads(place, active, branch_grad, size)
    hidden_grad = (nt(branch_grad, shrink_local) * slope).astype(bf16)
    expand_sum = scattered_grads(place, normed, hidden_grad, size)
    expand_offset_grad = jnp.sum(hidden_grad.astype(f32), axis=0)
    bias_grad = jnp.sum(branch_grad.astype(f32), axis=0)

    labels = segments.reshape(2, SEQ_LEN)
    labels = jnp.where(chip == 0, labels, labels[::-1])
    mixed, projected_grad = attention(
        normed,
        branch_grad,
        project_local,
        project_offset[None, :] + project_extra,
        dense_local,
        labels,
    )
    dense_sum = scattered_grads(place, mixed, branch_grad, size)
    project_sum = scattered_grads(place, normed, projected_grad, size)
    project_offset_grad = jnp.sum(projected_grad.astype(f32), axis=0)

    branch = (nn(mixed, dense_local) + nn(active, shrink_local)).astype(bf16)
    branch = owner_rows(branch, core, rows)
    output = (features + branch + out_bias[None, :]).astype(bf16)

    normed_grad = (nt(projected_grad, project_local) + nt(hidden_grad, expand_local)).astype(bf16)
    normed_grad = owner_rows(normed_grad, core, rows)
    inner = jnp.mean(normed_grad * normed_own, axis=-1, keepdims=True)
    centre = jnp.mean(normed_grad, axis=-1, keepdims=True)
    inputs_gradient = (upstream + rate * (normed_grad - centre - normed_own * inner)).astype(bf16)

    totals = sum_over(
        jnp.concatenate([project_offset_grad, expand_offset_grad, bias_grad])[None, :],
        "fsdp",
        size,
    )[0]
    wide = project_offset_grad.shape[0]
    hidden_units = expand_offset_grad.shape[0]
    project_totals = totals[:wide]
    expand_totals = totals[wide : wide + hidden_units]
    bias_totals = totals[wide + hidden_units :]

    def mine(vector, count, start):
        return lax.dynamic_slice_in_dim(vector, start * count, count, 0)

    own_project = by_part(project_weight).astype(f32)
    own_expand = expand_weight.astype(f32)
    partial = jnp.stack(
        [
            jnp.sum(own_project * project_sum, axis=1),
            jnp.sum(own_project * project_totals[None, :], axis=1),
            jnp.sum(own_expand * expand_sum, axis=1),
            jnp.sum(own_expand * expand_totals[None, :], axis=1),
        ]
    )
    partial = sum_over(partial, "tensor", across)
    partial = lax.dynamic_slice_in_dim(partial, rank * piece, piece, 1)
    project_gradient = own_vectors[0][:, None] * project_sum + (
        own_vectors[1][:, None] * project_totals[None, :]
    )
    expand_gradient = own_vectors[2][:, None] * expand_sum + (
        own_vectors[3][:, None] * expand_totals[None, :]
    )
    bias_sum = mine(bias_totals, piece, index * across + rank)
    return (
        output,
        inputs_gradient,
        partial[0],
        partial[1],
        partial[2],
        partial[3],
        by_head(project_gradient),
        mine(by_head(project_totals), project_bias.shape[0], index),
        dense_sum,
        bias_sum,
        expand_gradient,
        mine(expand_totals, expand_bias.shape[0], index),
        shrink_sum,
        bias_sum,
    )


def solution(mesh):
    in_specs = (
        P(("fsdp", "tensor"), None),
        P("fsdp"),
        P(("fsdp", "tensor"), None),
        P(("fsdp", "tensor")),
        P(("fsdp", "tensor")),
        P(("fsdp", "tensor")),
        P(("fsdp", "tensor")),
        P("fsdp", "tensor"),
        P(("tensor", "fsdp")),
        P(("tensor", "fsdp"), None),
        P(("fsdp", "tensor")),
        P("fsdp", "tensor"),
        P(("tensor", "fsdp")),
        P(("tensor", "fsdp"), None),
        P(("fsdp", "tensor")),
    )
    out_specs = (
        P(("fsdp", "tensor"), None),
        P(("fsdp", "tensor"), None),
        P(("fsdp", "tensor")),
        P(("fsdp", "tensor")),
        P(("fsdp", "tensor")),
        P(("fsdp", "tensor")),
        P("fsdp", "tensor"),
        P(("tensor", "fsdp")),
        P(("tensor", "fsdp"), None),
        P(("fsdp", "tensor")),
        P("fsdp", "tensor"),
        P(("tensor", "fsdp")),
        P(("tensor", "fsdp"), None),
        P(("fsdp", "tensor")),
    )
    return jax.shard_map(local, mesh=mesh, in_specs=in_specs, out_specs=out_specs, check_vma=False)
```

```python
import functools
import math

import jax
import jax.numpy as jnp
from jax import lax
from jax.experimental import pallas as pl
from jax.experimental.pallas import tpu as pltpu
from jax.sharding import PartitionSpec as P

HD = 64
ROT = 16
SEQ_LEN = 1024
EPS = 1e-05
NEGATIVE = -1e30
QB = 256
CHUNK = 128
PARAMS = pltpu.CompilerParams(vmem_limit_bytes=60 * 1024 * 1024)
BF16 = jnp.bfloat16
F32 = jnp.float32
COST = 1.0
VMEM = pl.BlockSpec(memory_space=pltpu.VMEM)
SMEM = pl.BlockSpec(memory_space=pltpu.SMEM)
ANY = pl.BlockSpec(memory_space=pl.ANY)


def shape_of(dims, kind=BF16):
    return jax.ShapeDtypeStruct(dims, kind)


def cost(flops, moved):
    return pl.CostEstimate(
        flops=int(flops * COST), bytes_accessed=int(moved * COST), transcendentals=0
    )


def nn(left, right):
    return lax.dot_general(left, right, (((1,), (0,)), ((), ())), preferred_element_type=F32)


def nt(left, right):
    return lax.dot_general(left, right, (((1,), (1,)), ((), ())), preferred_element_type=F32)


def tn(left, right):
    return lax.dot_general(left, right, (((0,), (0,)), ((), ())), preferred_element_type=F32)


def copies(pairs, sems, first=0):
    made = [pltpu.make_async_copy(s, d, sems.at[first + i]) for i, (s, d) in enumerate(pairs)]
    for copy in made:
        copy.start()
    return made


def pack_kernel(project_ref, dense_ref, shrink_ref, turns_ref, out_ref, cos_ref, up_ref, dn_ref):
    heads = project_ref.shape[1] // (3 * HD)
    rows = dense_ref.shape[0]
    width = heads * HD
    out_ref[0] = shrink_ref[...]
    for part in range(3):
        pieces = [
            project_ref[:, (3 * head + part) * HD : (3 * head + part + 1) * HD]
            for head in range(heads)
        ]
        out_ref[1, :, part * width : (part + 1) * width] = jnp.concatenate(pieces, axis=1)
    for j in range(4):
        columns = slice(j * width, (j + 1) * width)
        out_ref[1, j * rows : (j + 1) * rows, 3 * width :] = dense_ref[:, columns]
    half = ROT // 2
    length = turns_ref.shape[0]
    cosine, sine = turns_ref[:, :half], turns_ref[:, half:]
    rest = jnp.zeros((length, HD - ROT), F32)
    none = jnp.zeros((length, half), F32)
    cos_ref[...] = jnp.concatenate([cosine, cosine, rest + 1.0] * 2, axis=1)
    up_ref[...] = jnp.concatenate([none, sine, rest] * 2, axis=1)
    dn_ref[...] = jnp.concatenate([-sine, none, rest] * 2, axis=1)


def pack(project, dense, shrink, turns):
    table = shape_of((turns.shape[0], 2 * HD), F32)
    return pl.pallas_call(
        pack_kernel,
        in_specs=[VMEM] * 4,
        out_specs=[VMEM] * 4,
        out_shape=[shape_of((2,) + shrink.shape)] + [table] * 3,
        compiler_params=PARAMS,
        cost_estimate=cost(0, 3 << 20),
        name="pack",
    )(project, dense, shrink, turns)


def column(row):
    return jnp.broadcast_to(row, (8, row.shape[1])).T[:, :1]


def shift_times(shift, weight):
    high = shift.astype(BF16)
    rest = shift - high.astype(F32)
    middle = rest.astype(BF16)
    low = (rest - middle.astype(F32)).astype(BF16)
    parts = nn(jnp.concatenate([high, middle, low], axis=0), weight)
    return jnp.sum(parts, axis=0, keepdims=True)


def scaled_rows(place, k, weight, gain_ref, shift_ref):
    rows = weight.shape[0]
    start = pl.multiple_of(lax.bitwise_xor(place, k) * rows, rows)
    part = shift_times(shift_ref[:, pl.ds(start, rows)], weight)
    gain = column(gain_ref[:, pl.ds(start, rows)])
    return start, (weight.astype(F32) * gain).astype(BF16), part


def block_list(refs):
    own, near, far, far_near, pair, pair_near = refs
    return [own, near, pair.at[0], pair_near.at[0], far, far_near, pair.at[1], pair_near.at[1]]


def join_rest_kernel(place_ref, *refs):
    gain_ref, shift_ref, offset_ref, shrink_ref, project_ref, dense_ref, bias_ref = refs[6:]
    total = offset_ref[...]
    wide = project_ref.shape[1]
    for k, ref in enumerate(block_list(refs[:6])):
        block = ref[1]
        start, scaled, part = scaled_rows(
            place_ref[0], k, block[:, :wide], gain_ref, shift_ref
        )
        shrink_ref[pl.ds(start, block.shape[0]), :] = ref[0]
        project_ref[pl.ds(start, block.shape[0]), :] = scaled
        total = total + part
        rows = block.shape[0] // 4
        across = block.shape[1] // 4
        base = pl.multiple_of(lax.bitwise_xor(place_ref[0], k) * rows, rows)
        for j in range(4):
            dense_ref[pl.ds(base, rows), j * across : (j + 1) * across] = block[
                j * rows : (j + 1) * rows, wide:
            ]
    bias_ref[...] = total


def join_rest(place, blocks, gain, shift, offset):
    _, rows, columns = blocks[0].shape
    total = 8 * rows
    wide = offset.shape[1]
    return pl.pallas_call(
        join_rest_kernel,
        in_specs=[SMEM] + [VMEM] * 9,
        out_specs=[VMEM] * 4,
        out_shape=[
            shape_of((total, columns)),
            shape_of((total, wide)),
            shape_of((total // 4, columns)),
            shape_of((1, wide), F32),
        ],
        compiler_params=PARAMS,
        cost_estimate=cost(1e9, 10 << 20),
        name="join_rest",
    )(place, *blocks, gain, shift, offset)


def join_expand_kernel(place_ref, *refs):
    gain_ref, shift_ref, offset_ref, out_ref, bias_ref = refs[6:]
    total = offset_ref[...]
    for k, ref in enumerate(block_list(refs[:6])):
        start, scaled, part = scaled_rows(place_ref[0], k, ref[...], gain_ref, shift_ref)
        out_ref[pl.ds(start, scaled.shape[0]), :] = scaled
        total = total + part
    bias_ref[...] = total


def join_expand(place, blocks, gain, shift, offset):
    rows, columns = blocks[0].shape
    return pl.pallas_call(
        join_expand_kernel,
        in_specs=[SMEM] + [VMEM] * 9,
        out_specs=[VMEM] * 2,
        out_shape=[shape_of((8 * rows, columns)), shape_of((1, columns), F32)],
        compiler_params=PARAMS,
        cost_estimate=cost(1e9, 6 << 20),
        name="join_expand",
    )(place, *blocks, gain, shift, offset)


def normalise(features):
    centre = features - jnp.mean(features, axis=-1, keepdims=True)
    rate = lax.rsqrt(jnp.mean(centre * centre, axis=-1, keepdims=True) + EPS)
    return centre * rate, rate


def prepare_kernel(inputs_ref, cotangent_ref, keep_ref, both_ref, sum_ref):
    both_ref[0] = normalise(inputs_ref[...].astype(F32))[0].astype(BF16)
    upstream = cotangent_ref[...].astype(F32) * keep_ref[...]
    both_ref[1] = upstream.astype(BF16)
    sum_ref[...] = jnp.sum(upstream, axis=0, keepdims=True)


def prepare(inputs, cotangent, keep):
    return pl.pallas_call(
        prepare_kernel,
        in_specs=[VMEM] * 3,
        out_specs=[VMEM] * 2,
        out_shape=[shape_of((2,) + inputs.shape), shape_of((1, inputs.shape[1]), F32)],
        compiler_params=PARAMS,
        cost_estimate=cost(0, 6 << 20),
        name="prepare",
    )(inputs, cotangent, keep)


def attention_kernel(
    core_ref,
    first_ref,
    second_ref,
    w_ref,
    b_ref,
    d_ref,
    lrow_ref,
    cos_ref,
    up_ref,
    dn_ref,
    mixed_ref,
    pg_ref,
    sum_ref,
    q_s,
    k_s,
    v_s,
    g_s,
    kt_s,
    vt_s,
    gt_s,
    pt_s,
    dst_s,
    ot_s,
    dqt_s,
    dk_s,
    dv_s,
    out_s,
    scores_s,
    qm_s,
    gm_s,
    lcol_s,
):
    half_rows = first_ref.shape[1]
    length = 2 * half_rows
    width = d_ref.shape[0]
    blocks = length // QB
    scale = 1.0 / math.sqrt(HD)

    def starts(piece):
        return pl.multiple_of(lax.bitwise_xor(core_ref[0], piece) * half_rows, half_rows)

    for piece, ref in enumerate((first_ref, second_ref)):
        rows = pl.ds(starts(piece), half_rows)
        cos, up, dn = cos_ref[rows, :], up_ref[rows, :], dn_ref[rows, :]

        def rotate(u):
            return u * cos + pltpu.roll(u, 8, axis=1) * up + pltpu.roll(u, 120, axis=1) * dn

        tokens = ref[0]
        g_s[rows, :] = nt(ref[1], d_ref[...]).astype(BF16)
        q = nn(tokens, w_ref[:, :width]) + b_ref[:, :width]
        k = nn(tokens, w_ref[:, width : 2 * width]) + b_ref[:, width : 2 * width]
        for lo in range(0, width, 128):
            sl = slice(lo, lo + 128)
            turned = rotate(q[:, sl]).astype(BF16).astype(F32)
            q_s[rows, sl] = (turned * scale).astype(BF16)
            k_s[rows, sl] = rotate(k[:, sl]).astype(BF16)
        v_s[rows, :] = (nn(tokens, w_ref[:, 2 * width :]) + b_ref[:, 2 * width :]).astype(BF16)

    cos, up, dn = cos_ref[...], up_ref[...], dn_ref[...]

    def rotate_back(w):
        return w * cos + pltpu.roll(w * up, 120, axis=1) + pltpu.roll(w * dn, 8, axis=1)

    lane = lax.broadcasted_iota(jnp.int32, (1, 128), 1)
    zero = jnp.zeros((), BF16)
    lcol_s[...] = column(lrow_ref[...])

    def folded_rows(value, fold):
        return fold(value.reshape(value.shape[0] // 8, 8, value.shape[1]), axis=0)

    def pair(p, carry):
        lo = pl.multiple_of(p * 128, 128)
        sl = pl.ds(lo, 128)
        kt_s[...] = k_s[:, sl].T
        vt_s[...] = v_s[:, sl].T
        gt_s[...] = g_s[:, sl].astype(F32).T
        for a in range(2):
            half = (lane >= HD * a) & (lane < HD * (a + 1))
            qm_s[a] = jnp.where(half, q_s[:, sl], zero)
            gm_s[a] = jnp.where(half, g_s[:, sl], zero)
        for i in range(blocks):
            for a in range(2):
                hs = slice(HD * a, HD * (a + 1))
                end = (i + 1) * QB
                rows = slice(i * QB, end)
                qm = qm_s[a, rows, :]
                gm = gm_s[a, rows, :]
                chunks = [slice(c, c + CHUNK) for c in range(0, end, CHUNK)]
                top = None
                for cs in chunks:
                    s = nt(k_s[cs, sl], qm)
                    same = lcol_s[cs, :] == lrow_ref[:, rows]
                    if cs.start >= i * QB:
                        key = lax.broadcasted_iota(jnp.int32, (CHUNK, QB), 0)
                        query = lax.broadcasted_iota(jnp.int32, (CHUNK, QB), 1)
                        same = same & (key + (cs.start - i * QB) <= query)
                    s = jnp.where(same, s, NEGATIVE)
                    scores_s[a, cs, :] = s
                    part = folded_rows(s, jnp.max)
                    top = part if top is None else jnp.maximum(top, part)
                top = jnp.max(top, axis=0, keepdims=True)
                total = None
                for cs in chunks:
                    e = jnp.exp(scores_s[a, cs, :] - top)
                    scores_s[a, cs, :] = e
                    part = folded_rows(e, jnp.sum)
                    total = part if total is None else total + part
                rate = 1.0 / jnp.sum(total, axis=0, keepdims=True)
                for cs in chunks:
                    pt_s[a, cs, rows] = (scores_s[a, cs, :] * rate).astype(BF16)
                out = nn(vt_s[hs, 0:end], pt_s[a, 0:end, rows])
                ot_s[hs, rows] = out
                inner = jnp.sum(gt_s[hs, rows] * out, axis=0, keepdims=True)
                for cs in chunks:
                    dp = nt(v_s[cs, sl], gm) - inner
                    dst_s[a, cs, rows] = (scores_s[a, cs, :] * rate * dp).astype(BF16)
                dqt_s[hs, rows] = nn(kt_s[hs, 0:end], dst_s[a, 0:end, rows]) * scale
        for j in range(blocks):
            rows = slice(j * QB, length)
            out = slice(j * QB, (j + 1) * QB)
            dk_s[out, :] = nn(dst_s[0, out, rows], qm_s[0, rows, :]) + nn(
                dst_s[1, out, rows], qm_s[1, rows, :]
            )
            dv_s[out, :] = nn(pt_s[0, out, rows], gm_s[0, rows, :]) + nn(
                pt_s[1, out, rows], gm_s[1, rows, :]
            )

        def put(at, values):
            cols = pl.ds(pl.multiple_of(at + lo, 128), 128)
            values = values.astype(BF16)
            sum_ref[:, cols] = jnp.sum(values.astype(F32), axis=0, keepdims=True)
            out_s[...] = values
            for piece in range(2):
                pg_ref[piece, :, cols] = out_s[pl.ds(starts(piece), half_rows), :]

        put(0, rotate_back(dqt_s[...].T))
        put(width, rotate_back(dk_s[...]))
        put(2 * width, dv_s[...])
        out_s[...] = ot_s[...].T.astype(BF16)
        for piece in range(2):
            mixed_ref[piece, :, sl] = out_s[pl.ds(starts(piece), half_rows), :]
        return carry

    lax.fori_loop(0, width // 128, pair, 0)


def attention(core, parts, w, b, dense, marks, tables):
    half_rows = parts[0].shape[1]
    length = 2 * half_rows
    width = dense.shape[0]
    return pl.pallas_call(
        attention_kernel,
        in_specs=[SMEM] + [VMEM] * 9,
        out_specs=[VMEM] * 3,
        out_shape=[
            shape_of((2, half_rows, width)),
            shape_of((2, half_rows, 3 * width)),
            shape_of((1, 3 * width), F32),
        ],
        scratch_shapes=[pltpu.VMEM((length, width), BF16)] * 4
        + [pltpu.VMEM((128, length), BF16)] * 2
        + [pltpu.VMEM((128, length), F32)]
        + [pltpu.VMEM((2, length, length), BF16)] * 2
        + [pltpu.VMEM((128, length), F32)] * 2
        + [pltpu.VMEM((length, 128), F32)] * 2
        + [pltpu.VMEM((length, 128), BF16)]
        + [pltpu.VMEM((2, length, QB), F32)]
        + [pltpu.VMEM((2, length, 128), BF16)] * 2
        + [pltpu.VMEM((length, 1), jnp.int32)],
        compiler_params=PARAMS,
        cost_estimate=cost(2.3e10, 8 << 20),
        name="attention",
    )(core, *parts, w, b, dense, marks[None, :], *tables)


def rotary_turns():
    half = ROT // 2
    places = jnp.arange(SEQ_LEN, dtype=jnp.int32).astype(F32)
    rates = jnp.exp(
        jnp.arange(half, dtype=jnp.int32).astype(F32) * (-2.0 * math.log(10000.0) / ROT)
    )
    angles = places[:, None] * rates[None, :]
    return jnp.concatenate([jnp.cos(angles), jnp.sin(angles)], axis=1)


def turn(slot):
    return 2 * (slot % 2) + slot // 2


def put_pair(place_ref, m, product, near_s, own_s, columns=slice(None)):
    rows = product.shape[0] // 2
    low, high = product[:rows], product[rows:]
    swap = (place_ref[0] & 1) == 1
    own_s[m, :, columns] = jnp.where(swap, high, low).astype(BF16)
    near_s[m, :, columns] = jnp.where(swap, low, high).astype(BF16)


def pair_rows(place_ref, m, width):
    other = lax.bitwise_xor(lax.shift_right_logical(place_ref[0], 1), turn(m))
    return pl.ds(pl.multiple_of(other * width, width), width)


def loaded(parts, held, sems, first, which=None):
    if which is not None:
        parts = [ref.at[which] for ref in parts]
    rows = parts[0].shape[0]
    return copies(
        [(ref, held.at[pl.ds(p * rows, rows), :]) for p, ref in enumerate(parts)], sems, first
    )


def hidden_kernel(
    a_ref,
    b_ref,
    c_ref,
    d_ref,
    w_ref,
    bias_ref,
    act_ref,
    slope_ref,
    tokens_s,
    w_s,
    act_s,
    slope_s,
    in_sems,
    out_sems,
):
    rows = a_ref.shape[1]
    loads = copies([(w_ref, w_s)], in_sems)
    loads += loaded((a_ref, b_ref, c_ref, d_ref), tokens_s, in_sems, 1, 0)
    loads[0].wait()
    stores = []
    for p in range(4):
        loads[1 + p].wait()
        at = pl.ds(p * rows, rows)
        hidden = nn(tokens_s[at, :], w_s[...]) + bias_ref[...]
        phi = 0.5 * (1.0 + lax.erf(hidden * (1.0 / math.sqrt(2.0))))
        act_s[at, :] = (hidden * phi).astype(BF16)
        bell = jnp.exp(-0.5 * hidden * hidden) * (1.0 / math.sqrt(2.0 * math.pi))
        slope_s[at, :] = (phi + hidden * bell).astype(BF16)
        stores += copies(
            [(act_s.at[at, :], act_ref.at[at, :]), (slope_s.at[at, :], slope_ref.at[at, :])],
            out_sems,
            2 * p,
        )
    for copy in stores:
        copy.wait()


def hidden_layer(parts, w, bias):
    _, rows, width = parts[0].shape
    units = w.shape[1]
    return pl.pallas_call(
        hidden_kernel,
        in_specs=[ANY] * 5 + [VMEM],
        out_specs=[ANY] * 2,
        out_shape=[shape_of((4 * rows, units))] * 2,
        scratch_shapes=[pltpu.VMEM((4 * rows, width), BF16), pltpu.VMEM(w.shape, BF16)]
        + [pltpu.VMEM((4 * rows, units), BF16)] * 2
        + [pltpu.SemaphoreType.DMA((5,)), pltpu.SemaphoreType.DMA((8,))],
        compiler_params=PARAMS,
        cost_estimate=cost(6e9, 14 << 20),
        name="hidden",
    )(*parts, w, bias)


def shrink_grads_kernel(
    place_ref, act_ref, a_ref, b_ref, c_ref, d_ref, near_ref, own_ref, grads_s, in_sems
):
    m = pl.program_id(0)

    @pl.when(m == 0)
    def _():
        for copy in loaded((a_ref, b_ref, c_ref, d_ref), grads_s, in_sems, 0, 1):
            copy.wait()

    product = tn(act_ref[...], grads_s[...])
    rows = product.shape[0] // 2
    low, high = product[:rows], product[rows:]
    swap = (place_ref[0] & 1) == 1
    own_ref[...] = jnp.where(swap, high, low).astype(BF16)
    near_ref[...] = jnp.where(swap, low, high).astype(BF16)


def shrink_grads(place, active, parts, pairs):
    _, rows, width = parts[0].shape
    units = active.shape[1]
    block = units // (2 * pairs)
    return pl.pallas_call(
        shrink_grads_kernel,
        grid_spec=pltpu.PrefetchScalarGridSpec(
            num_scalar_prefetch=1,
            grid=(pairs,),
            in_specs=[
                pl.BlockSpec(
                    (4 * rows, 2 * block),
                    lambda m, place: (
                        0,
                        lax.bitwise_xor(lax.shift_right_logical(place[0], 1), turn(m)),
                    ),
                )
            ]
            + [ANY] * 4,
            out_specs=[pl.BlockSpec((None, block, width), lambda m, place: (m, 0, 0))] * 2,
            scratch_shapes=[
                pltpu.VMEM((4 * rows, width), BF16),
                pltpu.SemaphoreType.DMA((4,)),
            ],
        ),
        out_shape=[shape_of((pairs, block, width))] * 2,
        compiler_params=PARAMS,
        cost_estimate=cost(6e9, 10 << 20),
        name="shrink_grads",
    )(place, active, *parts)


def unhidden_kernel(
    place_ref,
    a_ref,
    b_ref,
    c_ref,
    d_ref,
    w_ref,
    slope_ref,
    grad_ref,
    near_ref,
    own_ref,
    sum_ref,
    grads_s,
    tokens_s,
    w_s,
    slope_s,
    near_s,
    own_s,
    in_sems,
    out_sems,
):
    rows = a_ref.shape[1]
    parts = (a_ref, b_ref, c_ref, d_ref)
    loads = copies([(w_ref, w_s)], in_sems)
    loads += loaded(parts, grads_s, in_sems, 1, 1)
    loads += copies(
        [
            (slope_ref.at[pl.ds(p * rows, rows), :], slope_s.at[pl.ds(p * rows, rows), :])
            for p in range(4)
        ],
        in_sems,
        5,
    )
    loads += loaded(parts, tokens_s, in_sems, 9, 0)
    loads[0].wait()
    stores = []
    for p in range(4):
        loads[1 + p].wait()
        loads[5 + p].wait()
        at = pl.ds(p * rows, rows)
        grad = (nt(grads_s[at, :], w_s[...]) * slope_s[at, :].astype(F32)).astype(BF16)
        slope_s[at, :] = grad
        part = jnp.sum(grad.astype(F32), axis=0, keepdims=True)
        if p == 0:
            sum_ref[...] = part
        else:
            sum_ref[...] += part
        stores += copies([(slope_s.at[at, :], grad_ref.at[at, :])], out_sems, p)
    for copy in loads[9:]:
        copy.wait()
    count, block, _ = near_ref.shape
    for m in range(count):
        product = tn(tokens_s[:, pair_rows(place_ref, m, 2 * block)], slope_s[...])
        put_pair(place_ref, m, product, near_s, own_s)
        stores += copies(
            [(near_s.at[m], near_ref.at[m]), (own_s.at[m], own_ref.at[m])], out_sems, 4 + 2 * m
        )
    for copy in stores:
        copy.wait()


def unhidden_layer(place, parts, w, slope, pairs):
    _, rows, width = parts[0].shape
    units = w.shape[0]
    blocks = (pairs, width // (2 * pairs), units)
    return pl.pallas_call(
        unhidden_kernel,
        in_specs=[SMEM] + [ANY] * 6,
        out_specs=[ANY] * 3 + [VMEM],
        out_shape=[shape_of((4 * rows, units))]
        + [shape_of(blocks)] * 2
        + [shape_of((1, units), F32)],
        scratch_shapes=[pltpu.VMEM((4 * rows, width), BF16)] * 2
        + [pltpu.VMEM(w.shape, BF16)]
        + [pltpu.VMEM((4 * rows, units), BF16)]
        + [pltpu.VMEM(blocks, BF16)] * 2
        + [pltpu.SemaphoreType.DMA((13,)), pltpu.SemaphoreType.DMA((4 + 2 * pairs,))],
        compiler_params=PARAMS,
        cost_estimate=cost(1.2e10, 22 << 20),
        name="unhidden",
    )(place, *parts, w, slope)


def attention_grads_kernel(
    place_ref,
    a_ref,
    b_ref,
    c_ref,
    d_ref,
    mixed_one_ref,
    pg_one_ref,
    mixed_two_ref,
    pg_two_ref,
    near_ref,
    late_ref,
    own_ref,
    grads_s,
    tokens_s,
    mixed_s,
    pg_s,
    dense_s,
    near_s,
    own_s,
    in_sems,
    out_sems,
):
    parts = (a_ref, b_ref, c_ref, d_ref)
    mixed = [ref.at[p] for ref in (mixed_one_ref, mixed_two_ref) for p in range(2)]
    pg = [ref.at[p] for ref in (pg_one_ref, pg_two_ref) for p in range(2)]
    loads = loaded(parts, grads_s, in_sems, 0, 1)
    loads += loaded(mixed, mixed_s, in_sems, 4)
    loads += loaded(parts, tokens_s, in_sems, 8, 0)
    loads += loaded(pg, pg_s, in_sems, 12)
    for copy in loads[:8]:
        copy.wait()
    count, block, columns = own_ref.shape
    wide = pg_s.shape[1]
    few = block // 4
    dense_s[...] = tn(mixed_s[...], grads_s[...])
    for copy in loads[8:]:
        copy.wait()
    across = columns // 4
    swap = (place_ref[0] & 1) == 1
    stores = []
    for m in (2, 3, 0, 1):
        product = tn(tokens_s[:, pair_rows(place_ref, m, 2 * block)], pg_s[...])
        put_pair(place_ref, m, product, near_s, own_s, slice(0, wide))
        product = dense_s[pair_rows(place_ref, m, 2 * few), :]
        low, high = product[:few], product[few:]
        own = jnp.where(swap, high, low).astype(BF16)
        near = jnp.where(swap, low, high).astype(BF16)
        for j in range(4):
            cols = slice(j * across, (j + 1) * across)
            own_s[m, j * few : (j + 1) * few, wide:] = own[:, cols]
            near_s[m, j * few : (j + 1) * few, wide:] = near[:, cols]
        near_at = near_ref if m >= count // 2 else late_ref
        stores += copies(
            [(near_s.at[m], near_at.at[m % 2]), (own_s.at[m], own_ref.at[m])], out_sems, 2 * m
        )
    for copy in stores:
        copy.wait()


def attention_grads(place, parts, one, two, pairs):
    _, rows, width = parts[0].shape
    heads = one[0].shape[-1]
    wide = one[1].shape[-1]
    blocks = (pairs, width // (2 * pairs), wide + heads)
    return pl.pallas_call(
        attention_grads_kernel,
        in_specs=[SMEM] + [ANY] * 8,
        out_specs=[ANY] * 3,
        out_shape=[shape_of((pairs // 2,) + blocks[1:])] * 2 + [shape_of(blocks)],
        scratch_shapes=[pltpu.VMEM((4 * rows, width), BF16)] * 2
        + [pltpu.VMEM((4 * rows, heads), BF16), pltpu.VMEM((4 * rows, wide), BF16)]
        + [pltpu.VMEM((heads, width), F32)]
        + [pltpu.VMEM(blocks, BF16)] * 2
        + [pltpu.SemaphoreType.DMA((16,)), pltpu.SemaphoreType.DMA((2 * pairs,))],
        compiler_params=PARAMS,
        cost_estimate=cost(7e9, 16 << 20),
        name="attention_grads",
    )(place, *parts, *one, *two)


def results_kernel(
    mixed_ref,
    pg_ref,
    act_ref,
    grad_ref,
    dense_ref,
    shrink_ref,
    project_ref,
    expand_ref,
    mine_ref,
    theirs_ref,
    mixed_s,
    pg_s,
    act_s,
    grad_s,
    dense_s,
    shrink_s,
    project_s,
    expand_s,
    out_s,
    in_sems,
    out_sems,
    *,
    first,
):
    rows = mixed_ref.shape[1]
    theirs = pl.ds((first + 1) * rows, rows)
    mine = pl.ds(first * rows, rows)
    loads = copies(
        [
            (shrink_ref, shrink_s),
            (act_ref.at[theirs, :], act_s.at[1]),
            (mixed_ref, mixed_s),
            (dense_ref, dense_s),
            (expand_ref, expand_s),
            (grad_ref.at[theirs, :], grad_s.at[1]),
            (pg_ref, pg_s),
            (project_ref, project_s),
            (act_ref.at[mine, :], act_s.at[0]),
            (grad_ref.at[mine, :], grad_s.at[0]),
        ],
        in_sems,
    )
    stores = []
    for at, (piece, gradient, waits) in enumerate(
        ((1, 0, loads[:4]), (1, 1, loads[4:8]), (0, 0, loads[8:9]), (0, 1, loads[9:]))
    ):
        for copy in waits:
            copy.wait()
        if gradient:
            total = nt(grad_s[piece], expand_s[...]) + nt(pg_s[piece], project_s[...])
        else:
            total = nn(act_s[piece], shrink_s[...]) + nn(mixed_s[piece], dense_s[...])
        out_s[at] = total.astype(BF16)
        out_ref = theirs_ref if piece else mine_ref
        stores += copies([(out_s.at[at], out_ref.at[gradient])], out_sems, at)
    for copy in stores:
        copy.wait()


def results(mixed, pg, act, grad, dense, shrink, project, expand, first):
    _, rows, heads = mixed.shape
    wide = pg.shape[-1]
    units = act.shape[-1]
    width = dense.shape[1]
    return pl.pallas_call(
        functools.partial(results_kernel, first=first),
        in_specs=[ANY] * 8,
        out_specs=[ANY] * 2,
        out_shape=[shape_of((2, rows, width))] * 2,
        scratch_shapes=[pltpu.VMEM(mixed.shape, BF16), pltpu.VMEM(pg.shape, BF16)]
        + [pltpu.VMEM((2, rows, units), BF16)] * 2
        + [pltpu.VMEM(w.shape, BF16) for w in (dense, shrink, project, expand)]
        + [pltpu.VMEM((4, rows, width), BF16)]
        + [pltpu.SemaphoreType.DMA((10,)), pltpu.SemaphoreType.DMA((4,))],
        compiler_params=PARAMS,
        cost_estimate=cost(8e9, 16 << 20),
        name="results",
    )(mixed, pg, act, grad, dense, shrink, project, expand)


def exchange(value, axis, size, offset):
    return lax.ppermute(value, axis, [(i, i ^ offset) for i in range(size)])


def sum_over(value, axis, size, offset=1):
    while offset < size:
        value = value + exchange(value, axis, size, offset)
        offset *= 2
    return value


def slots(value, index, size):
    row = lax.broadcasted_iota(jnp.int32, (size, 1), 0)
    return jnp.where(row == index, value[None, :], 0.0)


def after(values, *first):
    return lax.optimization_barrier(tuple(values) + first)[: len(values)]


def hop(value, size, offset):
    return exchange(value, "fsdp", size, offset)


class Gather:
    def __init__(self, block, size, near=True):
        self.own, self.size = block, size
        self.far = hop(block, size, 4)
        self.near = hop(block, size, 1) if near else None
        self.far_near = None

    def second(self, *first):
        own, far = after((self.own, self.far), *first) if first else (self.own, self.far)
        self.pair = hop(jnp.stack([own, far]), self.size, 2)
        if self.far_near is None:
            self.far_near = hop(far, self.size, 1)

    def second_near(self):
        self.far_near = hop(self.far, self.size, 1)

    def third(self, *first):
        (pair,) = after((self.pair,), *first) if first else (self.pair,)
        self.pair_near = hop(pair, self.size, 1)

    def blocks(self, *first):
        every = (self.own, self.near, self.far, self.far_near, self.pair, self.pair_near)
        return after(every, *first) if first else every


class Scatter:
    def __init__(self, near, own, size, late=None):
        self.own, self.size = own, size
        if late is None:
            near = hop(near, size, 1)
            self.near, self.late = near[2:], near[:2]
            self.arrived = near
        else:
            self.near, self.late = hop(near, size, 1), hop(late, size, 1)
            self.arrived = self.near

    def second(self, *first):
        near, own = after((self.near, self.own[2:]), self.late, *first)
        self.pair = hop((own.astype(F32) + near.astype(F32)).astype(BF16), self.size, 2)
        return self.arrived

    def third(self, *first):
        pair, near = after((self.pair, self.late), *first) if first else (self.pair, self.late)
        total = self.own[1].astype(F32) + near[1].astype(F32) + pair[1].astype(F32)
        self.far = hop(total.astype(BF16), self.size, 4)
        return pair

    def terms(self):
        return self.own, self.late, self.pair, self.far

    def total(self):
        return sum(term.astype(F32) for term in (self.own[0], self.late[0], self.pair[0], self.far))


def row_of(value):
    return jnp.broadcast_to(value, (value.shape[0], 128)).T[:1, :]


def block_total(own_ref, late_ref, pair_ref, far_ref, columns):
    total = own_ref[:, columns].astype(F32) + late_ref[:, columns].astype(F32)
    return total + pair_ref[:, columns].astype(F32) + far_ref[:, columns].astype(F32)


def finish_project_kernel(
    own_ref, late_ref, pair_ref, far_ref, w_ref, sum_ref, vector_ref, grad_ref, dense_ref, part_ref
):
    wide = w_ref.shape[1]
    heads = wide // (3 * HD)
    gain, shift = column(vector_ref[0:1, :]), column(vector_ref[1:2, :])
    first = second = 0.0
    for head in range(heads):
        for part in range(3):
            at = (part * heads + head) * HD
            to = (head * 3 + part) * HD
            total = block_total(own_ref, late_ref, pair_ref, far_ref, slice(at, at + HD))
            weight = w_ref[:, to : to + HD].astype(F32)
            sums = sum_ref[:, at : at + HD]
            grad_ref[:, to : to + HD] = gain * total + shift * sums
            first = first + jnp.sum(weight * total, axis=1, keepdims=True)
            second = second + jnp.sum(weight * sums, axis=1, keepdims=True)
    part_ref[0:1, :] = row_of(first)
    part_ref[1:2, :] = row_of(second)
    rows, width = dense_ref.shape
    across = width // 4
    total = block_total(own_ref, late_ref, pair_ref, far_ref, slice(wide, wide + across))
    for j in range(4):
        dense_ref[:, j * across : (j + 1) * across] = total[j * rows : (j + 1) * rows, :]


def finish_project(terms, weight, sums, vectors, rows):
    width = weight.shape[0] * 8
    lead = pl.BlockSpec((None, weight.shape[0], width), lambda i: (0, 0, 0))
    whole = [
        pl.BlockSpec(shape, lambda i: (0, 0))
        for shape in (terms[3].shape, weight.shape, sums.shape, vectors.shape)
    ]
    outs = (weight.shape, (rows, width), (2, weight.shape[0]))
    return pl.pallas_call(
        finish_project_kernel,
        grid=(1,),
        in_specs=[lead] * 3 + whole,
        out_specs=[pl.BlockSpec(shape, lambda i: (0, 0)) for shape in outs],
        out_shape=[shape_of(shape, F32) for shape in outs],
        compiler_params=PARAMS,
        cost_estimate=cost(0, 4 << 20),
        name="finish_project",
    )(*terms, weight, sums, vectors)


def finish_expand_kernel(
    own_ref, late_ref, pair_ref, far_ref, w_ref, sum_ref, vector_ref, grad_ref, part_ref
):
    gain, shift = column(vector_ref[2:3, :]), column(vector_ref[3:4, :])
    total = block_total(own_ref, late_ref, pair_ref, far_ref, slice(None))
    weight = w_ref[...].astype(F32)
    grad_ref[...] = gain * total + shift * sum_ref[...]
    part_ref[0:1, :] = row_of(jnp.sum(weight * total, axis=1, keepdims=True))
    part_ref[1:2, :] = row_of(jnp.sum(weight * sum_ref[...], axis=1, keepdims=True))


def finish_expand(terms, weight, sums, vectors):
    lead = pl.BlockSpec((None,) + weight.shape, lambda i: (0, 0, 0))
    whole = [
        pl.BlockSpec(shape, lambda i: (0, 0))
        for shape in (terms[3].shape, weight.shape, sums.shape, vectors.shape)
    ]
    outs = (weight.shape, (2, weight.shape[0]))
    return pl.pallas_call(
        finish_expand_kernel,
        grid=(1,),
        in_specs=[lead] * 3 + whole,
        out_specs=[pl.BlockSpec(shape, lambda i: (0, 0)) for shape in outs],
        out_shape=[shape_of(shape, F32) for shape in outs],
        compiler_params=PARAMS,
        cost_estimate=cost(0, 4 << 20),
        name="finish_expand",
    )(*terms, weight, sums, vectors)


def finish_tokens_kernel(
    mine_ref, near_ref, far_ref, inputs_ref, cotangent_ref, keep_ref, bias_ref, out_ref, grad_ref
):
    def total(which):
        return (
            mine_ref[which].astype(F32) + near_ref[which].astype(F32) + far_ref[which].astype(F32)
        )

    features = inputs_ref[...].astype(F32)
    out_ref[...] = (features + total(0) + bias_ref[...]).astype(BF16)
    normed, rate = normalise(features)
    grad = total(1)
    inner = jnp.mean(grad * normed, axis=-1, keepdims=True)
    centre = jnp.mean(grad, axis=-1, keepdims=True)
    upstream = cotangent_ref[...].astype(F32) * keep_ref[...]
    grad_ref[...] = (upstream + rate * (grad - centre - normed * inner)).astype(BF16)


def finish_tokens(mine, near, far, inputs, cotangent, keep, bias):
    rows, width = inputs.shape
    step = rows // 4
    both = pl.BlockSpec((2, step, width), lambda i: (0, i, 0))
    block = pl.BlockSpec((step, width), lambda i: (i, 0))
    return pl.pallas_call(
        finish_tokens_kernel,
        grid=(4,),
        in_specs=[both] * 3
        + [block] * 2
        + [pl.BlockSpec((step, 1), lambda i: (i, 0)), pl.BlockSpec((1, width), lambda i: (0, 0))],
        out_specs=[block] * 2,
        out_shape=[shape_of((rows, width))] * 2,
        compiler_params=PARAMS,
        cost_estimate=cost(0, 12 << 20),
        name="finish_tokens",
    )(mine, near, far, inputs, cotangent, keep, bias)


def by_part(array):
    shape = array.shape
    array = array.reshape(shape[:-1] + (shape[-1] // (3 * HD), 3, HD))
    return jnp.swapaxes(array, -3, -2).reshape(shape)


def by_head(array):
    shape = array.shape
    array = array.reshape(shape[:-1] + (3, shape[-1] // (3 * HD), HD))
    return jnp.swapaxes(array, -3, -2).reshape(shape)


def gathered(weight):
    return lax.all_gather(weight, "fsdp", axis=0, tiled=True)


def folded(weight, gain, shift, offset):
    weight = gathered(weight).astype(F32)
    bias = offset[None, :] + jnp.sum(weight * shift[:, None], axis=0, keepdims=True)
    return (weight * gain[:, None]).astype(BF16), bias


def whole_rows(own, near):
    whole = jnp.stack([own, near], axis=1).astype(F32)[jnp.array([0, 2, 1, 3])]
    return whole.reshape(-1, whole.shape[-1])


def scattered(value):
    return lax.psum_scatter(value, "fsdp", scatter_dimension=0, tiled=True)


def local(
    inputs,
    segments,
    cotangent,
    attention_gain,
    attention_shift,
    feedforward_gain,
    feedforward_shift,
    project_weight,
    project_bias,
    dense_weight,
    dense_bias,
    expand_weight,
    expand_bias,
    shrink_weight,
    shrink_bias,
):
    size = lax.axis_size("fsdp")
    across = lax.axis_size("tensor")
    rows, width = inputs.shape
    assert across == 4 and 2 * rows == SEQ_LEN and segments.shape[0] == 2 * SEQ_LEN
    index = lax.axis_index("fsdp")
    rank = lax.axis_index("tensor")
    core = (rank % 2).astype(jnp.int32)[None]
    chip = rank // 2
    block = width // size
    pairs = 4
    direct = size == 2 * pairs
    place = (index if direct else index * 0).astype(jnp.int32)[None]

    own_labels = lax.dynamic_slice_in_dim(segments, rank * rows, rows, 0)
    keep = (own_labels != 0).astype(F32)[:, None]
    early = inputs
    if direct:
        first = Gather(expand_weight, size)
    packed_weights, *tables = pack(project_weight, dense_weight, shrink_weight, rotary_turns())
    if direct:
        (early,) = after((early,), packed_weights)
    own, bias_grad = prepare(early, cotangent, keep)

    small = jnp.concatenate(
        [
            attention_gain,
            attention_shift,
            feedforward_gain,
            feedforward_shift,
            dense_bias + shrink_bias,
        ]
    )
    piece = small.shape[0] // 5
    small = slots(small, rank, across)
    small_far = small + exchange(small, "tensor", across, 2)
    small = small_far + exchange(small_far, "tensor", across, 1)
    own_vectors = jnp.swapaxes(small.reshape(across, 5, piece), 0, 1).reshape(5, block)
    counts = (5 * block, project_bias.shape[0], expand_bias.shape[0])
    packed = jnp.concatenate(
        [own_vectors.reshape(-1), project_bias.astype(F32), expand_bias.astype(F32)]
    )
    packed = slots(packed, index, size)
    packed_near = packed + exchange(packed, "fsdp", size, 1)
    if direct:
        (packed_near,) = after((packed_near,), first.far, first.near, own)
    if direct:
        packed_far = packed_near + exchange(packed_near, "fsdp", size, 4)
        packed = packed_far + exchange(packed_far, "fsdp", size, 2)
    else:
        packed = sum_over(packed_near, "fsdp", size, 2)
    vectors = jnp.swapaxes(packed[:, : counts[0]].reshape(size, 5, block), 0, 1).reshape(5, width)
    project_offset = by_part(packed[:, counts[0] : counts[0] + counts[1]].reshape(-1))
    expand_offset = packed[:, counts[0] + counts[1] :].reshape(-1)

    (own,) = after((own,), small_far)

    def chip_pair(value):
        return exchange(value, "tensor", across, 1)

    def other_chip(value):
        return exchange(value, "tensor", across, 2)

    labels = segments.reshape(2, SEQ_LEN)
    labels = jnp.where(chip == 0, labels, labels[::-1])
    places = jnp.arange(SEQ_LEN, dtype=jnp.int32)[None, :]
    marks = jnp.where(labels != 0, labels, -1 - places)
    across_chip = other_chip(own)
    own_near, _ = after((own, small), packed_far) if direct else (own, small)
    partner = chip_pair(own_near)
    if direct:
        first.second_near()
        (own_block,) = after((packed_weights,), packed_near)
        rest_near = hop(own_block, size, 1)
        first.second(packed, rest_near)
        (packed_weights,) = after((packed_weights,), packed)
        rest = Gather(packed_weights, size, False)
        first.third(first.far_near)
        rest.near = rest_near
        rest.second(first.pair, first.far_near)
        expand, expand_row = join_expand(
            place,
            first.blocks(rest.far),
            vectors[2][None, :],
            vectors[3][None, :],
            expand_offset[None, :],
        )
        across_chip, expand = after((across_chip, expand), rest.far_near, rest.pair, partner)
        rest.third(expand)
    else:
        expand, expand_row = folded(expand_weight, vectors[2], vectors[3], expand_offset)
        project, project_row = folded(
            by_part(project_weight), vectors[0], vectors[1], project_offset
        )
        dense = gathered(dense_weight)
        shrink = gathered(shrink_weight)
    parts = (own, partner, across_chip, chip_pair(across_chip))

    active, slope = hidden_layer(parts, expand, expand_row)
    shrink_near, shrink_own = shrink_grads(place, active, parts, pairs)
    if direct:
        shrink_sums = Scatter(shrink_near, shrink_own, size)
        shrink, project, dense, project_row = join_rest(
            place,
            rest.blocks(shrink_own),
            vectors[0][None, :],
            vectors[1][None, :],
            project_offset[None, :],
        )
    hidden_grad, expand_near, expand_own, expand_offset_grad = unhidden_layer(
        place, parts, shrink, slope, pairs
    )
    if direct:
        expand_sums = Scatter(expand_near, expand_own, size)
        ready = shrink_sums.second(expand_own)
        (project,) = after((project,), ready)
    else:
        (project,) = after((project,), expand_own)

    def attend(sequence):
        at = slice(2 * sequence, 2 * sequence + 2)
        return attention(core, parts[at], project, project_row, dense, marks[sequence], tables)

    two = attend(1)
    weights = (dense, shrink, project, expand)
    act = active
    if direct:
        ready = shrink_sums.third(two[2])
        more = expand_sums.second(two[2])
        (act,) = after((active,), ready, more)
    far_mine, far_theirs = results(two[0], two[1], act, hidden_grad, *weights, first=2)
    far = chip_pair(far_theirs)
    far_sum = (far_mine.astype(F32) + far.astype(F32)).astype(BF16)
    far = other_chip(far_sum)
    if direct:
        ready = expand_sums.third(far_mine)
        (project,) = after((project,), ready, shrink_sums.far)
    else:
        (project,) = after((project,), far_mine)
    one = attend(0)
    if direct:
        (pair_grads,) = after((one[1],), expand_sums.far, far_sum)
        one = (one[0], pair_grads, one[2])
    both_near, both_late, both_own = attention_grads(place, parts, one[:2], two[:2], pairs)
    project_offset_grad = one[2] + two[2]
    wide = project_offset_grad.shape[1]
    units = expand_offset_grad.shape[1]
    few = dense_weight.shape[0]
    totals = jnp.concatenate([project_offset_grad, expand_offset_grad, bias_grad], axis=1)
    (totals,) = after((totals,), both_own)
    totals = totals_near = totals + exchange(totals, "fsdp", size, 1)
    if direct:
        totals = totals_pair = totals + exchange(totals, "fsdp", size, 2)
        totals = totals + exchange(totals, "fsdp", size, 4)
    else:
        totals = sum_over(totals, "fsdp", size, 2)
    project_totals = totals[:, :wide]
    expand_totals = totals[:, wide : wide + units]
    bias_totals = totals[0, wide + units :]

    act = active
    if direct:
        both_sums = Scatter(both_near, both_own, size, both_late)
        (act,) = after((active,), both_own)
    near_mine, near_theirs = results(one[0], one[1], act, hidden_grad, *weights, first=0)
    def mine(vector, count, start):
        return lax.dynamic_slice_in_dim(vector, start * count, count, 0)

    own_rows = own_vectors[:4]
    if direct:
        both_sums.second(near_mine, totals_pair)
        shrink_sum = shrink_sums.total()
        expand_gradient, expand_parts = finish_expand(
            expand_sums.terms(), expand_weight, expand_totals, own_rows
        )
        ready = both_sums.third(expand_gradient, shrink_sum)
        far, near_mine, near_theirs = after((far, near_mine, near_theirs), ready)
        near = chip_pair(near_theirs)
        output, inputs_gradient = finish_tokens(
            near_mine, near, far, inputs, cotangent, keep, vectors[4][None, :]
        )
        (project_totals,) = after((project_totals,), output)
        project_gradient, dense_sum, project_parts = finish_project(
            both_sums.terms(), project_weight, project_totals, own_rows, few
        )
        partial = [project_parts, expand_parts]
    else:
        near = chip_pair(near_theirs)
        output, inputs_gradient = finish_tokens(
            near_mine, near, far, inputs, cotangent, keep, vectors[4][None, :]
        )
        shrink_sum = scattered(whole_rows(shrink_own, shrink_near))
        expand_sum = scattered(whole_rows(expand_own, expand_near))
        both = whole_rows(both_own, jnp.concatenate([both_late, both_near]))
        project_sum = scattered(both[:, :wide])
        dense_sum = both[:, wide:].reshape(2 * pairs, 4, -1, width // 4)
        dense_sum = scattered(jnp.swapaxes(dense_sum, 1, 2).reshape(-1, width))
        columns = own_rows[:, :, None]
        project_gradient = by_head(columns[0] * project_sum + columns[1] * project_totals)
        expand_gradient = columns[2] * expand_sum + columns[3] * expand_totals
        own_project = by_part(project_weight).astype(F32)
        own_expand = expand_weight.astype(F32)
        partial = [
            jnp.sum(term, axis=1)[None, :]
            for term in (
                own_project * project_sum,
                own_project * project_totals,
                own_expand * expand_sum,
                own_expand * expand_totals,
            )
        ]
    partial = jnp.concatenate(partial + [mine(bias_totals, block, index)[None, :]])
    partial = sum_over(partial, "tensor", across)
    partial = lax.dynamic_slice_in_dim(partial, rank * piece, piece, 1)
    return (
        output,
        inputs_gradient,
        partial[0],
        partial[1],
        partial[2],
        partial[3],
        project_gradient,
        mine(by_head(project_totals[0]), project_bias.shape[0], index),
        dense_sum,
        partial[4],
        expand_gradient,
        mine(expand_totals[0], expand_bias.shape[0], index),
        shrink_sum,
        partial[4],
    )


def solution(mesh):
    in_specs = (
        P(("fsdp", "tensor"), None),
        P("fsdp"),
        P(("fsdp", "tensor"), None),
        P(("fsdp", "tensor")),
        P(("fsdp", "tensor")),
        P(("fsdp", "tensor")),
        P(("fsdp", "tensor")),
        P("fsdp", "tensor"),
        P(("tensor", "fsdp")),
        P(("tensor", "fsdp"), None),
        P(("fsdp", "tensor")),
        P("fsdp", "tensor"),
        P(("tensor", "fsdp")),
        P(("tensor", "fsdp"), None),
        P(("fsdp", "tensor")),
    )
    out_specs = (
        P(("fsdp", "tensor"), None),
        P(("fsdp", "tensor"), None),
        P(("fsdp", "tensor")),
        P(("fsdp", "tensor")),
        P(("fsdp", "tensor")),
        P(("fsdp", "tensor")),
        P("fsdp", "tensor"),
        P(("tensor", "fsdp")),
        P(("tensor", "fsdp"), None),
        P(("fsdp", "tensor")),
        P("fsdp", "tensor"),
        P(("tensor", "fsdp")),
        P(("tensor", "fsdp"), None),
        P(("fsdp", "tensor")),
    )
    return jax.shard_map(local, mesh=mesh, in_specs=in_specs, out_specs=out_specs, check_vma=False)
```

```python
import functools
import math

import jax
import jax.numpy as jnp
from jax import lax
from jax.experimental import pallas as pl
from jax.experimental.pallas import tpu as pltpu
from jax.sharding import PartitionSpec as P

HD = 64
ROT = 16
SEQ_LEN = 1024
EPS = 1e-05
NEGATIVE = -1e30
QB = 256
CHUNK = 128
PARAMS = pltpu.CompilerParams(vmem_limit_bytes=60 * 1024 * 1024)
BF16 = jnp.bfloat16
F32 = jnp.float32
COST = 1.0
VMEM = pl.BlockSpec(memory_space=pltpu.VMEM)
SMEM = pl.BlockSpec(memory_space=pltpu.SMEM)
ANY = pl.BlockSpec(memory_space=pl.ANY)


def shape_of(dims, kind=BF16):
    return jax.ShapeDtypeStruct(dims, kind)


def cost(flops, moved):
    return pl.CostEstimate(
        flops=int(flops * COST), bytes_accessed=int(moved * COST), transcendentals=0
    )


def nn(left, right):
    return lax.dot_general(left, right, (((1,), (0,)), ((), ())), preferred_element_type=F32)


def nt(left, right):
    return lax.dot_general(left, right, (((1,), (1,)), ((), ())), preferred_element_type=F32)


def tn(left, right):
    return lax.dot_general(left, right, (((0,), (0,)), ((), ())), preferred_element_type=F32)


def copies(pairs, sems, first=0):
    made = [pltpu.make_async_copy(s, d, sems.at[first + i]) for i, (s, d) in enumerate(pairs)]
    for copy in made:
        copy.start()
    return made


def pack_kernel(project_ref, dense_ref, turns_ref, out_ref, cos_ref, up_ref, dn_ref):
    heads = project_ref.shape[1] // (3 * HD)
    rows = dense_ref.shape[0]
    width = heads * HD
    for part in range(3):
        pieces = [
            project_ref[:, (3 * head + part) * HD : (3 * head + part + 1) * HD]
            for head in range(heads)
        ]
        out_ref[:, part * width : (part + 1) * width] = jnp.concatenate(pieces, axis=1)
    for j in range(4):
        columns = slice(j * width, (j + 1) * width)
        out_ref[j * rows : (j + 1) * rows, 3 * width :] = dense_ref[:, columns]
    half = ROT // 2
    length = turns_ref.shape[0]
    cosine, sine = turns_ref[:, :half], turns_ref[:, half:]
    rest = jnp.zeros((length, HD - ROT), F32)
    none = jnp.zeros((length, half), F32)
    cos_ref[...] = jnp.concatenate([cosine, cosine, rest + 1.0] * 2, axis=1)
    up_ref[...] = jnp.concatenate([none, sine, rest] * 2, axis=1)
    dn_ref[...] = jnp.concatenate([-sine, none, rest] * 2, axis=1)


def pack(project, dense, turns):
    table = shape_of((turns.shape[0], 2 * HD), F32)
    return pl.pallas_call(
        pack_kernel,
        in_specs=[VMEM] * 3,
        out_specs=[VMEM] * 4,
        out_shape=[shape_of((project.shape[0], dense.shape[1]))] + [table] * 3,
        compiler_params=PARAMS,
        cost_estimate=cost(0, 3 << 20),
        name="pack",
    )(project, dense, turns)


def column(row):
    return jnp.broadcast_to(row, (8, row.shape[1])).T[:, :1]


def shift_times(shift, weight):
    high = shift.astype(BF16)
    rest = shift - high.astype(F32)
    middle = rest.astype(BF16)
    low = (rest - middle.astype(F32)).astype(BF16)
    parts = nn(jnp.concatenate([high, middle, low], axis=0), weight)
    return jnp.sum(parts, axis=0, keepdims=True)


def scaled_rows(place, k, weight, gain_ref, shift_ref):
    rows = weight.shape[0]
    start = pl.multiple_of(lax.bitwise_xor(place, k) * rows, rows)
    part = shift_times(shift_ref[:, pl.ds(start, rows)], weight)
    gain = column(gain_ref[:, pl.ds(start, rows)])
    return start, (weight.astype(F32) * gain).astype(BF16), part


def block_list(refs):
    own, near, far, far_near, pair, pair_near = refs
    return [own, near, pair.at[0], pair_near.at[0], far, far_near, pair.at[1], pair_near.at[1]]


def join_project_kernel(place_ref, *refs):
    gain_ref, shift_ref, offset_ref, project_ref, dense_ref, bias_ref = refs[6:]
    total = offset_ref[...]
    wide = project_ref.shape[1]
    for k, ref in enumerate(block_list(refs[:6])):
        block = ref[...]
        start, scaled, part = scaled_rows(
            place_ref[0], k, block[:, :wide], gain_ref, shift_ref
        )
        project_ref[pl.ds(start, block.shape[0]), :] = scaled
        total = total + part
        rows = block.shape[0] // 4
        across = block.shape[1] // 4
        base = pl.multiple_of(lax.bitwise_xor(place_ref[0], k) * rows, rows)
        for j in range(4):
            dense_ref[pl.ds(base, rows), j * across : (j + 1) * across] = block[
                j * rows : (j + 1) * rows, wide:
            ]
    bias_ref[...] = total


def join_project(place, blocks, gain, shift, offset):
    rows, columns = blocks[0].shape
    total = 8 * rows
    wide = offset.shape[1]
    return pl.pallas_call(
        join_project_kernel,
        in_specs=[SMEM] + [VMEM] * 9,
        out_specs=[VMEM] * 3,
        out_shape=[
            shape_of((total, wide)),
            shape_of((total // 4, columns)),
            shape_of((1, wide), F32),
        ],
        compiler_params=PARAMS,
        cost_estimate=cost(1e9, 10 << 20),
        name="join_project",
    )(place, *blocks, gain, shift, offset)


def join_expand_kernel(place_ref, *refs):
    gain_ref, shift_ref, offset_ref, out_ref, bias_ref = refs[6:]
    total = offset_ref[...]
    for k, ref in enumerate(block_list(refs[:6])):
        start, scaled, part = scaled_rows(place_ref[0], k, ref[...], gain_ref, shift_ref)
        out_ref[pl.ds(start, scaled.shape[0]), :] = scaled
        total = total + part
    bias_ref[...] = total


def join_expand(place, blocks, gain, shift, offset):
    rows, columns = blocks[0].shape
    return pl.pallas_call(
        join_expand_kernel,
        in_specs=[SMEM] + [VMEM] * 9,
        out_specs=[VMEM] * 2,
        out_shape=[shape_of((8 * rows, columns)), shape_of((1, columns), F32)],
        compiler_params=PARAMS,
        cost_estimate=cost(1e9, 6 << 20),
        name="join_expand",
    )(place, *blocks, gain, shift, offset)


def join_kernel(place_ref, *refs):
    out_ref = refs[6]
    for k, ref in enumerate(block_list(refs[:6])):
        rows = ref.shape[0]
        start = pl.multiple_of(lax.bitwise_xor(place_ref[0], k) * rows, rows)
        out_ref[pl.ds(start, rows), :] = ref[...]


def join(place, blocks):
    rows, columns = blocks[0].shape
    return pl.pallas_call(
        join_kernel,
        in_specs=[SMEM] + [VMEM] * 6,
        out_specs=VMEM,
        out_shape=shape_of((8 * rows, columns)),
        compiler_params=PARAMS,
        cost_estimate=cost(0, 4 << 20),
        name="join",
    )(place, *blocks)


def normalise(features):
    centre = features - jnp.mean(features, axis=-1, keepdims=True)
    rate = lax.rsqrt(jnp.mean(centre * centre, axis=-1, keepdims=True) + EPS)
    return centre * rate, rate


def prepare_kernel(inputs_ref, cotangent_ref, keep_ref, both_ref, sum_ref):
    both_ref[0] = normalise(inputs_ref[...].astype(F32))[0].astype(BF16)
    upstream = cotangent_ref[...].astype(F32) * keep_ref[...]
    both_ref[1] = upstream.astype(BF16)
    sum_ref[...] = jnp.sum(upstream, axis=0, keepdims=True)


def prepare(inputs, cotangent, keep):
    return pl.pallas_call(
        prepare_kernel,
        in_specs=[VMEM] * 3,
        out_specs=[VMEM] * 2,
        out_shape=[shape_of((2,) + inputs.shape), shape_of((1, inputs.shape[1]), F32)],
        compiler_params=PARAMS,
        cost_estimate=cost(0, 6 << 20),
        name="prepare",
    )(inputs, cotangent, keep)


def attention_kernel(
    core_ref,
    first_ref,
    second_ref,
    w_ref,
    b_ref,
    d_ref,
    lrow_ref,
    cos_ref,
    up_ref,
    dn_ref,
    mixed_ref,
    pg_ref,
    sum_ref,
    q_s,
    k_s,
    v_s,
    g_s,
    kt_s,
    vt_s,
    gt_s,
    pt_s,
    dst_s,
    ot_s,
    dqt_s,
    dk_s,
    dv_s,
    out_s,
    scores_s,
    qm_s,
    gm_s,
    lcol_s,
):
    half_rows = first_ref.shape[1]
    length = 2 * half_rows
    width = d_ref.shape[0]
    blocks = length // QB
    scale = 1.0 / math.sqrt(HD)

    def starts(piece):
        return pl.multiple_of(lax.bitwise_xor(core_ref[0], piece) * half_rows, half_rows)

    for piece, ref in enumerate((first_ref, second_ref)):
        rows = pl.ds(starts(piece), half_rows)
        cos, up, dn = cos_ref[rows, :], up_ref[rows, :], dn_ref[rows, :]

        def rotate(u):
            return u * cos + pltpu.roll(u, 8, axis=1) * up + pltpu.roll(u, 120, axis=1) * dn

        tokens = ref[0]
        g_s[rows, :] = nt(ref[1], d_ref[...]).astype(BF16)
        q = nn(tokens, w_ref[:, :width]) + b_ref[:, :width]
        k = nn(tokens, w_ref[:, width : 2 * width]) + b_ref[:, width : 2 * width]
        for lo in range(0, width, 128):
            sl = slice(lo, lo + 128)
            turned = rotate(q[:, sl]).astype(BF16).astype(F32)
            q_s[rows, sl] = (turned * scale).astype(BF16)
            k_s[rows, sl] = rotate(k[:, sl]).astype(BF16)
        v_s[rows, :] = (nn(tokens, w_ref[:, 2 * width :]) + b_ref[:, 2 * width :]).astype(BF16)

    cos, up, dn = cos_ref[...], up_ref[...], dn_ref[...]

    def rotate_back(w):
        return w * cos + pltpu.roll(w * up, 120, axis=1) + pltpu.roll(w * dn, 8, axis=1)

    lane = lax.broadcasted_iota(jnp.int32, (1, 128), 1)
    zero = jnp.zeros((), BF16)
    lcol_s[...] = column(lrow_ref[...])

    def folded_rows(value, fold):
        return fold(value.reshape(value.shape[0] // 8, 8, value.shape[1]), axis=0)

    def pair(p, carry):
        lo = pl.multiple_of(p * 128, 128)
        sl = pl.ds(lo, 128)
        kt_s[...] = k_s[:, sl].T
        vt_s[...] = v_s[:, sl].T
        gt_s[...] = g_s[:, sl].astype(F32).T
        for a in range(2):
            half = (lane >= HD * a) & (lane < HD * (a + 1))
            qm_s[a] = jnp.where(half, q_s[:, sl], zero)
            gm_s[a] = jnp.where(half, g_s[:, sl], zero)
        for i in range(blocks):
            for a in range(2):
                hs = slice(HD * a, HD * (a + 1))
                end = (i + 1) * QB
                rows = slice(i * QB, end)
                qm = qm_s[a, rows, :]
                gm = gm_s[a, rows, :]
                chunks = [slice(c, c + CHUNK) for c in range(0, end, CHUNK)]
                top = None
                for cs in chunks:
                    s = nt(k_s[cs, sl], qm)
                    same = lcol_s[cs, :] == lrow_ref[:, rows]
                    if cs.start >= i * QB:
                        key = lax.broadcasted_iota(jnp.int32, (CHUNK, QB), 0)
                        query = lax.broadcasted_iota(jnp.int32, (CHUNK, QB), 1)
                        same = same & (key + (cs.start - i * QB) <= query)
                    s = jnp.where(same, s, NEGATIVE)
                    scores_s[a, cs, :] = s
                    part = folded_rows(s, jnp.max)
                    top = part if top is None else jnp.maximum(top, part)
                top = jnp.max(top, axis=0, keepdims=True)
                total = None
                for cs in chunks:
                    e = jnp.exp(scores_s[a, cs, :] - top)
                    scores_s[a, cs, :] = e
                    part = folded_rows(e, jnp.sum)
                    total = part if total is None else total + part
                rate = 1.0 / jnp.sum(total, axis=0, keepdims=True)
                for cs in chunks:
                    pt_s[a, cs, rows] = (scores_s[a, cs, :] * rate).astype(BF16)
                out = nn(vt_s[hs, 0:end], pt_s[a, 0:end, rows])
                ot_s[hs, rows] = out
                inner = jnp.sum(gt_s[hs, rows] * out, axis=0, keepdims=True)
                for cs in chunks:
                    dp = nt(v_s[cs, sl], gm) - inner
                    dst_s[a, cs, rows] = (scores_s[a, cs, :] * rate * dp).astype(BF16)
                dqt_s[hs, rows] = nn(kt_s[hs, 0:end], dst_s[a, 0:end, rows]) * scale
        for j in range(blocks):
            rows = slice(j * QB, length)
            out = slice(j * QB, (j + 1) * QB)
            dk_s[out, :] = nn(dst_s[0, out, rows], qm_s[0, rows, :]) + nn(
                dst_s[1, out, rows], qm_s[1, rows, :]
            )
            dv_s[out, :] = nn(pt_s[0, out, rows], gm_s[0, rows, :]) + nn(
                pt_s[1, out, rows], gm_s[1, rows, :]
            )

        def put(at, values):
            cols = pl.ds(pl.multiple_of(at + lo, 128), 128)
            values = values.astype(BF16)
            sum_ref[:, cols] = jnp.sum(values.astype(F32), axis=0, keepdims=True)
            out_s[...] = values
            for piece in range(2):
                pg_ref[piece, :, cols] = out_s[pl.ds(starts(piece), half_rows), :]

        put(0, rotate_back(dqt_s[...].T))
        put(width, rotate_back(dk_s[...]))
        put(2 * width, dv_s[...])
        out_s[...] = ot_s[...].T.astype(BF16)
        for piece in range(2):
            mixed_ref[piece, :, sl] = out_s[pl.ds(starts(piece), half_rows), :]
        return carry

    lax.fori_loop(0, width // 128, pair, 0)


def attention(core, parts, w, b, dense, marks, tables):
    half_rows = parts[0].shape[1]
    length = 2 * half_rows
    width = dense.shape[0]
    return pl.pallas_call(
        attention_kernel,
        in_specs=[SMEM] + [VMEM] * 9,
        out_specs=[VMEM] * 3,
        out_shape=[
            shape_of((2, half_rows, width)),
            shape_of((2, half_rows, 3 * width)),
            shape_of((1, 3 * width), F32),
        ],
        scratch_shapes=[pltpu.VMEM((length, width), BF16)] * 4
        + [pltpu.VMEM((128, length), BF16)] * 2
        + [pltpu.VMEM((128, length), F32)]
        + [pltpu.VMEM((2, length, length), BF16)] * 2
        + [pltpu.VMEM((128, length), F32)] * 2
        + [pltpu.VMEM((length, 128), F32)] * 2
        + [pltpu.VMEM((length, 128), BF16)]
        + [pltpu.VMEM((2, length, QB), F32)]
        + [pltpu.VMEM((2, length, 128), BF16)] * 2
        + [pltpu.VMEM((length, 1), jnp.int32)],
        compiler_params=PARAMS,
        cost_estimate=cost(2.3e10, 8 << 20),
        name="attention",
    )(core, *parts, w, b, dense, marks[None, :], *tables)


def rotary_turns():
    half = ROT // 2
    places = jnp.arange(SEQ_LEN, dtype=jnp.int32).astype(F32)
    rates = jnp.exp(
        jnp.arange(half, dtype=jnp.int32).astype(F32) * (-2.0 * math.log(10000.0) / ROT)
    )
    angles = places[:, None] * rates[None, :]
    return jnp.concatenate([jnp.cos(angles), jnp.sin(angles)], axis=1)


def turn(slot):
    return 2 * (slot % 2) + slot // 2


def put_pair(place_ref, m, product, near_s, own_s, columns=slice(None)):
    rows = product.shape[0] // 2
    low, high = product[:rows], product[rows:]
    swap = (place_ref[0] & 1) == 1
    own_s[m, :, columns] = jnp.where(swap, high, low).astype(BF16)
    near_s[m, :, columns] = jnp.where(swap, low, high).astype(BF16)


def pair_rows(place_ref, m, width):
    other = lax.bitwise_xor(lax.shift_right_logical(place_ref[0], 1), turn(m))
    return pl.ds(pl.multiple_of(other * width, width), width)


def loaded(parts, held, sems, first, which=None):
    if which is not None:
        parts = [ref.at[which] for ref in parts]
    rows = parts[0].shape[0]
    return copies(
        [(ref, held.at[pl.ds(p * rows, rows), :]) for p, ref in enumerate(parts)], sems, first
    )


def send_pairs(near_s, own_s, near_ref, own_ref, sems, first):
    def copy(m):
        return (
            pltpu.make_async_copy(near_s.at[m], near_ref.at[m], sems.at[first + 2 * m]),
            pltpu.make_async_copy(own_s.at[m], own_ref.at[m], sems.at[first + 2 * m + 1]),
        )

    return copy


def hidden_kernel(
    place_ref,
    a_ref,
    b_ref,
    c_ref,
    d_ref,
    w_ref,
    bias_ref,
    act_ref,
    slope_ref,
    near_ref,
    own_ref,
    tokens_s,
    grads_s,
    w_s,
    act_s,
    slope_s,
    near_s,
    own_s,
    in_sems,
    out_sems,
):
    rows = a_ref.shape[1]
    parts = (a_ref, b_ref, c_ref, d_ref)
    loads = copies([(w_ref, w_s)], in_sems)
    loads += loaded(parts, tokens_s, in_sems, 1, 0)
    loads += loaded(parts, grads_s, in_sems, 5, 1)
    loads[0].wait()
    stores = []
    for p in range(4):
        loads[1 + p].wait()
        at = pl.ds(p * rows, rows)
        hidden = nn(tokens_s[at, :], w_s[...]) + bias_ref[...]
        phi = 0.5 * (1.0 + lax.erf(hidden * (1.0 / math.sqrt(2.0))))
        act_s[at, :] = (hidden * phi).astype(BF16)
        bell = jnp.exp(-0.5 * hidden * hidden) * (1.0 / math.sqrt(2.0 * math.pi))
        slope_s[at, :] = (phi + hidden * bell).astype(BF16)
        stores += copies(
            [(act_s.at[at, :], act_ref.at[at, :]), (slope_s.at[at, :], slope_ref.at[at, :])],
            out_sems,
            2 * p,
        )
    for copy in loads[5:]:
        copy.wait()
    count, block, _ = near_ref.shape
    send = send_pairs(near_s, own_s, near_ref, own_ref, out_sems, 8)

    def one_pair(m, carry):
        product = tn(act_s[:, pair_rows(place_ref, m, 2 * block)], grads_s[...])
        put_pair(place_ref, m, product, near_s, own_s)
        for copy in send(m):
            copy.start()
        return carry

    lax.fori_loop(0, count, one_pair, 0)
    for m in range(count):
        stores += send(m)
    for copy in stores:
        copy.wait()


def hidden_layer(place, parts, w, bias, pairs):
    _, rows, width = parts[0].shape
    units = w.shape[1]
    blocks = (pairs, units // (2 * pairs), width)
    return pl.pallas_call(
        hidden_kernel,
        in_specs=[SMEM] + [ANY] * 5 + [VMEM],
        out_specs=[ANY] * 4,
        out_shape=[shape_of((4 * rows, units))] * 2 + [shape_of(blocks)] * 2,
        scratch_shapes=[pltpu.VMEM((4 * rows, width), BF16)] * 2
        + [pltpu.VMEM(w.shape, BF16)]
        + [pltpu.VMEM((4 * rows, units), BF16)] * 2
        + [pltpu.VMEM(blocks, BF16)] * 2
        + [pltpu.SemaphoreType.DMA((9,)), pltpu.SemaphoreType.DMA((8 + 2 * pairs,))],
        compiler_params=PARAMS,
        cost_estimate=cost(1.2e10, 20 << 20),
        name="hidden",
    )(place, *parts, w, bias)


def unhidden_kernel(
    place_ref,
    a_ref,
    b_ref,
    c_ref,
    d_ref,
    w_ref,
    slope_ref,
    grad_ref,
    near_ref,
    own_ref,
    sum_ref,
    grads_s,
    tokens_s,
    w_s,
    slope_s,
    near_s,
    own_s,
    in_sems,
    out_sems,
):
    rows = a_ref.shape[1]
    parts = (a_ref, b_ref, c_ref, d_ref)
    loads = copies([(w_ref, w_s)], in_sems)
    loads += loaded(parts, grads_s, in_sems, 1, 1)
    loads += copies(
        [
            (slope_ref.at[pl.ds(p * rows, rows), :], slope_s.at[pl.ds(p * rows, rows), :])
            for p in range(4)
        ],
        in_sems,
        5,
    )
    loads += loaded(parts, tokens_s, in_sems, 9, 0)
    loads[0].wait()
    stores = []
    for p in range(4):
        loads[1 + p].wait()
        loads[5 + p].wait()
        at = pl.ds(p * rows, rows)
        grad = (nt(grads_s[at, :], w_s[...]) * slope_s[at, :].astype(F32)).astype(BF16)
        slope_s[at, :] = grad
        part = jnp.sum(grad.astype(F32), axis=0, keepdims=True)
        if p == 0:
            sum_ref[...] = part
        else:
            sum_ref[...] += part
        stores += copies([(slope_s.at[at, :], grad_ref.at[at, :])], out_sems, p)
    for copy in loads[9:]:
        copy.wait()
    count, block, _ = near_ref.shape
    for m in range(count):
        product = tn(tokens_s[:, pair_rows(place_ref, m, 2 * block)], slope_s[...])
        put_pair(place_ref, m, product, near_s, own_s)
        stores += copies(
            [(near_s.at[m], near_ref.at[m]), (own_s.at[m], own_ref.at[m])], out_sems, 4 + 2 * m
        )
    for copy in stores:
        copy.wait()


def unhidden_layer(place, parts, w, slope, pairs):
    _, rows, width = parts[0].shape
    units = w.shape[0]
    blocks = (pairs, width // (2 * pairs), units)
    return pl.pallas_call(
        unhidden_kernel,
        in_specs=[SMEM] + [ANY] * 6,
        out_specs=[ANY] * 3 + [VMEM],
        out_shape=[shape_of((4 * rows, units))]
        + [shape_of(blocks)] * 2
        + [shape_of((1, units), F32)],
        scratch_shapes=[pltpu.VMEM((4 * rows, width), BF16)] * 2
        + [pltpu.VMEM(w.shape, BF16)]
        + [pltpu.VMEM((4 * rows, units), BF16)]
        + [pltpu.VMEM(blocks, BF16)] * 2
        + [pltpu.SemaphoreType.DMA((13,)), pltpu.SemaphoreType.DMA((4 + 2 * pairs,))],
        compiler_params=PARAMS,
        cost_estimate=cost(1.2e10, 22 << 20),
        name="unhidden",
    )(place, *parts, w, slope)


def attention_grads_kernel(
    place_ref,
    a_ref,
    b_ref,
    c_ref,
    d_ref,
    mixed_one_ref,
    pg_one_ref,
    mixed_two_ref,
    pg_two_ref,
    near_ref,
    late_ref,
    own_ref,
    grads_s,
    tokens_s,
    mixed_s,
    pg_s,
    dense_s,
    near_s,
    own_s,
    in_sems,
    out_sems,
):
    parts = (a_ref, b_ref, c_ref, d_ref)
    mixed = [ref.at[p] for ref in (mixed_one_ref, mixed_two_ref) for p in range(2)]
    pg = [ref.at[p] for ref in (pg_one_ref, pg_two_ref) for p in range(2)]
    loads = loaded(parts, grads_s, in_sems, 0, 1)
    loads += loaded(mixed, mixed_s, in_sems, 4)
    loads += loaded(parts, tokens_s, in_sems, 8, 0)
    loads += loaded(pg, pg_s, in_sems, 12)
    for copy in loads[:8]:
        copy.wait()
    count, block, columns = own_ref.shape
    wide = pg_s.shape[1]
    few = block // 4
    dense_s[...] = tn(mixed_s[...], grads_s[...])
    for copy in loads[8:]:
        copy.wait()
    across = columns // 4
    swap = (place_ref[0] & 1) == 1
    stores = []
    for m in (2, 3, 0, 1):
        product = tn(tokens_s[:, pair_rows(place_ref, m, 2 * block)], pg_s[...])
        put_pair(place_ref, m, product, near_s, own_s, slice(0, wide))
        product = dense_s[pair_rows(place_ref, m, 2 * few), :]
        low, high = product[:few], product[few:]
        own = jnp.where(swap, high, low).astype(BF16)
        near = jnp.where(swap, low, high).astype(BF16)
        for j in range(4):
            cols = slice(j * across, (j + 1) * across)
            own_s[m, j * few : (j + 1) * few, wide:] = own[:, cols]
            near_s[m, j * few : (j + 1) * few, wide:] = near[:, cols]
        near_at = near_ref if m >= count // 2 else late_ref
        stores += copies(
            [(near_s.at[m], near_at.at[m % 2]), (own_s.at[m], own_ref.at[m])], out_sems, 2 * m
        )
    for copy in stores:
        copy.wait()


def attention_grads(place, parts, one, two, pairs):
    _, rows, width = parts[0].shape
    heads = one[0].shape[-1]
    wide = one[1].shape[-1]
    blocks = (pairs, width // (2 * pairs), wide + heads)
    return pl.pallas_call(
        attention_grads_kernel,
        in_specs=[SMEM] + [ANY] * 8,
        out_specs=[ANY] * 3,
        out_shape=[shape_of((pairs // 2,) + blocks[1:])] * 2 + [shape_of(blocks)],
        scratch_shapes=[pltpu.VMEM((4 * rows, width), BF16)] * 2
        + [pltpu.VMEM((4 * rows, heads), BF16), pltpu.VMEM((4 * rows, wide), BF16)]
        + [pltpu.VMEM((heads, width), F32)]
        + [pltpu.VMEM(blocks, BF16)] * 2
        + [pltpu.SemaphoreType.DMA((16,)), pltpu.SemaphoreType.DMA((2 * pairs,))],
        compiler_params=PARAMS,
        cost_estimate=cost(7e9, 16 << 20),
        name="attention_grads",
    )(place, *parts, *one, *two)


def results_kernel(
    mixed_ref,
    pg_ref,
    act_ref,
    grad_ref,
    dense_ref,
    shrink_ref,
    project_ref,
    expand_ref,
    mine_ref,
    theirs_ref,
    mixed_s,
    pg_s,
    act_s,
    grad_s,
    dense_s,
    shrink_s,
    project_s,
    expand_s,
    out_s,
    in_sems,
    out_sems,
    *,
    first,
):
    rows = mixed_ref.shape[1]
    theirs = pl.ds((first + 1) * rows, rows)
    mine = pl.ds(first * rows, rows)
    loads = copies(
        [
            (shrink_ref, shrink_s),
            (act_ref.at[theirs, :], act_s.at[1]),
            (mixed_ref, mixed_s),
            (dense_ref, dense_s),
            (expand_ref, expand_s),
            (grad_ref.at[theirs, :], grad_s.at[1]),
            (pg_ref, pg_s),
            (project_ref, project_s),
            (act_ref.at[mine, :], act_s.at[0]),
            (grad_ref.at[mine, :], grad_s.at[0]),
        ],
        in_sems,
    )
    stores = []
    for at, (piece, gradient, waits) in enumerate(
        ((1, 0, loads[:4]), (1, 1, loads[4:8]), (0, 0, loads[8:9]), (0, 1, loads[9:]))
    ):
        for copy in waits:
            copy.wait()
        if gradient:
            total = nt(grad_s[piece], expand_s[...]) + nt(pg_s[piece], project_s[...])
        else:
            total = nn(act_s[piece], shrink_s[...]) + nn(mixed_s[piece], dense_s[...])
        out_s[at] = total.astype(BF16)
        out_ref = theirs_ref if piece else mine_ref
        stores += copies([(out_s.at[at], out_ref.at[gradient])], out_sems, at)
    for copy in stores:
        copy.wait()


def results(mixed, pg, act, grad, dense, shrink, project, expand, first):
    _, rows, heads = mixed.shape
    wide = pg.shape[-1]
    units = act.shape[-1]
    width = dense.shape[1]
    return pl.pallas_call(
        functools.partial(results_kernel, first=first),
        in_specs=[ANY] * 8,
        out_specs=[ANY] * 2,
        out_shape=[shape_of((2, rows, width))] * 2,
        scratch_shapes=[pltpu.VMEM(mixed.shape, BF16), pltpu.VMEM(pg.shape, BF16)]
        + [pltpu.VMEM((2, rows, units), BF16)] * 2
        + [pltpu.VMEM(w.shape, BF16) for w in (dense, shrink, project, expand)]
        + [pltpu.VMEM((4, rows, width), BF16)]
        + [pltpu.SemaphoreType.DMA((10,)), pltpu.SemaphoreType.DMA((4,))],
        compiler_params=PARAMS,
        cost_estimate=cost(8e9, 16 << 20),
        name="results",
    )(mixed, pg, act, grad, dense, shrink, project, expand)


def exchange(value, axis, size, offset):
    return lax.ppermute(value, axis, [(i, i ^ offset) for i in range(size)])


def sum_over(value, axis, size, offset=1):
    while offset < size:
        value = value + exchange(value, axis, size, offset)
        offset *= 2
    return value


def slots(value, index, size):
    row = lax.broadcasted_iota(jnp.int32, (size, 1), 0)
    return jnp.where(row == index, value[None, :], 0.0)


def after(values, *first):
    return lax.optimization_barrier(tuple(values) + first)[: len(values)]


def hop(value, size, offset):
    return exchange(value, "fsdp", size, offset)


class Gather:
    def __init__(self, block, size, near=True):
        self.own, self.size = block, size
        self.far = hop(block, size, 4)
        self.near = hop(block, size, 1) if near else None
        self.far_near = None

    def second(self, *first):
        own, far = after((self.own, self.far), *first) if first else (self.own, self.far)
        self.pair = hop(jnp.stack([own, far]), self.size, 2)
        if self.far_near is None:
            self.far_near = hop(far, self.size, 1)

    def second_near(self):
        self.far_near = hop(self.far, self.size, 1)

    def third(self, *first):
        (pair,) = after((self.pair,), *first) if first else (self.pair,)
        self.pair_near = hop(pair, self.size, 1)

    def blocks(self, *first):
        every = (self.own, self.near, self.far, self.far_near, self.pair, self.pair_near)
        return after(every, *first) if first else every


class Scatter:
    def __init__(self, near, own, size, late=None):
        self.own, self.size = own, size
        if late is None:
            near = hop(near, size, 1)
            self.near, self.late = near[2:], near[:2]
            self.arrived = near
        else:
            self.near, self.late = hop(near, size, 1), hop(late, size, 1)
            self.arrived = self.near

    def second(self, *first):
        near, own = after((self.near, self.own[2:]), *first)
        self.pair = hop((own.astype(F32) + near.astype(F32)).astype(BF16), self.size, 2)
        return self.arrived

    def third(self, *first):
        pair, near = after((self.pair, self.late), *first) if first else (self.pair, self.late)
        total = self.own[1].astype(F32) + near[1].astype(F32) + pair[1].astype(F32)
        self.far = hop(total.astype(BF16), self.size, 4)
        return pair

    def terms(self):
        return self.own, self.late, self.pair, self.far

    def total(self):
        return sum(term.astype(F32) for term in (self.own[0], self.late[0], self.pair[0], self.far))


def row_of(value):
    return jnp.broadcast_to(value, (value.shape[0], 128)).T[:1, :]


def block_total(own_ref, late_ref, pair_ref, far_ref, columns):
    total = own_ref[:, columns].astype(F32) + late_ref[:, columns].astype(F32)
    return total + pair_ref[:, columns].astype(F32) + far_ref[:, columns].astype(F32)


def finish_project_kernel(
    own_ref, late_ref, pair_ref, far_ref, w_ref, sum_ref, vector_ref, grad_ref, dense_ref, part_ref
):
    wide = w_ref.shape[1]
    heads = wide // (3 * HD)
    gain, shift = column(vector_ref[0:1, :]), column(vector_ref[1:2, :])
    first = second = 0.0
    for head in range(heads):
        for part in range(3):
            at = (part * heads + head) * HD
            to = (head * 3 + part) * HD
            total = block_total(own_ref, late_ref, pair_ref, far_ref, slice(at, at + HD))
            weight = w_ref[:, to : to + HD].astype(F32)
            sums = sum_ref[:, at : at + HD]
            grad_ref[:, to : to + HD] = gain * total + shift * sums
            first = first + jnp.sum(weight * total, axis=1, keepdims=True)
            second = second + jnp.sum(weight * sums, axis=1, keepdims=True)
    part_ref[0:1, :] = row_of(first)
    part_ref[1:2, :] = row_of(second)
    rows, width = dense_ref.shape
    across = width // 4
    total = block_total(own_ref, late_ref, pair_ref, far_ref, slice(wide, wide + across))
    for j in range(4):
        dense_ref[:, j * across : (j + 1) * across] = total[j * rows : (j + 1) * rows, :]


def finish_project(terms, weight, sums, vectors, rows):
    width = weight.shape[0] * 8
    lead = pl.BlockSpec((None, weight.shape[0], width), lambda i: (0, 0, 0))
    whole = [
        pl.BlockSpec(shape, lambda i: (0, 0))
        for shape in (terms[3].shape, weight.shape, sums.shape, vectors.shape)
    ]
    outs = (weight.shape, (rows, width), (2, weight.shape[0]))
    return pl.pallas_call(
        finish_project_kernel,
        grid=(1,),
        in_specs=[lead] * 3 + whole,
        out_specs=[pl.BlockSpec(shape, lambda i: (0, 0)) for shape in outs],
        out_shape=[shape_of(shape, F32) for shape in outs],
        compiler_params=PARAMS,
        cost_estimate=cost(0, 4 << 20),
        name="finish_project",
    )(*terms, weight, sums, vectors)


def finish_expand_kernel(
    own_ref, late_ref, pair_ref, far_ref, w_ref, sum_ref, vector_ref, grad_ref, part_ref
):
    gain, shift = column(vector_ref[2:3, :]), column(vector_ref[3:4, :])
    total = block_total(own_ref, late_ref, pair_ref, far_ref, slice(None))
    weight = w_ref[...].astype(F32)
    grad_ref[...] = gain * total + shift * sum_ref[...]
    part_ref[0:1, :] = row_of(jnp.sum(weight * total, axis=1, keepdims=True))
    part_ref[1:2, :] = row_of(jnp.sum(weight * sum_ref[...], axis=1, keepdims=True))


def finish_expand(terms, weight, sums, vectors):
    lead = pl.BlockSpec((None,) + weight.shape, lambda i: (0, 0, 0))
    whole = [
        pl.BlockSpec(shape, lambda i: (0, 0))
        for shape in (terms[3].shape, weight.shape, sums.shape, vectors.shape)
    ]
    outs = (weight.shape, (2, weight.shape[0]))
    return pl.pallas_call(
        finish_expand_kernel,
        grid=(1,),
        in_specs=[lead] * 3 + whole,
        out_specs=[pl.BlockSpec(shape, lambda i: (0, 0)) for shape in outs],
        out_shape=[shape_of(shape, F32) for shape in outs],
        compiler_params=PARAMS,
        cost_estimate=cost(0, 4 << 20),
        name="finish_expand",
    )(*terms, weight, sums, vectors)


def finish_tokens_kernel(
    mine_ref, near_ref, far_ref, inputs_ref, cotangent_ref, keep_ref, bias_ref, out_ref, grad_ref
):
    def total(which):
        return (
            mine_ref[which].astype(F32) + near_ref[which].astype(F32) + far_ref[which].astype(F32)
        )

    features = inputs_ref[...].astype(F32)
    out_ref[...] = (features + total(0) + bias_ref[...]).astype(BF16)
    normed, rate = normalise(features)
    grad = total(1)
    inner = jnp.mean(grad * normed, axis=-1, keepdims=True)
    centre = jnp.mean(grad, axis=-1, keepdims=True)
    upstream = cotangent_ref[...].astype(F32) * keep_ref[...]
    grad_ref[...] = (upstream + rate * (grad - centre - normed * inner)).astype(BF16)


def finish_tokens(mine, near, far, inputs, cotangent, keep, bias):
    rows, width = inputs.shape
    step = rows // 4
    both = pl.BlockSpec((2, step, width), lambda i: (0, i, 0))
    block = pl.BlockSpec((step, width), lambda i: (i, 0))
    return pl.pallas_call(
        finish_tokens_kernel,
        grid=(4,),
        in_specs=[both] * 3
        + [block] * 2
        + [pl.BlockSpec((step, 1), lambda i: (i, 0)), pl.BlockSpec((1, width), lambda i: (0, 0))],
        out_specs=[block] * 2,
        out_shape=[shape_of((rows, width))] * 2,
        compiler_params=PARAMS,
        cost_estimate=cost(0, 12 << 20),
        name="finish_tokens",
    )(mine, near, far, inputs, cotangent, keep, bias)


def by_part(array):
    shape = array.shape
    array = array.reshape(shape[:-1] + (shape[-1] // (3 * HD), 3, HD))
    return jnp.swapaxes(array, -3, -2).reshape(shape)


def by_head(array):
    shape = array.shape
    array = array.reshape(shape[:-1] + (3, shape[-1] // (3 * HD), HD))
    return jnp.swapaxes(array, -3, -2).reshape(shape)


def gathered(weight):
    return lax.all_gather(weight, "fsdp", axis=0, tiled=True)


def folded(weight, gain, shift, offset):
    weight = gathered(weight).astype(F32)
    bias = offset[None, :] + jnp.sum(weight * shift[:, None], axis=0, keepdims=True)
    return (weight * gain[:, None]).astype(BF16), bias


def whole_rows(own, near):
    whole = jnp.stack([own, near], axis=1).astype(F32)[jnp.array([0, 2, 1, 3])]
    return whole.reshape(-1, whole.shape[-1])


def scattered(value):
    return lax.psum_scatter(value, "fsdp", scatter_dimension=0, tiled=True)


def local(
    inputs,
    segments,
    cotangent,
    attention_gain,
    attention_shift,
    feedforward_gain,
    feedforward_shift,
    project_weight,
    project_bias,
    dense_weight,
    dense_bias,
    expand_weight,
    expand_bias,
    shrink_weight,
    shrink_bias,
):
    size = lax.axis_size("fsdp")
    across = lax.axis_size("tensor")
    rows, width = inputs.shape
    assert across == 4 and 2 * rows == SEQ_LEN and segments.shape[0] == 2 * SEQ_LEN
    index = lax.axis_index("fsdp")
    rank = lax.axis_index("tensor")
    core = (rank % 2).astype(jnp.int32)[None]
    chip = rank // 2
    block = width // size
    pairs = 4
    direct = size == 2 * pairs
    place = (index if direct else index * 0).astype(jnp.int32)[None]

    own_labels = lax.dynamic_slice_in_dim(segments, rank * rows, rows, 0)
    keep = (own_labels != 0).astype(F32)[:, None]
    early = inputs
    if direct:
        first = Gather(expand_weight, size)
    packed_weights, *tables = pack(project_weight, dense_weight, rotary_turns())
    if direct:
        (early,) = after((early,), packed_weights)
    own, bias_grad = prepare(early, cotangent, keep)

    small = jnp.concatenate(
        [
            attention_gain,
            attention_shift,
            feedforward_gain,
            feedforward_shift,
            dense_bias + shrink_bias,
        ]
    )
    piece = small.shape[0] // 5
    small = slots(small, rank, across)
    small_far = small + exchange(small, "tensor", across, 2)
    small = small_far + exchange(small_far, "tensor", across, 1)
    own_vectors = jnp.swapaxes(small.reshape(across, 5, piece), 0, 1).reshape(5, block)
    counts = (5 * block, project_bias.shape[0], expand_bias.shape[0])
    packed = jnp.concatenate(
        [own_vectors.reshape(-1), project_bias.astype(F32), expand_bias.astype(F32)]
    )
    packed = slots(packed, index, size)
    packed_near = packed + exchange(packed, "fsdp", size, 1)
    if direct:
        (packed_near,) = after((packed_near,), first.far, first.near, own)
    if direct:
        packed_far = packed_near + exchange(packed_near, "fsdp", size, 4)
        packed = packed_far + exchange(packed_far, "fsdp", size, 2)
    else:
        packed = sum_over(packed_near, "fsdp", size, 2)
    vectors = jnp.swapaxes(packed[:, : counts[0]].reshape(size, 5, block), 0, 1).reshape(5, width)
    project_offset = by_part(packed[:, counts[0] : counts[0] + counts[1]].reshape(-1))
    expand_offset = packed[:, counts[0] + counts[1] :].reshape(-1)

    (own,) = after((own,), small_far)

    def chip_pair(value):
        return exchange(value, "tensor", across, 1)

    def other_chip(value):
        return exchange(value, "tensor", across, 2)

    labels = segments.reshape(2, SEQ_LEN)
    labels = jnp.where(chip == 0, labels, labels[::-1])
    places = jnp.arange(SEQ_LEN, dtype=jnp.int32)[None, :]
    marks = jnp.where(labels != 0, labels, -1 - places)
    across_chip = other_chip(own)
    own_near, _ = after((own, small), packed_far) if direct else (own, small)
    partner = chip_pair(own_near)
    if direct:
        first.second_near()
        (near_block,) = after((shrink_weight,), packed_near)
        near_block = hop(near_block, size, 1)
        first.second(packed)
        (far_block,) = after((shrink_weight,), packed)
        second = Gather(far_block, size, False)
        second.near = near_block
        second.second(first.pair, first.far_near)
        (far_block,) = after((packed_weights,), second.far)
        third = Gather(far_block, size, False)
        first.third(first.far_near, near_block)
        expand, expand_row = join_expand(
            place,
            first.blocks(),
            vectors[2][None, :],
            vectors[3][None, :],
            expand_offset[None, :],
        )
        across_chip, expand = after(
            (across_chip, expand), second.far_near, second.pair, third.far, partner
        )
        second.third(expand)
        third.second(second.pair)
    else:
        expand, expand_row = folded(expand_weight, vectors[2], vectors[3], expand_offset)
        project, project_row = folded(
            by_part(project_weight), vectors[0], vectors[1], project_offset
        )
        dense = gathered(dense_weight)
        shrink = gathered(shrink_weight)
    parts = (own, partner, across_chip, chip_pair(across_chip))

    active, slope, shrink_near, shrink_own = hidden_layer(place, parts, expand, expand_row, pairs)
    if direct:
        shrink_sums = Scatter(shrink_near, shrink_own, size)
        (near_block,) = after((packed_weights,), shrink_own)
        third.near = hop(near_block, size, 1)
        third.third(shrink_own)
        shrink = join(place, second.blocks(shrink_own))
    hidden_grad, expand_near, expand_own, expand_offset_grad = unhidden_layer(
        place, parts, shrink, slope, pairs
    )
    if direct:
        expand_sums = Scatter(expand_near, expand_own, size)
        project, dense, project_row = join_project(
            place,
            third.blocks(expand_own),
            vectors[0][None, :],
            vectors[1][None, :],
            project_offset[None, :],
        )
    else:
        (project,) = after((project,), expand_own)

    def attend(sequence):
        at = slice(2 * sequence, 2 * sequence + 2)
        return attention(core, parts[at], project, project_row, dense, marks[sequence], tables)

    two = attend(1)
    weights = (dense, shrink, project, expand)
    act = active
    if direct:
        ready = shrink_sums.second(two[2])
        (act,) = after((active,), ready)
    far_mine, far_theirs = results(two[0], two[1], act, hidden_grad, *weights, first=2)
    far = chip_pair(far_theirs)
    far_sum = (far_mine.astype(F32) + far.astype(F32)).astype(BF16)
    far = other_chip(far_sum)
    if direct:
        ready = shrink_sums.third(far_mine)
        more = expand_sums.second(far_mine)
        (project,) = after((project,), ready, more)
    else:
        (project,) = after((project,), far_mine)
    one = attend(0)
    if direct:
        ready = expand_sums.third(one[2])
        (pair_grads,) = after((one[1],), ready, shrink_sums.far, far_sum)
        one = (one[0], pair_grads, one[2])
    both_near, both_late, both_own = attention_grads(place, parts, one[:2], two[:2], pairs)
    project_offset_grad = one[2] + two[2]
    wide = project_offset_grad.shape[1]
    units = expand_offset_grad.shape[1]
    few = dense_weight.shape[0]
    totals = jnp.concatenate([project_offset_grad, expand_offset_grad, bias_grad], axis=1)
    (totals,) = after((totals,), both_own)
    totals = totals_near = totals + exchange(totals, "fsdp", size, 1)
    if direct:
        totals = totals_pair = totals + exchange(totals, "fsdp", size, 2)
        totals = totals + exchange(totals, "fsdp", size, 4)
    else:
        totals = sum_over(totals, "fsdp", size, 2)
    project_totals = totals[:, :wide]
    expand_totals = totals[:, wide : wide + units]
    bias_totals = totals[0, wide + units :]

    act = active
    if direct:
        both_sums = Scatter(both_near, both_own, size, both_late)
        (act,) = after((active,), both_own, expand_sums.far)
    near_mine, near_theirs = results(one[0], one[1], act, hidden_grad, *weights, first=0)
    def mine(vector, count, start):
        return lax.dynamic_slice_in_dim(vector, start * count, count, 0)

    own_rows = own_vectors[:4]
    if direct:
        both_sums.second(near_mine, totals_pair)
        shrink_sum = shrink_sums.total()
        ready = both_sums.third(shrink_sum)
        (expand_totals,) = after((expand_totals,), ready)
        expand_gradient, expand_parts = finish_expand(
            expand_sums.terms(), expand_weight, expand_totals, own_rows
        )
        far, near_mine, near_theirs = after((far, near_mine, near_theirs), ready)
        near = chip_pair(near_theirs)
        output, inputs_gradient = finish_tokens(
            near_mine, near, far, inputs, cotangent, keep, vectors[4][None, :]
        )
        (project_totals,) = after((project_totals,), output, expand_parts)
        project_gradient, dense_sum, project_parts = finish_project(
            both_sums.terms(), project_weight, project_totals, own_rows, few
        )
        partial = [project_parts, expand_parts]
    else:
        near = chip_pair(near_theirs)
        output, inputs_gradient = finish_tokens(
            near_mine, near, far, inputs, cotangent, keep, vectors[4][None, :]
        )
        shrink_sum = scattered(whole_rows(shrink_own, shrink_near))
        expand_sum = scattered(whole_rows(expand_own, expand_near))
        both = whole_rows(both_own, jnp.concatenate([both_late, both_near]))
        project_sum = scattered(both[:, :wide])
        dense_sum = both[:, wide:].reshape(2 * pairs, 4, -1, width // 4)
        dense_sum = scattered(jnp.swapaxes(dense_sum, 1, 2).reshape(-1, width))
        columns = own_rows[:, :, None]
        project_gradient = by_head(columns[0] * project_sum + columns[1] * project_totals)
        expand_gradient = columns[2] * expand_sum + columns[3] * expand_totals
        own_project = by_part(project_weight).astype(F32)
        own_expand = expand_weight.astype(F32)
        partial = [
            jnp.sum(term, axis=1)[None, :]
            for term in (
                own_project * project_sum,
                own_project * project_totals,
                own_expand * expand_sum,
                own_expand * expand_totals,
            )
        ]
    partial = jnp.concatenate(partial + [mine(bias_totals, block, index)[None, :]])
    partial = sum_over(partial, "tensor", across)
    partial = lax.dynamic_slice_in_dim(partial, rank * piece, piece, 1)
    return (
        output,
        inputs_gradient,
        partial[0],
        partial[1],
        partial[2],
        partial[3],
        project_gradient,
        mine(by_head(project_totals[0]), project_bias.shape[0], index),
        dense_sum,
        partial[4],
        expand_gradient,
        mine(expand_totals[0], expand_bias.shape[0], index),
        shrink_sum,
        partial[4],
    )


def solution(mesh):
    in_specs = (
        P(("fsdp", "tensor"), None),
        P("fsdp"),
        P(("fsdp", "tensor"), None),
        P(("fsdp", "tensor")),
        P(("fsdp", "tensor")),
        P(("fsdp", "tensor")),
        P(("fsdp", "tensor")),
        P("fsdp", "tensor"),
        P(("tensor", "fsdp")),
        P(("tensor", "fsdp"), None),
        P(("fsdp", "tensor")),
        P("fsdp", "tensor"),
        P(("tensor", "fsdp")),
        P(("tensor", "fsdp"), None),
        P(("fsdp", "tensor")),
    )
    out_specs = (
        P(("fsdp", "tensor"), None),
        P(("fsdp", "tensor"), None),
        P(("fsdp", "tensor")),
        P(("fsdp", "tensor")),
        P(("fsdp", "tensor")),
        P(("fsdp", "tensor")),
        P("fsdp", "tensor"),
        P(("tensor", "fsdp")),
        P(("tensor", "fsdp"), None),
        P(("fsdp", "tensor")),
        P("fsdp", "tensor"),
        P(("tensor", "fsdp")),
        P(("tensor", "fsdp"), None),
        P(("fsdp", "tensor")),
    )
    return jax.shard_map(local, mesh=mesh, in_specs=in_specs, out_specs=out_specs, check_vma=False)
```

```python
import functools
import math

import jax
import jax.numpy as jnp
from jax import lax
from jax.experimental import pallas as pl
from jax.experimental.pallas import tpu as pltpu
from jax.sharding import PartitionSpec as P

HD = 64
ROT = 16
SEQ_LEN = 1024
EPS = 1e-05
NEGATIVE = -1e30
QB = 256
CHUNK = 128
PARAMS = pltpu.CompilerParams(vmem_limit_bytes=60 * 1024 * 1024)
BF16 = jnp.bfloat16
F32 = jnp.float32
COST = 1.0
VMEM = pl.BlockSpec(memory_space=pltpu.VMEM)
SMEM = pl.BlockSpec(memory_space=pltpu.SMEM)
ANY = pl.BlockSpec(memory_space=pl.ANY)


def shape_of(dims, kind=BF16):
    return jax.ShapeDtypeStruct(dims, kind)


def cost(flops, moved):
    return pl.CostEstimate(
        flops=int(flops * COST), bytes_accessed=int(moved * COST), transcendentals=0
    )


def nn(left, right):
    return lax.dot_general(left, right, (((1,), (0,)), ((), ())), preferred_element_type=F32)


def nt(left, right):
    return lax.dot_general(left, right, (((1,), (1,)), ((), ())), preferred_element_type=F32)


def tn(left, right):
    return lax.dot_general(left, right, (((0,), (0,)), ((), ())), preferred_element_type=F32)


def copies(pairs, sems, first=0):
    made = [pltpu.make_async_copy(s, d, sems.at[first + i]) for i, (s, d) in enumerate(pairs)]
    for copy in made:
        copy.start()
    return made


def pack_kernel(project_ref, dense_ref, turns_ref, out_ref, cos_ref, up_ref, dn_ref):
    heads = project_ref.shape[1] // (3 * HD)
    rows = dense_ref.shape[0]
    width = heads * HD
    for part in range(3):
        pieces = [
            project_ref[:, (3 * head + part) * HD : (3 * head + part + 1) * HD]
            for head in range(heads)
        ]
        out_ref[:, part * width : (part + 1) * width] = jnp.concatenate(pieces, axis=1)
    for j in range(4):
        columns = slice(j * width, (j + 1) * width)
        out_ref[j * rows : (j + 1) * rows, 3 * width :] = dense_ref[:, columns]
    half = ROT // 2
    length = turns_ref.shape[0]
    cosine, sine = turns_ref[:, :half], turns_ref[:, half:]
    rest = jnp.zeros((length, HD - ROT), F32)
    none = jnp.zeros((length, half), F32)
    cos_ref[...] = jnp.concatenate([cosine, cosine, rest + 1.0] * 2, axis=1)
    up_ref[...] = jnp.concatenate([none, sine, rest] * 2, axis=1)
    dn_ref[...] = jnp.concatenate([-sine, none, rest] * 2, axis=1)


def pack(project, dense, turns):
    table = shape_of((turns.shape[0], 2 * HD), F32)
    return pl.pallas_call(
        pack_kernel,
        in_specs=[VMEM] * 3,
        out_specs=[VMEM] * 4,
        out_shape=[shape_of((project.shape[0], dense.shape[1]))] + [table] * 3,
        compiler_params=PARAMS,
        cost_estimate=cost(0, 3 << 20),
        name="pack",
    )(project, dense, turns)


def column(row):
    return jnp.broadcast_to(row, (8, row.shape[1])).T[:, :1]


def shift_times(shift, weight):
    high = shift.astype(BF16)
    rest = shift - high.astype(F32)
    middle = rest.astype(BF16)
    low = (rest - middle.astype(F32)).astype(BF16)
    parts = nn(jnp.concatenate([high, middle, low], axis=0), weight)
    return jnp.sum(parts, axis=0, keepdims=True)


def scaled_rows(place, k, weight, gain_ref, shift_ref):
    rows = weight.shape[0]
    start = pl.multiple_of(lax.bitwise_xor(place, k) * rows, rows)
    part = shift_times(shift_ref[:, pl.ds(start, rows)], weight)
    gain = column(gain_ref[:, pl.ds(start, rows)])
    return start, (weight.astype(F32) * gain).astype(BF16), part


def block_list(refs):
    own, near, far, far_near, pair, pair_near = refs
    return [own, near, pair.at[0], pair_near.at[0], far, far_near, pair.at[1], pair_near.at[1]]


def join_project_kernel(place_ref, *refs):
    gain_ref, shift_ref, offset_ref, project_ref, dense_ref, bias_ref = refs[6:]
    total = offset_ref[...]
    wide = project_ref.shape[1]
    for k, ref in enumerate(block_list(refs[:6])):
        block = ref[...]
        start, scaled, part = scaled_rows(
            place_ref[0], k, block[:, :wide], gain_ref, shift_ref
        )
        project_ref[pl.ds(start, block.shape[0]), :] = scaled
        total = total + part
        rows = block.shape[0] // 4
        across = block.shape[1] // 4
        base = pl.multiple_of(lax.bitwise_xor(place_ref[0], k) * rows, rows)
        for j in range(4):
            dense_ref[pl.ds(base, rows), j * across : (j + 1) * across] = block[
                j * rows : (j + 1) * rows, wide:
            ]
    bias_ref[...] = total


def join_project(place, blocks, gain, shift, offset):
    rows, columns = blocks[0].shape
    total = 8 * rows
    wide = offset.shape[1]
    return pl.pallas_call(
        join_project_kernel,
        in_specs=[SMEM] + [VMEM] * 9,
        out_specs=[VMEM] * 3,
        out_shape=[
            shape_of((total, wide)),
            shape_of((total // 4, columns)),
            shape_of((1, wide), F32),
        ],
        compiler_params=PARAMS,
        cost_estimate=cost(1e9, 10 << 20),
        name="join_project",
    )(place, *blocks, gain, shift, offset)


def join_expand_kernel(place_ref, *refs):
    gain_ref, shift_ref, offset_ref, out_ref, bias_ref = refs[6:]
    total = offset_ref[...]
    for k, ref in enumerate(block_list(refs[:6])):
        start, scaled, part = scaled_rows(place_ref[0], k, ref[...], gain_ref, shift_ref)
        out_ref[pl.ds(start, scaled.shape[0]), :] = scaled
        total = total + part
    bias_ref[...] = total


def join_expand(place, blocks, gain, shift, offset):
    rows, columns = blocks[0].shape
    return pl.pallas_call(
        join_expand_kernel,
        in_specs=[SMEM] + [VMEM] * 9,
        out_specs=[VMEM] * 2,
        out_shape=[shape_of((8 * rows, columns)), shape_of((1, columns), F32)],
        compiler_params=PARAMS,
        cost_estimate=cost(1e9, 6 << 20),
        name="join_expand",
    )(place, *blocks, gain, shift, offset)


def join_kernel(place_ref, *refs):
    out_ref = refs[6]
    for k, ref in enumerate(block_list(refs[:6])):
        rows = ref.shape[0]
        start = pl.multiple_of(lax.bitwise_xor(place_ref[0], k) * rows, rows)
        out_ref[pl.ds(start, rows), :] = ref[...]


def join(place, blocks):
    rows, columns = blocks[0].shape
    return pl.pallas_call(
        join_kernel,
        in_specs=[SMEM] + [VMEM] * 6,
        out_specs=VMEM,
        out_shape=shape_of((8 * rows, columns)),
        compiler_params=PARAMS,
        cost_estimate=cost(0, 4 << 20),
        name="join",
    )(place, *blocks)


def normalise(features):
    centre = features - jnp.mean(features, axis=-1, keepdims=True)
    rate = lax.rsqrt(jnp.mean(centre * centre, axis=-1, keepdims=True) + EPS)
    return centre * rate, rate


def prepare_kernel(inputs_ref, cotangent_ref, keep_ref, both_ref, sum_ref):
    both_ref[0] = normalise(inputs_ref[...].astype(F32))[0].astype(BF16)
    upstream = cotangent_ref[...].astype(F32) * keep_ref[...]
    both_ref[1] = upstream.astype(BF16)
    sum_ref[...] = jnp.sum(upstream, axis=0, keepdims=True)


def prepare(inputs, cotangent, keep):
    return pl.pallas_call(
        prepare_kernel,
        in_specs=[VMEM] * 3,
        out_specs=[VMEM] * 2,
        out_shape=[shape_of((2,) + inputs.shape), shape_of((1, inputs.shape[1]), F32)],
        compiler_params=PARAMS,
        cost_estimate=cost(0, 6 << 20),
        name="prepare",
    )(inputs, cotangent, keep)


def attention_kernel(
    core_ref,
    first_ref,
    second_ref,
    w_ref,
    b_ref,
    d_ref,
    lrow_ref,
    cos_ref,
    up_ref,
    dn_ref,
    mixed_ref,
    pg_ref,
    sum_ref,
    q_s,
    k_s,
    v_s,
    g_s,
    kt_s,
    vt_s,
    gt_s,
    pt_s,
    dst_s,
    ot_s,
    dqt_s,
    dk_s,
    dv_s,
    out_s,
    scores_s,
    qm_s,
    gm_s,
    lcol_s,
):
    half_rows = first_ref.shape[1]
    length = 2 * half_rows
    width = d_ref.shape[0]
    blocks = length // QB
    scale = 1.0 / math.sqrt(HD)

    def starts(piece):
        return pl.multiple_of(lax.bitwise_xor(core_ref[0], piece) * half_rows, half_rows)

    for piece, ref in enumerate((first_ref, second_ref)):
        rows = pl.ds(starts(piece), half_rows)
        cos, up, dn = cos_ref[rows, :], up_ref[rows, :], dn_ref[rows, :]

        def rotate(u):
            return u * cos + pltpu.roll(u, 8, axis=1) * up + pltpu.roll(u, 120, axis=1) * dn

        tokens = ref[0]
        g_s[rows, :] = nt(ref[1], d_ref[...]).astype(BF16)
        q = nn(tokens, w_ref[:, :width]) + b_ref[:, :width]
        k = nn(tokens, w_ref[:, width : 2 * width]) + b_ref[:, width : 2 * width]
        for lo in range(0, width, 128):
            sl = slice(lo, lo + 128)
            turned = rotate(q[:, sl]).astype(BF16).astype(F32)
            q_s[rows, sl] = (turned * scale).astype(BF16)
            k_s[rows, sl] = rotate(k[:, sl]).astype(BF16)
        v_s[rows, :] = (nn(tokens, w_ref[:, 2 * width :]) + b_ref[:, 2 * width :]).astype(BF16)

    cos, up, dn = cos_ref[...], up_ref[...], dn_ref[...]

    def rotate_back(w):
        return w * cos + pltpu.roll(w * up, 120, axis=1) + pltpu.roll(w * dn, 8, axis=1)

    lane = lax.broadcasted_iota(jnp.int32, (1, 128), 1)
    zero = jnp.zeros((), BF16)
    lcol_s[...] = column(lrow_ref[...])

    def folded_rows(value, fold):
        return fold(value.reshape(value.shape[0] // 8, 8, value.shape[1]), axis=0)

    def pair(p, carry):
        lo = pl.multiple_of(p * 128, 128)
        sl = pl.ds(lo, 128)
        kt_s[...] = k_s[:, sl].T
        vt_s[...] = v_s[:, sl].T
        gt_s[...] = g_s[:, sl].astype(F32).T
        for a in range(2):
            half = (lane >= HD * a) & (lane < HD * (a + 1))
            qm_s[a] = jnp.where(half, q_s[:, sl], zero)
            gm_s[a] = jnp.where(half, g_s[:, sl], zero)
        for i in range(blocks):
            for a in range(2):
                hs = slice(HD * a, HD * (a + 1))
                end = (i + 1) * QB
                rows = slice(i * QB, end)
                qm = qm_s[a, rows, :]
                gm = gm_s[a, rows, :]
                chunks = [slice(c, c + CHUNK) for c in range(0, end, CHUNK)]
                top = None
                for cs in chunks:
                    s = nt(k_s[cs, sl], qm)
                    same = lcol_s[cs, :] == lrow_ref[:, rows]
                    if cs.start >= i * QB:
                        key = lax.broadcasted_iota(jnp.int32, (CHUNK, QB), 0)
                        query = lax.broadcasted_iota(jnp.int32, (CHUNK, QB), 1)
                        same = same & (key + (cs.start - i * QB) <= query)
                    s = jnp.where(same, s, NEGATIVE)
                    scores_s[a, cs, :] = s
                    part = folded_rows(s, jnp.max)
                    top = part if top is None else jnp.maximum(top, part)
                top = jnp.max(top, axis=0, keepdims=True)
                total = None
                for cs in chunks:
                    e = jnp.exp(scores_s[a, cs, :] - top)
                    scores_s[a, cs, :] = e
                    part = folded_rows(e, jnp.sum)
                    total = part if total is None else total + part
                rate = 1.0 / jnp.sum(total, axis=0, keepdims=True)
                for cs in chunks:
                    pt_s[a, cs, rows] = (scores_s[a, cs, :] * rate).astype(BF16)
                out = nn(vt_s[hs, 0:end], pt_s[a, 0:end, rows])
                ot_s[hs, rows] = out
                inner = jnp.sum(gt_s[hs, rows] * out, axis=0, keepdims=True)
                for cs in chunks:
                    dp = nt(v_s[cs, sl], gm) - inner
                    dst_s[a, cs, rows] = (scores_s[a, cs, :] * rate * dp).astype(BF16)
                dqt_s[hs, rows] = nn(kt_s[hs, 0:end], dst_s[a, 0:end, rows]) * scale
        for j in range(blocks):
            rows = slice(j * QB, length)
            out = slice(j * QB, (j + 1) * QB)
            dk_s[out, :] = nn(dst_s[0, out, rows], qm_s[0, rows, :]) + nn(
                dst_s[1, out, rows], qm_s[1, rows, :]
            )
            dv_s[out, :] = nn(pt_s[0, out, rows], gm_s[0, rows, :]) + nn(
                pt_s[1, out, rows], gm_s[1, rows, :]
            )

        def put(at, values):
            cols = pl.ds(pl.multiple_of(at + lo, 128), 128)
            values = values.astype(BF16)
            sum_ref[:, cols] = jnp.sum(values.astype(F32), axis=0, keepdims=True)
            out_s[...] = values
            for piece in range(2):
                pg_ref[piece, :, cols] = out_s[pl.ds(starts(piece), half_rows), :]

        put(0, rotate_back(dqt_s[...].T))
        put(width, rotate_back(dk_s[...]))
        put(2 * width, dv_s[...])
        out_s[...] = ot_s[...].T.astype(BF16)
        for piece in range(2):
            mixed_ref[piece, :, sl] = out_s[pl.ds(starts(piece), half_rows), :]
        return carry

    lax.fori_loop(0, width // 128, pair, 0)


def attention(core, parts, w, b, dense, marks, tables):
    half_rows = parts[0].shape[1]
    length = 2 * half_rows
    width = dense.shape[0]
    return pl.pallas_call(
        attention_kernel,
        in_specs=[SMEM] + [VMEM] * 9,
        out_specs=[VMEM] * 3,
        out_shape=[
            shape_of((2, half_rows, width)),
            shape_of((2, half_rows, 3 * width)),
            shape_of((1, 3 * width), F32),
        ],
        scratch_shapes=[pltpu.VMEM((length, width), BF16)] * 4
        + [pltpu.VMEM((128, length), BF16)] * 2
        + [pltpu.VMEM((128, length), F32)]
        + [pltpu.VMEM((2, length, length), BF16)] * 2
        + [pltpu.VMEM((128, length), F32)] * 2
        + [pltpu.VMEM((length, 128), F32)] * 2
        + [pltpu.VMEM((length, 128), BF16)]
        + [pltpu.VMEM((2, length, QB), F32)]
        + [pltpu.VMEM((2, length, 128), BF16)] * 2
        + [pltpu.VMEM((length, 1), jnp.int32)],
        compiler_params=PARAMS,
        cost_estimate=cost(2.3e10, 8 << 20),
        name="attention",
    )(core, *parts, w, b, dense, marks[None, :], *tables)


def rotary_turns():
    half = ROT // 2
    places = jnp.arange(SEQ_LEN, dtype=jnp.int32).astype(F32)
    rates = jnp.exp(
        jnp.arange(half, dtype=jnp.int32).astype(F32) * (-2.0 * math.log(10000.0) / ROT)
    )
    angles = places[:, None] * rates[None, :]
    return jnp.concatenate([jnp.cos(angles), jnp.sin(angles)], axis=1)


def turn(slot):
    return 2 * (slot % 2) + slot // 2


def put_pair(place_ref, m, product, near_s, own_s, columns=slice(None)):
    rows = product.shape[0] // 2
    low, high = product[:rows], product[rows:]
    swap = (place_ref[0] & 1) == 1
    own_s[m, :, columns] = jnp.where(swap, high, low).astype(BF16)
    near_s[m, :, columns] = jnp.where(swap, low, high).astype(BF16)


def pair_rows(place_ref, m, width):
    other = lax.bitwise_xor(lax.shift_right_logical(place_ref[0], 1), turn(m))
    return pl.ds(pl.multiple_of(other * width, width), width)


def loaded(parts, held, sems, first, which=None):
    if which is not None:
        parts = [ref.at[which] for ref in parts]
    rows = parts[0].shape[0]
    return copies(
        [(ref, held.at[pl.ds(p * rows, rows), :]) for p, ref in enumerate(parts)], sems, first
    )


def send_pairs(near_s, own_s, near_ref, own_ref, sems, first):
    def copy(m):
        return (
            pltpu.make_async_copy(near_s.at[m], near_ref.at[m], sems.at[first + 2 * m]),
            pltpu.make_async_copy(own_s.at[m], own_ref.at[m], sems.at[first + 2 * m + 1]),
        )

    return copy


def hidden_kernel(
    place_ref,
    a_ref,
    b_ref,
    c_ref,
    d_ref,
    w_ref,
    bias_ref,
    act_ref,
    slope_ref,
    near_ref,
    own_ref,
    tokens_s,
    grads_s,
    w_s,
    act_s,
    slope_s,
    near_s,
    own_s,
    in_sems,
    out_sems,
):
    rows = a_ref.shape[1]
    parts = (a_ref, b_ref, c_ref, d_ref)
    loads = copies([(w_ref, w_s)], in_sems)
    loads += loaded(parts, tokens_s, in_sems, 1, 0)
    loads += loaded(parts, grads_s, in_sems, 5, 1)
    loads[0].wait()
    stores = []
    for p in range(4):
        loads[1 + p].wait()
        at = pl.ds(p * rows, rows)
        hidden = nn(tokens_s[at, :], w_s[...]) + bias_ref[...]
        phi = 0.5 * (1.0 + lax.erf(hidden * (1.0 / math.sqrt(2.0))))
        act_s[at, :] = (hidden * phi).astype(BF16)
        bell = jnp.exp(-0.5 * hidden * hidden) * (1.0 / math.sqrt(2.0 * math.pi))
        slope_s[at, :] = (phi + hidden * bell).astype(BF16)
        stores += copies(
            [(act_s.at[at, :], act_ref.at[at, :]), (slope_s.at[at, :], slope_ref.at[at, :])],
            out_sems,
            2 * p,
        )
    for copy in loads[5:]:
        copy.wait()
    count, block, _ = near_ref.shape
    send = send_pairs(near_s, own_s, near_ref, own_ref, out_sems, 8)

    def one_pair(m, carry):
        product = tn(act_s[:, pair_rows(place_ref, m, 2 * block)], grads_s[...])
        put_pair(place_ref, m, product, near_s, own_s)
        for copy in send(m):
            copy.start()
        return carry

    lax.fori_loop(0, count, one_pair, 0)
    for m in range(count):
        stores += send(m)
    for copy in stores:
        copy.wait()


def hidden_layer(place, parts, w, bias, pairs):
    _, rows, width = parts[0].shape
    units = w.shape[1]
    blocks = (pairs, units // (2 * pairs), width)
    return pl.pallas_call(
        hidden_kernel,
        in_specs=[SMEM] + [ANY] * 5 + [VMEM],
        out_specs=[ANY] * 4,
        out_shape=[shape_of((4 * rows, units))] * 2 + [shape_of(blocks)] * 2,
        scratch_shapes=[pltpu.VMEM((4 * rows, width), BF16)] * 2
        + [pltpu.VMEM(w.shape, BF16)]
        + [pltpu.VMEM((4 * rows, units), BF16)] * 2
        + [pltpu.VMEM(blocks, BF16)] * 2
        + [pltpu.SemaphoreType.DMA((9,)), pltpu.SemaphoreType.DMA((8 + 2 * pairs,))],
        compiler_params=PARAMS,
        cost_estimate=cost(1.2e10, 20 << 20),
        name="hidden",
    )(place, *parts, w, bias)


def unhidden_kernel(
    place_ref,
    a_ref,
    b_ref,
    c_ref,
    d_ref,
    w_ref,
    slope_ref,
    grad_ref,
    near_ref,
    own_ref,
    sum_ref,
    grads_s,
    tokens_s,
    w_s,
    slope_s,
    near_s,
    own_s,
    in_sems,
    out_sems,
):
    rows = a_ref.shape[1]
    parts = (a_ref, b_ref, c_ref, d_ref)
    loads = copies([(w_ref, w_s)], in_sems)
    loads += loaded(parts, grads_s, in_sems, 1, 1)
    loads += copies(
        [
            (slope_ref.at[pl.ds(p * rows, rows), :], slope_s.at[pl.ds(p * rows, rows), :])
            for p in range(4)
        ],
        in_sems,
        5,
    )
    loads += loaded(parts, tokens_s, in_sems, 9, 0)
    loads[0].wait()
    stores = []
    for p in range(4):
        loads[1 + p].wait()
        loads[5 + p].wait()
        at = pl.ds(p * rows, rows)
        grad = (nt(grads_s[at, :], w_s[...]) * slope_s[at, :].astype(F32)).astype(BF16)
        slope_s[at, :] = grad
        part = jnp.sum(grad.astype(F32), axis=0, keepdims=True)
        if p == 0:
            sum_ref[...] = part
        else:
            sum_ref[...] += part
        stores += copies([(slope_s.at[at, :], grad_ref.at[at, :])], out_sems, p)
    for copy in loads[9:]:
        copy.wait()
    count, block, _ = near_ref.shape
    for m in range(count):
        product = tn(tokens_s[:, pair_rows(place_ref, m, 2 * block)], slope_s[...])
        put_pair(place_ref, m, product, near_s, own_s)
        stores += copies(
            [(near_s.at[m], near_ref.at[m]), (own_s.at[m], own_ref.at[m])], out_sems, 4 + 2 * m
        )
    for copy in stores:
        copy.wait()


def unhidden_layer(place, parts, w, slope, pairs):
    _, rows, width = parts[0].shape
    units = w.shape[0]
    blocks = (pairs, width // (2 * pairs), units)
    return pl.pallas_call(
        unhidden_kernel,
        in_specs=[SMEM] + [ANY] * 6,
        out_specs=[ANY] * 3 + [VMEM],
        out_shape=[shape_of((4 * rows, units))]
        + [shape_of(blocks)] * 2
        + [shape_of((1, units), F32)],
        scratch_shapes=[pltpu.VMEM((4 * rows, width), BF16)] * 2
        + [pltpu.VMEM(w.shape, BF16)]
        + [pltpu.VMEM((4 * rows, units), BF16)]
        + [pltpu.VMEM(blocks, BF16)] * 2
        + [pltpu.SemaphoreType.DMA((13,)), pltpu.SemaphoreType.DMA((4 + 2 * pairs,))],
        compiler_params=PARAMS,
        cost_estimate=cost(1.2e10, 22 << 20),
        name="unhidden",
    )(place, *parts, w, slope)


def attention_grads_kernel(
    place_ref,
    a_ref,
    b_ref,
    c_ref,
    d_ref,
    mixed_one_ref,
    pg_one_ref,
    mixed_two_ref,
    pg_two_ref,
    near_ref,
    late_ref,
    own_ref,
    grads_s,
    tokens_s,
    mixed_s,
    pg_s,
    dense_s,
    near_s,
    own_s,
    in_sems,
    out_sems,
):
    parts = (a_ref, b_ref, c_ref, d_ref)
    mixed = [ref.at[p] for ref in (mixed_one_ref, mixed_two_ref) for p in range(2)]
    pg = [ref.at[p] for ref in (pg_one_ref, pg_two_ref) for p in range(2)]
    loads = loaded(parts, grads_s, in_sems, 0, 1)
    loads += loaded(mixed, mixed_s, in_sems, 4)
    loads += loaded(parts, tokens_s, in_sems, 8, 0)
    loads += loaded(pg, pg_s, in_sems, 12)
    for copy in loads[:8]:
        copy.wait()
    count, block, columns = own_ref.shape
    wide = pg_s.shape[1]
    few = block // 4
    dense_s[...] = tn(mixed_s[...], grads_s[...])
    for copy in loads[8:]:
        copy.wait()
    across = columns // 4
    swap = (place_ref[0] & 1) == 1
    stores = []
    for m in (2, 3, 0, 1):
        product = tn(tokens_s[:, pair_rows(place_ref, m, 2 * block)], pg_s[...])
        put_pair(place_ref, m, product, near_s, own_s, slice(0, wide))
        product = dense_s[pair_rows(place_ref, m, 2 * few), :]
        low, high = product[:few], product[few:]
        own = jnp.where(swap, high, low).astype(BF16)
        near = jnp.where(swap, low, high).astype(BF16)
        for j in range(4):
            cols = slice(j * across, (j + 1) * across)
            own_s[m, j * few : (j + 1) * few, wide:] = own[:, cols]
            near_s[m, j * few : (j + 1) * few, wide:] = near[:, cols]
        near_at = near_ref if m >= count // 2 else late_ref
        stores += copies(
            [(near_s.at[m], near_at.at[m % 2]), (own_s.at[m], own_ref.at[m])], out_sems, 2 * m
        )
    for copy in stores:
        copy.wait()


def attention_grads(place, parts, one, two, pairs):
    _, rows, width = parts[0].shape
    heads = one[0].shape[-1]
    wide = one[1].shape[-1]
    blocks = (pairs, width // (2 * pairs), wide + heads)
    return pl.pallas_call(
        attention_grads_kernel,
        in_specs=[SMEM] + [ANY] * 8,
        out_specs=[ANY] * 3,
        out_shape=[shape_of((pairs // 2,) + blocks[1:])] * 2 + [shape_of(blocks)],
        scratch_shapes=[pltpu.VMEM((4 * rows, width), BF16)] * 2
        + [pltpu.VMEM((4 * rows, heads), BF16), pltpu.VMEM((4 * rows, wide), BF16)]
        + [pltpu.VMEM((heads, width), F32)]
        + [pltpu.VMEM(blocks, BF16)] * 2
        + [pltpu.SemaphoreType.DMA((16,)), pltpu.SemaphoreType.DMA((2 * pairs,))],
        compiler_params=PARAMS,
        cost_estimate=cost(7e9, 16 << 20),
        name="attention_grads",
    )(place, *parts, *one, *two)


def results_kernel(
    mixed_ref,
    pg_ref,
    act_ref,
    grad_ref,
    dense_ref,
    shrink_ref,
    project_ref,
    expand_ref,
    mine_ref,
    theirs_ref,
    mixed_s,
    pg_s,
    act_s,
    grad_s,
    dense_s,
    shrink_s,
    project_s,
    expand_s,
    out_s,
    in_sems,
    out_sems,
    *,
    first,
):
    rows = mixed_ref.shape[1]
    theirs = pl.ds((first + 1) * rows, rows)
    mine = pl.ds(first * rows, rows)
    loads = copies(
        [
            (shrink_ref, shrink_s),
            (act_ref.at[theirs, :], act_s.at[1]),
            (mixed_ref, mixed_s),
            (dense_ref, dense_s),
            (expand_ref, expand_s),
            (grad_ref.at[theirs, :], grad_s.at[1]),
            (pg_ref, pg_s),
            (project_ref, project_s),
            (act_ref.at[mine, :], act_s.at[0]),
            (grad_ref.at[mine, :], grad_s.at[0]),
        ],
        in_sems,
    )
    stores = []
    for at, (piece, gradient, waits) in enumerate(
        ((1, 0, loads[:4]), (1, 1, loads[4:8]), (0, 0, loads[8:9]), (0, 1, loads[9:]))
    ):
        for copy in waits:
            copy.wait()
        if gradient:
            total = nt(grad_s[piece], expand_s[...]) + nt(pg_s[piece], project_s[...])
        else:
            total = nn(act_s[piece], shrink_s[...]) + nn(mixed_s[piece], dense_s[...])
        out_s[at] = total.astype(BF16)
        out_ref = theirs_ref if piece else mine_ref
        stores += copies([(out_s.at[at], out_ref.at[gradient])], out_sems, at)
    for copy in stores:
        copy.wait()


def results(mixed, pg, act, grad, dense, shrink, project, expand, first):
    _, rows, heads = mixed.shape
    wide = pg.shape[-1]
    units = act.shape[-1]
    width = dense.shape[1]
    return pl.pallas_call(
        functools.partial(results_kernel, first=first),
        in_specs=[ANY] * 8,
        out_specs=[ANY] * 2,
        out_shape=[shape_of((2, rows, width))] * 2,
        scratch_shapes=[pltpu.VMEM(mixed.shape, BF16), pltpu.VMEM(pg.shape, BF16)]
        + [pltpu.VMEM((2, rows, units), BF16)] * 2
        + [pltpu.VMEM(w.shape, BF16) for w in (dense, shrink, project, expand)]
        + [pltpu.VMEM((4, rows, width), BF16)]
        + [pltpu.SemaphoreType.DMA((10,)), pltpu.SemaphoreType.DMA((4,))],
        compiler_params=PARAMS,
        cost_estimate=cost(8e9, 16 << 20),
        name="results",
    )(mixed, pg, act, grad, dense, shrink, project, expand)


def exchange(value, axis, size, offset):
    return lax.ppermute(value, axis, [(i, i ^ offset) for i in range(size)])


def sum_over(value, axis, size, offset=1):
    while offset < size:
        value = value + exchange(value, axis, size, offset)
        offset *= 2
    return value


def slots(value, index, size):
    row = lax.broadcasted_iota(jnp.int32, (size, 1), 0)
    return jnp.where(row == index, value[None, :], 0.0)


def after(values, *first):
    return lax.optimization_barrier(tuple(values) + first)[: len(values)]


def hop(value, size, offset):
    return exchange(value, "fsdp", size, offset)


class Gather:
    def __init__(self, block, size, near=True):
        self.own, self.size = block, size
        self.far = hop(block, size, 4)
        self.near = hop(block, size, 1) if near else None
        self.far_near = None

    def second(self, *first, near=True):
        own, far = after((self.own, self.far), *first) if first else (self.own, self.far)
        self.pair = hop(jnp.stack([own, far]), self.size, 2)
        if near and self.far_near is None:
            self.far_near = hop(far, self.size, 1)

    def second_near(self):
        self.far_near = hop(self.far, self.size, 1)

    def third(self, *first):
        (pair,) = after((self.pair,), *first) if first else (self.pair,)
        self.pair_near = hop(pair, self.size, 1)

    def blocks(self, *first):
        every = (self.own, self.near, self.far, self.far_near, self.pair, self.pair_near)
        return after(every, *first) if first else every


class Scatter:
    def __init__(self, near, own, size, late=None):
        self.own, self.size = own, size
        self.near = hop(near, size, 1)
        self.late = self.near if late is None else hop(late, size, 1)
        self.start = 2 if late is None else 0

    def second(self, *first):
        near, own = after((self.near, self.own), *first)
        near, own = near[self.start : self.start + 2], own[2:]
        self.pair = hop((own.astype(F32) + near.astype(F32)).astype(BF16), self.size, 2)
        return self.near

    def third(self, *first):
        pair, near = after((self.pair, self.late), *first) if first else (self.pair, self.late)
        total = self.own[1].astype(F32) + near[1].astype(F32) + pair[1].astype(F32)
        self.far = hop(total.astype(BF16), self.size, 4)
        return pair

    def terms(self):
        return self.own, self.late, self.pair, self.far

    def total(self):
        return sum(term.astype(F32) for term in (self.own[0], self.late[0], self.pair[0], self.far))


def row_of(value):
    return jnp.broadcast_to(value, (value.shape[0], 128)).T[:1, :]


def block_total(own_ref, late_ref, pair_ref, far_ref, columns):
    total = own_ref[:, columns].astype(F32) + late_ref[:, columns].astype(F32)
    return total + pair_ref[:, columns].astype(F32) + far_ref[:, columns].astype(F32)


def finish_project_kernel(
    own_ref, late_ref, pair_ref, far_ref, w_ref, sum_ref, vector_ref, grad_ref, dense_ref, part_ref
):
    wide = w_ref.shape[1]
    heads = wide // (3 * HD)
    gain, shift = column(vector_ref[0:1, :]), column(vector_ref[1:2, :])
    first = second = 0.0
    for head in range(heads):
        for part in range(3):
            at = (part * heads + head) * HD
            to = (head * 3 + part) * HD
            total = block_total(own_ref, late_ref, pair_ref, far_ref, slice(at, at + HD))
            weight = w_ref[:, to : to + HD].astype(F32)
            sums = sum_ref[:, at : at + HD]
            grad_ref[:, to : to + HD] = gain * total + shift * sums
            first = first + jnp.sum(weight * total, axis=1, keepdims=True)
            second = second + jnp.sum(weight * sums, axis=1, keepdims=True)
    part_ref[0:1, :] = row_of(first)
    part_ref[1:2, :] = row_of(second)
    rows, width = dense_ref.shape
    across = width // 4
    total = block_total(own_ref, late_ref, pair_ref, far_ref, slice(wide, wide + across))
    for j in range(4):
        dense_ref[:, j * across : (j + 1) * across] = total[j * rows : (j + 1) * rows, :]


def finish_project(terms, weight, sums, vectors, rows):
    width = weight.shape[0] * 8
    lead = pl.BlockSpec((None, weight.shape[0], width), lambda i: (0, 0, 0))
    whole = [
        pl.BlockSpec(shape, lambda i: (0, 0))
        for shape in (terms[3].shape, weight.shape, sums.shape, vectors.shape)
    ]
    outs = (weight.shape, (rows, width), (2, weight.shape[0]))
    return pl.pallas_call(
        finish_project_kernel,
        grid=(1,),
        in_specs=[lead] * 3 + whole,
        out_specs=[pl.BlockSpec(shape, lambda i: (0, 0)) for shape in outs],
        out_shape=[shape_of(shape, F32) for shape in outs],
        compiler_params=PARAMS,
        cost_estimate=cost(0, 4 << 20),
        name="finish_project",
    )(*terms, weight, sums, vectors)


def finish_expand_kernel(
    own_ref, late_ref, pair_ref, far_ref, w_ref, sum_ref, vector_ref, grad_ref, part_ref
):
    gain, shift = column(vector_ref[2:3, :]), column(vector_ref[3:4, :])
    total = block_total(own_ref, late_ref, pair_ref, far_ref, slice(None))
    weight = w_ref[...].astype(F32)
    grad_ref[...] = gain * total + shift * sum_ref[...]
    part_ref[0:1, :] = row_of(jnp.sum(weight * total, axis=1, keepdims=True))
    part_ref[1:2, :] = row_of(jnp.sum(weight * sum_ref[...], axis=1, keepdims=True))


def finish_expand(terms, weight, sums, vectors):
    lead = pl.BlockSpec((None,) + weight.shape, lambda i: (0, 0, 0))
    whole = [
        pl.BlockSpec(shape, lambda i: (0, 0))
        for shape in (terms[3].shape, weight.shape, sums.shape, vectors.shape)
    ]
    outs = (weight.shape, (2, weight.shape[0]))
    return pl.pallas_call(
        finish_expand_kernel,
        grid=(1,),
        in_specs=[lead] * 3 + whole,
        out_specs=[pl.BlockSpec(shape, lambda i: (0, 0)) for shape in outs],
        out_shape=[shape_of(shape, F32) for shape in outs],
        compiler_params=PARAMS,
        cost_estimate=cost(0, 4 << 20),
        name="finish_expand",
    )(*terms, weight, sums, vectors)


def finish_tokens_kernel(
    mine_ref, near_ref, far_ref, inputs_ref, cotangent_ref, keep_ref, bias_ref, out_ref, grad_ref
):
    def total(which):
        return (
            mine_ref[which].astype(F32) + near_ref[which].astype(F32) + far_ref[which].astype(F32)
        )

    features = inputs_ref[...].astype(F32)
    out_ref[...] = (features + total(0) + bias_ref[...]).astype(BF16)
    normed, rate = normalise(features)
    grad = total(1)
    inner = jnp.mean(grad * normed, axis=-1, keepdims=True)
    centre = jnp.mean(grad, axis=-1, keepdims=True)
    upstream = cotangent_ref[...].astype(F32) * keep_ref[...]
    grad_ref[...] = (upstream + rate * (grad - centre - normed * inner)).astype(BF16)


def finish_tokens(mine, near, far, inputs, cotangent, keep, bias):
    rows, width = inputs.shape
    step = rows // 4
    both = pl.BlockSpec((2, step, width), lambda i: (0, i, 0))
    block = pl.BlockSpec((step, width), lambda i: (i, 0))
    return pl.pallas_call(
        finish_tokens_kernel,
        grid=(4,),
        in_specs=[both] * 3
        + [block] * 2
        + [pl.BlockSpec((step, 1), lambda i: (i, 0)), pl.BlockSpec((1, width), lambda i: (0, 0))],
        out_specs=[block] * 2,
        out_shape=[shape_of((rows, width))] * 2,
        compiler_params=PARAMS,
        cost_estimate=cost(0, 12 << 20),
        name="finish_tokens",
    )(mine, near, far, inputs, cotangent, keep, bias)


def by_part(array):
    shape = array.shape
    array = array.reshape(shape[:-1] + (shape[-1] // (3 * HD), 3, HD))
    return jnp.swapaxes(array, -3, -2).reshape(shape)


def by_head(array):
    shape = array.shape
    array = array.reshape(shape[:-1] + (3, shape[-1] // (3 * HD), HD))
    return jnp.swapaxes(array, -3, -2).reshape(shape)


def gathered(weight):
    return lax.all_gather(weight, "fsdp", axis=0, tiled=True)


def folded(weight, gain, shift, offset):
    weight = gathered(weight).astype(F32)
    bias = offset[None, :] + jnp.sum(weight * shift[:, None], axis=0, keepdims=True)
    return (weight * gain[:, None]).astype(BF16), bias


def whole_rows(own, near):
    whole = jnp.stack([own, near], axis=1).astype(F32)[jnp.array([0, 2, 1, 3])]
    return whole.reshape(-1, whole.shape[-1])


def scattered(value):
    return lax.psum_scatter(value, "fsdp", scatter_dimension=0, tiled=True)


def local(
    inputs,
    segments,
    cotangent,
    attention_gain,
    attention_shift,
    feedforward_gain,
    feedforward_shift,
    project_weight,
    project_bias,
    dense_weight,
    dense_bias,
    expand_weight,
    expand_bias,
    shrink_weight,
    shrink_bias,
):
    size = lax.axis_size("fsdp")
    across = lax.axis_size("tensor")
    rows, width = inputs.shape
    assert across == 4 and 2 * rows == SEQ_LEN and segments.shape[0] == 2 * SEQ_LEN
    index = lax.axis_index("fsdp")
    rank = lax.axis_index("tensor")
    core = (rank % 2).astype(jnp.int32)[None]
    chip = rank // 2
    block = width // size
    pairs = 4
    direct = size == 2 * pairs
    place = (index if direct else index * 0).astype(jnp.int32)[None]

    own_labels = lax.dynamic_slice_in_dim(segments, rank * rows, rows, 0)
    keep = (own_labels != 0).astype(F32)[:, None]
    if direct:
        first = Gather(expand_weight, size)
    early = after((inputs,), first.near)[0] if direct else inputs
    own, bias_grad = prepare(early, cotangent, keep)

    small = jnp.concatenate(
        [
            attention_gain,
            attention_shift,
            feedforward_gain,
            feedforward_shift,
            dense_bias + shrink_bias,
        ]
    )
    piece = small.shape[0] // 5
    small = slots(small, rank, across)
    small_far = small + exchange(small, "tensor", across, 2)
    (small_far,) = after((small_far,), own)
    small = small_far + exchange(small_far, "tensor", across, 1)
    own_vectors = jnp.swapaxes(small.reshape(across, 5, piece), 0, 1).reshape(5, block)
    counts = (5 * block, project_bias.shape[0], expand_bias.shape[0])
    packed = jnp.concatenate(
        [own_vectors.reshape(-1), project_bias.astype(F32), expand_bias.astype(F32)]
    )
    packed = slots(packed, index, size)
    packed_near = packed + exchange(packed, "fsdp", size, 1)
    if direct:
        (packed_near,) = after((packed_near,), first.far, first.near, own)
    if direct:
        packed_far = packed_near + exchange(packed_near, "fsdp", size, 4)
        packed = packed_far + exchange(packed_far, "fsdp", size, 2)
    else:
        packed = sum_over(packed_near, "fsdp", size, 2)
    vectors = jnp.swapaxes(packed[:, : counts[0]].reshape(size, 5, block), 0, 1).reshape(5, width)
    project_offset = by_part(packed[:, counts[0] : counts[0] + counts[1]].reshape(-1))
    expand_offset = packed[:, counts[0] + counts[1] :].reshape(-1)

    (own,) = after((own,), small_far)

    def chip_pair(value):
        return exchange(value, "tensor", across, 1)

    def other_chip(value):
        return exchange(value, "tensor", across, 2)

    labels = segments.reshape(2, SEQ_LEN)
    labels = jnp.where(chip == 0, labels, labels[::-1])
    places = jnp.arange(SEQ_LEN, dtype=jnp.int32)[None, :]
    marks = jnp.where(labels != 0, labels, -1 - places)
    across_chip = other_chip(own)
    own_near, _ = after((own, small), packed_far) if direct else (own, small)
    partner = chip_pair(own_near)
    if direct:
        first.second_near()
        (pack_weight,) = after((project_weight,), first.far_near)
        packed_weights, *tables = pack(pack_weight, dense_weight, rotary_turns())
        (near_block,) = after((shrink_weight,), packed_near)
        near_block = hop(near_block, size, 1)
        first.second(packed)
        (far_block,) = after((shrink_weight,), packed)
        second = Gather(far_block, size, False)
        second.near = near_block
        second.second(first.pair, first.far_near, packed_weights, near_block)
        (far_block,) = after((packed_weights,), second.far)
        third = Gather(far_block, size, False)
        first.third(first.far_near, packed_weights)
        expand, expand_row = join_expand(
            place,
            first.blocks(),
            vectors[2][None, :],
            vectors[3][None, :],
            expand_offset[None, :],
        )
        (across_chip,) = after((across_chip,), second.pair, third.far, expand_row)
        (expand,) = after((expand,), second.pair, second.far_near, third.far, partner)
        second.third(expand)
        third.second(second.pair, near=False)
    else:
        _, *tables = pack(project_weight, dense_weight, rotary_turns())
        expand, expand_row = folded(expand_weight, vectors[2], vectors[3], expand_offset)
        project, project_row = folded(
            by_part(project_weight), vectors[0], vectors[1], project_offset
        )
        dense = gathered(dense_weight)
        shrink = gathered(shrink_weight)
    parts = (own, partner, across_chip, chip_pair(across_chip))

    active, slope, shrink_near, shrink_own = hidden_layer(place, parts, expand, expand_row, pairs)
    if direct:
        shrink_sums = Scatter(shrink_near, shrink_own, size)
        near_block, far_block = after((packed_weights, third.far), shrink_own)
        third.near = hop(near_block, size, 1)
        third.far_near = hop(far_block, size, 1)
        third.third(shrink_own)
        shrink = join(place, second.blocks(shrink_own))
    hidden_grad, expand_near, expand_own, expand_offset_grad = unhidden_layer(
        place, parts, shrink, slope, pairs
    )
    if direct:
        expand_sums = Scatter(expand_near, expand_own, size)
        project, dense, project_row = join_project(
            place,
            third.blocks(expand_own),
            vectors[0][None, :],
            vectors[1][None, :],
            project_offset[None, :],
        )
    else:
        (project,) = after((project,), expand_own)

    def attend(sequence):
        at = slice(2 * sequence, 2 * sequence + 2)
        return attention(core, parts[at], project, project_row, dense, marks[sequence], tables)

    two = attend(1)
    weights = (dense, shrink, project, expand)
    act = active
    if direct:
        ready = shrink_sums.second(two[2])
        (act,) = after((active,), ready)
    far_mine, far_theirs = results(two[0], two[1], act, hidden_grad, *weights, first=2)
    far = chip_pair(far_theirs)
    far_sum = (far_mine.astype(F32) + far.astype(F32)).astype(BF16)
    far = other_chip(far_sum)
    if direct:
        ready = shrink_sums.third(far_mine)
        more = expand_sums.second(far_mine)
        (project,) = after((project,), ready, more)
    else:
        (project,) = after((project,), far_mine)
    one = attend(0)
    if direct:
        ready = expand_sums.third(one[2], far_sum)
        (pair_grads,) = after((one[1],), ready, shrink_sums.far, far_sum)
        one = (one[0], pair_grads, one[2])
    both_near, both_late, both_own = attention_grads(place, parts, one[:2], two[:2], pairs)
    project_offset_grad = one[2] + two[2]
    wide = project_offset_grad.shape[1]
    units = expand_offset_grad.shape[1]
    few = dense_weight.shape[0]
    totals = jnp.concatenate([project_offset_grad, expand_offset_grad, bias_grad], axis=1)
    (totals,) = after((totals,), both_own)
    totals = totals_near = totals + exchange(totals, "fsdp", size, 1)
    if direct:
        totals = totals_pair = totals + exchange(totals, "fsdp", size, 2)
        totals = totals + exchange(totals, "fsdp", size, 4)
    else:
        totals = sum_over(totals, "fsdp", size, 2)
    project_totals = totals[:, :wide]
    expand_totals = totals[:, wide : wide + units]
    bias_totals = totals[0, wide + units :]

    act = active
    if direct:
        both_sums = Scatter(both_near, both_own, size, both_late)
        (act,) = after((active,), both_own, expand_sums.far)
    near_mine, near_theirs = results(one[0], one[1], act, hidden_grad, *weights, first=0)
    def mine(vector, count, start):
        return lax.dynamic_slice_in_dim(vector, start * count, count, 0)

    own_rows = own_vectors[:4]
    if direct:
        both_sums.second(near_mine, totals)
        shrink_sum = shrink_sums.total()
        ready = both_sums.third(shrink_sum)
        (expand_totals,) = after((expand_totals,), ready)
        expand_gradient, expand_parts = finish_expand(
            expand_sums.terms(), expand_weight, expand_totals, own_rows
        )
        far, near_mine, near_theirs = after((far, near_mine, near_theirs), ready)
        near = chip_pair(near_theirs)
        output, inputs_gradient = finish_tokens(
            near_mine, near, far, inputs, cotangent, keep, vectors[4][None, :]
        )
        (project_totals,) = after((project_totals,), output, expand_parts)
        project_gradient, dense_sum, project_parts = finish_project(
            both_sums.terms(), project_weight, project_totals, own_rows, few
        )
        partial = [project_parts, expand_parts]
    else:
        near = chip_pair(near_theirs)
        output, inputs_gradient = finish_tokens(
            near_mine, near, far, inputs, cotangent, keep, vectors[4][None, :]
        )
        shrink_sum = scattered(whole_rows(shrink_own, shrink_near))
        expand_sum = scattered(whole_rows(expand_own, expand_near))
        both = whole_rows(both_own, jnp.concatenate([both_late, both_near]))
        project_sum = scattered(both[:, :wide])
        dense_sum = both[:, wide:].reshape(2 * pairs, 4, -1, width // 4)
        dense_sum = scattered(jnp.swapaxes(dense_sum, 1, 2).reshape(-1, width))
        columns = own_rows[:, :, None]
        project_gradient = by_head(columns[0] * project_sum + columns[1] * project_totals)
        expand_gradient = columns[2] * expand_sum + columns[3] * expand_totals
        own_project = by_part(project_weight).astype(F32)
        own_expand = expand_weight.astype(F32)
        partial = [
            jnp.sum(term, axis=1)[None, :]
            for term in (
                own_project * project_sum,
                own_project * project_totals,
                own_expand * expand_sum,
                own_expand * expand_totals,
            )
        ]
    partial = jnp.concatenate(partial + [mine(bias_totals, block, index)[None, :]])
    partial = sum_over(partial, "tensor", across)
    partial = lax.dynamic_slice_in_dim(partial, rank * piece, piece, 1)
    return (
        output,
        inputs_gradient,
        partial[0],
        partial[1],
        partial[2],
        partial[3],
        project_gradient,
        mine(by_head(project_totals[0]), project_bias.shape[0], index),
        dense_sum,
        partial[4],
        expand_gradient,
        mine(expand_totals[0], expand_bias.shape[0], index),
        shrink_sum,
        partial[4],
    )


def solution(mesh):
    in_specs = (
        P(("fsdp", "tensor"), None),
        P("fsdp"),
        P(("fsdp", "tensor"), None),
        P(("fsdp", "tensor")),
        P(("fsdp", "tensor")),
        P(("fsdp", "tensor")),
        P(("fsdp", "tensor")),
        P("fsdp", "tensor"),
        P(("tensor", "fsdp")),
        P(("tensor", "fsdp"), None),
        P(("fsdp", "tensor")),
        P("fsdp", "tensor"),
        P(("tensor", "fsdp")),
        P(("tensor", "fsdp"), None),
        P(("fsdp", "tensor")),
    )
    out_specs = (
        P(("fsdp", "tensor"), None),
        P(("fsdp", "tensor"), None),
        P(("fsdp", "tensor")),
        P(("fsdp", "tensor")),
        P(("fsdp", "tensor")),
        P(("fsdp", "tensor")),
        P("fsdp", "tensor"),
        P(("tensor", "fsdp")),
        P(("tensor", "fsdp"), None),
        P(("fsdp", "tensor")),
        P("fsdp", "tensor"),
        P(("tensor", "fsdp")),
        P(("tensor", "fsdp"), None),
        P(("fsdp", "tensor")),
    )
    return jax.shard_map(local, mesh=mesh, in_specs=in_specs, out_specs=out_specs, check_vma=False)
```

```python
import functools
import math

import jax
import jax.numpy as jnp
from jax import lax
from jax.experimental import pallas as pl
from jax.experimental.pallas import tpu as pltpu
from jax.sharding import PartitionSpec as P

HD = 64
ROT = 16
SEQ_LEN = 1024
EPS = 1e-05
NEGATIVE = -1e30
QB = 256
CHUNK = 128
PARAMS = pltpu.CompilerParams(vmem_limit_bytes=60 * 1024 * 1024)
BF16 = jnp.bfloat16
F32 = jnp.float32
COST = 1.0
VMEM = pl.BlockSpec(memory_space=pltpu.VMEM)
SMEM = pl.BlockSpec(memory_space=pltpu.SMEM)
ANY = pl.BlockSpec(memory_space=pl.ANY)


def shape_of(dims, kind=BF16):
    return jax.ShapeDtypeStruct(dims, kind)


def cost(flops, moved):
    return pl.CostEstimate(
        flops=int(flops * COST), bytes_accessed=int(moved * COST), transcendentals=0
    )


def nn(left, right):
    return lax.dot_general(left, right, (((1,), (0,)), ((), ())), preferred_element_type=F32)


def nt(left, right):
    return lax.dot_general(left, right, (((1,), (1,)), ((), ())), preferred_element_type=F32)


def tn(left, right):
    return lax.dot_general(left, right, (((0,), (0,)), ((), ())), preferred_element_type=F32)


def copies(pairs, sems, first=0):
    made = [pltpu.make_async_copy(s, d, sems.at[first + i]) for i, (s, d) in enumerate(pairs)]
    for copy in made:
        copy.start()
    return made


def pack_kernel(project_ref, dense_ref, turns_ref, out_ref, cos_ref, up_ref, dn_ref):
    heads = project_ref.shape[1] // (3 * HD)
    rows = dense_ref.shape[0]
    width = heads * HD
    for part in range(3):
        pieces = [
            project_ref[:, (3 * head + part) * HD : (3 * head + part + 1) * HD]
            for head in range(heads)
        ]
        out_ref[:, part * width : (part + 1) * width] = jnp.concatenate(pieces, axis=1)
    for j in range(4):
        columns = slice(j * width, (j + 1) * width)
        out_ref[j * rows : (j + 1) * rows, 3 * width :] = dense_ref[:, columns]
    half = ROT // 2
    length = turns_ref.shape[0]
    cosine, sine = turns_ref[:, :half], turns_ref[:, half:]
    rest = jnp.zeros((length, HD - ROT), F32)
    none = jnp.zeros((length, half), F32)
    cos_ref[...] = jnp.concatenate([cosine, cosine, rest + 1.0] * 2, axis=1)
    up_ref[...] = jnp.concatenate([none, sine, rest] * 2, axis=1)
    dn_ref[...] = jnp.concatenate([-sine, none, rest] * 2, axis=1)


def pack(project, dense, turns):
    table = shape_of((turns.shape[0], 2 * HD), F32)
    return pl.pallas_call(
        pack_kernel,
        in_specs=[VMEM] * 3,
        out_specs=[VMEM] * 4,
        out_shape=[shape_of((project.shape[0], dense.shape[1]))] + [table] * 3,
        compiler_params=PARAMS,
        cost_estimate=cost(0, 3 << 20),
        name="pack",
    )(project, dense, turns)


def column(row):
    return jnp.broadcast_to(row, (8, row.shape[1])).T[:, :1]


def shift_times(shift, weight):
    high = shift.astype(BF16)
    rest = shift - high.astype(F32)
    middle = rest.astype(BF16)
    low = (rest - middle.astype(F32)).astype(BF16)
    parts = nn(jnp.concatenate([high, middle, low], axis=0), weight)
    return jnp.sum(parts, axis=0, keepdims=True)


def scaled_rows(place, k, weight, gain_ref, shift_ref):
    rows = weight.shape[0]
    start = pl.multiple_of(lax.bitwise_xor(place, k) * rows, rows)
    part = shift_times(shift_ref[:, pl.ds(start, rows)], weight)
    gain = column(gain_ref[:, pl.ds(start, rows)])
    return start, (weight.astype(F32) * gain).astype(BF16), part


def block_list(refs):
    own, near, far, far_near, pair, pair_near = refs
    return [own, near, pair.at[0], pair_near.at[0], far, far_near, pair.at[1], pair_near.at[1]]


def join_project_kernel(place_ref, *refs):
    gain_ref, shift_ref, offset_ref, project_ref, dense_ref, bias_ref = refs[6:]
    total = offset_ref[...]
    wide = project_ref.shape[1]
    for k, ref in enumerate(block_list(refs[:6])):
        block = ref[...]
        start, scaled, part = scaled_rows(
            place_ref[0], k, block[:, :wide], gain_ref, shift_ref
        )
        project_ref[pl.ds(start, block.shape[0]), :] = scaled
        total = total + part
        rows = block.shape[0] // 4
        across = block.shape[1] // 4
        base = pl.multiple_of(lax.bitwise_xor(place_ref[0], k) * rows, rows)
        for j in range(4):
            dense_ref[pl.ds(base, rows), j * across : (j + 1) * across] = block[
                j * rows : (j + 1) * rows, wide:
            ]
    bias_ref[...] = total


def join_project(place, blocks, gain, shift, offset):
    rows, columns = blocks[0].shape
    total = 8 * rows
    wide = offset.shape[1]
    return pl.pallas_call(
        join_project_kernel,
        in_specs=[SMEM] + [VMEM] * 9,
        out_specs=[VMEM] * 3,
        out_shape=[
            shape_of((total, wide)),
            shape_of((total // 4, columns)),
            shape_of((1, wide), F32),
        ],
        compiler_params=PARAMS,
        cost_estimate=cost(1e9, 10 << 20),
        name="join_project",
    )(place, *blocks, gain, shift, offset)


def join_expand_kernel(place_ref, *refs):
    gain_ref, shift_ref, offset_ref, out_ref, bias_ref = refs[6:]
    total = offset_ref[...]
    for k, ref in enumerate(block_list(refs[:6])):
        start, scaled, part = scaled_rows(place_ref[0], k, ref[...], gain_ref, shift_ref)
        out_ref[pl.ds(start, scaled.shape[0]), :] = scaled
        total = total + part
    bias_ref[...] = total


def join_expand(place, blocks, gain, shift, offset):
    rows, columns = blocks[0].shape
    return pl.pallas_call(
        join_expand_kernel,
        in_specs=[SMEM] + [VMEM] * 9,
        out_specs=[VMEM] * 2,
        out_shape=[shape_of((8 * rows, columns)), shape_of((1, columns), F32)],
        compiler_params=PARAMS,
        cost_estimate=cost(1e9, 6 << 20),
        name="join_expand",
    )(place, *blocks, gain, shift, offset)


def join_kernel(place_ref, *refs):
    out_ref = refs[6]
    for k, ref in enumerate(block_list(refs[:6])):
        rows = ref.shape[0]
        start = pl.multiple_of(lax.bitwise_xor(place_ref[0], k) * rows, rows)
        out_ref[pl.ds(start, rows), :] = ref[...]


def join(place, blocks):
    rows, columns = blocks[0].shape
    return pl.pallas_call(
        join_kernel,
        in_specs=[SMEM] + [VMEM] * 6,
        out_specs=VMEM,
        out_shape=shape_of((8 * rows, columns)),
        compiler_params=PARAMS,
        cost_estimate=cost(0, 4 << 20),
        name="join",
    )(place, *blocks)


def normalise(features):
    centre = features - jnp.mean(features, axis=-1, keepdims=True)
    rate = lax.rsqrt(jnp.mean(centre * centre, axis=-1, keepdims=True) + EPS)
    return centre * rate, rate


def prepare_kernel(inputs_ref, cotangent_ref, keep_ref, both_ref, sum_ref):
    both_ref[0] = normalise(inputs_ref[...].astype(F32))[0].astype(BF16)
    upstream = cotangent_ref[...].astype(F32) * keep_ref[...]
    both_ref[1] = upstream.astype(BF16)
    sum_ref[...] = jnp.sum(upstream, axis=0, keepdims=True)


def prepare(inputs, cotangent, keep):
    return pl.pallas_call(
        prepare_kernel,
        in_specs=[VMEM] * 3,
        out_specs=[VMEM] * 2,
        out_shape=[shape_of((2,) + inputs.shape), shape_of((1, inputs.shape[1]), F32)],
        compiler_params=PARAMS,
        cost_estimate=cost(0, 6 << 20),
        name="prepare",
    )(inputs, cotangent, keep)


def attention_kernel(
    core_ref,
    first_ref,
    second_ref,
    w_ref,
    b_ref,
    d_ref,
    lrow_ref,
    cos_ref,
    up_ref,
    dn_ref,
    mixed_ref,
    pg_ref,
    sum_ref,
    q_s,
    k_s,
    v_s,
    g_s,
    kt_s,
    vt_s,
    gt_s,
    pt_s,
    dst_s,
    ot_s,
    dqt_s,
    dk_s,
    dv_s,
    out_s,
    scores_s,
    qm_s,
    gm_s,
    lcol_s,
):
    half_rows = first_ref.shape[1]
    length = 2 * half_rows
    width = d_ref.shape[0]
    blocks = length // QB
    scale = 1.0 / math.sqrt(HD)

    def starts(piece):
        return pl.multiple_of(lax.bitwise_xor(core_ref[0], piece) * half_rows, half_rows)

    for piece, ref in enumerate((first_ref, second_ref)):
        rows = pl.ds(starts(piece), half_rows)
        cos, up, dn = cos_ref[rows, :], up_ref[rows, :], dn_ref[rows, :]

        def rotate(u):
            return u * cos + pltpu.roll(u, 8, axis=1) * up + pltpu.roll(u, 120, axis=1) * dn

        tokens = ref[0]
        g_s[rows, :] = nt(ref[1], d_ref[...]).astype(BF16)
        q = nn(tokens, w_ref[:, :width]) + b_ref[:, :width]
        k = nn(tokens, w_ref[:, width : 2 * width]) + b_ref[:, width : 2 * width]
        for lo in range(0, width, 128):
            sl = slice(lo, lo + 128)
            turned = rotate(q[:, sl]).astype(BF16).astype(F32)
            q_s[rows, sl] = (turned * scale).astype(BF16)
            k_s[rows, sl] = rotate(k[:, sl]).astype(BF16)
        v_s[rows, :] = (nn(tokens, w_ref[:, 2 * width :]) + b_ref[:, 2 * width :]).astype(BF16)

    cos, up, dn = cos_ref[...], up_ref[...], dn_ref[...]

    def rotate_back(w):
        return w * cos + pltpu.roll(w * up, 120, axis=1) + pltpu.roll(w * dn, 8, axis=1)

    lane = lax.broadcasted_iota(jnp.int32, (1, 128), 1)
    zero = jnp.zeros((), BF16)
    lcol_s[...] = column(lrow_ref[...])

    def folded_rows(value, fold):
        return fold(value.reshape(value.shape[0] // 8, 8, value.shape[1]), axis=0)

    def pair(p, carry):
        lo = pl.multiple_of(p * 128, 128)
        sl = pl.ds(lo, 128)
        kt_s[...] = k_s[:, sl].T
        vt_s[...] = v_s[:, sl].T
        gt_s[...] = g_s[:, sl].astype(F32).T
        for a in range(2):
            half = (lane >= HD * a) & (lane < HD * (a + 1))
            qm_s[a] = jnp.where(half, q_s[:, sl], zero)
            gm_s[a] = jnp.where(half, g_s[:, sl], zero)
        for i in range(blocks):
            for a in range(2):
                hs = slice(HD * a, HD * (a + 1))
                end = (i + 1) * QB
                rows = slice(i * QB, end)
                qm = qm_s[a, rows, :]
                gm = gm_s[a, rows, :]
                chunks = [slice(c, c + CHUNK) for c in range(0, end, CHUNK)]
                top = None
                for cs in chunks:
                    s = nt(k_s[cs, sl], qm)
                    same = lcol_s[cs, :] == lrow_ref[:, rows]
                    if cs.start >= i * QB:
                        key = lax.broadcasted_iota(jnp.int32, (CHUNK, QB), 0)
                        query = lax.broadcasted_iota(jnp.int32, (CHUNK, QB), 1)
                        same = same & (key + (cs.start - i * QB) <= query)
                    s = jnp.where(same, s, NEGATIVE)
                    scores_s[a, cs, :] = s
                    part = folded_rows(s, jnp.max)
                    top = part if top is None else jnp.maximum(top, part)
                top = jnp.max(top, axis=0, keepdims=True)
                total = None
                for cs in chunks:
                    e = jnp.exp(scores_s[a, cs, :] - top)
                    scores_s[a, cs, :] = e
                    part = folded_rows(e, jnp.sum)
                    total = part if total is None else total + part
                rate = 1.0 / jnp.sum(total, axis=0, keepdims=True)
                for cs in chunks:
                    pt_s[a, cs, rows] = (scores_s[a, cs, :] * rate).astype(BF16)
                out = nn(vt_s[hs, 0:end], pt_s[a, 0:end, rows])
                ot_s[hs, rows] = out
                inner = jnp.sum(gt_s[hs, rows] * out, axis=0, keepdims=True)
                for cs in chunks:
                    dp = nt(v_s[cs, sl], gm) - inner
                    dst_s[a, cs, rows] = (scores_s[a, cs, :] * rate * dp).astype(BF16)
                dqt_s[hs, rows] = nn(kt_s[hs, 0:end], dst_s[a, 0:end, rows]) * scale
        for j in range(blocks):
            rows = slice(j * QB, length)
            out = slice(j * QB, (j + 1) * QB)
            dk_s[out, :] = nn(dst_s[0, out, rows], qm_s[0, rows, :]) + nn(
                dst_s[1, out, rows], qm_s[1, rows, :]
            )
            dv_s[out, :] = nn(pt_s[0, out, rows], gm_s[0, rows, :]) + nn(
                pt_s[1, out, rows], gm_s[1, rows, :]
            )

        def put(at, values):
            cols = pl.ds(pl.multiple_of(at + lo, 128), 128)
            values = values.astype(BF16)
            sum_ref[:, cols] = jnp.sum(values.astype(F32), axis=0, keepdims=True)
            out_s[...] = values
            for piece in range(2):
                pg_ref[piece, :, cols] = out_s[pl.ds(starts(piece), half_rows), :]

        put(0, rotate_back(dqt_s[...].T))
        put(width, rotate_back(dk_s[...]))
        put(2 * width, dv_s[...])
        out_s[...] = ot_s[...].T.astype(BF16)
        for piece in range(2):
            mixed_ref[piece, :, sl] = out_s[pl.ds(starts(piece), half_rows), :]
        return carry

    lax.fori_loop(0, width // 128, pair, 0, unroll=True)


def attention(core, parts, w, b, dense, marks, tables):
    half_rows = parts[0].shape[1]
    length = 2 * half_rows
    width = dense.shape[0]
    return pl.pallas_call(
        attention_kernel,
        in_specs=[SMEM] + [VMEM] * 9,
        out_specs=[VMEM] * 3,
        out_shape=[
            shape_of((2, half_rows, width)),
            shape_of((2, half_rows, 3 * width)),
            shape_of((1, 3 * width), F32),
        ],
        scratch_shapes=[pltpu.VMEM((length, width), BF16)] * 4
        + [pltpu.VMEM((128, length), BF16)] * 2
        + [pltpu.VMEM((128, length), F32)]
        + [pltpu.VMEM((2, length, length), BF16)] * 2
        + [pltpu.VMEM((128, length), F32)] * 2
        + [pltpu.VMEM((length, 128), F32)] * 2
        + [pltpu.VMEM((length, 128), BF16)]
        + [pltpu.VMEM((2, length, QB), F32)]
        + [pltpu.VMEM((2, length, 128), BF16)] * 2
        + [pltpu.VMEM((length, 1), jnp.int32)],
        compiler_params=PARAMS,
        cost_estimate=cost(2.3e10, 8 << 20),
        name="attention",
    )(core, *parts, w, b, dense, marks[None, :], *tables)


def rotary_turns():
    half = ROT // 2
    places = jnp.arange(SEQ_LEN, dtype=jnp.int32).astype(F32)
    rates = jnp.exp(
        jnp.arange(half, dtype=jnp.int32).astype(F32) * (-2.0 * math.log(10000.0) / ROT)
    )
    angles = places[:, None] * rates[None, :]
    return jnp.concatenate([jnp.cos(angles), jnp.sin(angles)], axis=1)


def turn(slot):
    return 2 * (slot % 2) + slot // 2


def put_pair(place_ref, m, product, near_s, own_s, columns=slice(None)):
    rows = product.shape[0] // 2
    low, high = product[:rows], product[rows:]
    swap = (place_ref[0] & 1) == 1
    own_s[m, :, columns] = jnp.where(swap, high, low).astype(BF16)
    near_s[m, :, columns] = jnp.where(swap, low, high).astype(BF16)


def pair_rows(place_ref, m, width):
    other = lax.bitwise_xor(lax.shift_right_logical(place_ref[0], 1), turn(m))
    return pl.ds(pl.multiple_of(other * width, width), width)


def loaded(parts, held, sems, first, which=None):
    if which is not None:
        parts = [ref.at[which] for ref in parts]
    rows = parts[0].shape[0]
    return copies(
        [(ref, held.at[pl.ds(p * rows, rows), :]) for p, ref in enumerate(parts)], sems, first
    )


def send_pairs(near_s, own_s, near_ref, own_ref, sems, first):
    def copy(m):
        return (
            pltpu.make_async_copy(near_s.at[m], near_ref.at[m], sems.at[first + 2 * m]),
            pltpu.make_async_copy(own_s.at[m], own_ref.at[m], sems.at[first + 2 * m + 1]),
        )

    return copy


def hidden_kernel(
    place_ref,
    a_ref,
    b_ref,
    c_ref,
    d_ref,
    w_ref,
    bias_ref,
    act_ref,
    slope_ref,
    near_ref,
    own_ref,
    tokens_s,
    grads_s,
    w_s,
    act_s,
    slope_s,
    near_s,
    own_s,
    in_sems,
    out_sems,
):
    rows = a_ref.shape[1]
    parts = (a_ref, b_ref, c_ref, d_ref)
    loads = copies([(w_ref, w_s)], in_sems)
    loads += loaded(parts, tokens_s, in_sems, 1, 0)
    loads += loaded(parts, grads_s, in_sems, 5, 1)
    loads[0].wait()
    stores = []
    for p in range(4):
        loads[1 + p].wait()
        at = pl.ds(p * rows, rows)
        hidden = nn(tokens_s[at, :], w_s[...]) + bias_ref[...]
        phi = 0.5 * (1.0 + lax.erf(hidden * (1.0 / math.sqrt(2.0))))
        act_s[at, :] = (hidden * phi).astype(BF16)
        bell = jnp.exp(-0.5 * hidden * hidden) * (1.0 / math.sqrt(2.0 * math.pi))
        slope_s[at, :] = (phi + hidden * bell).astype(BF16)
        stores += copies(
            [(act_s.at[at, :], act_ref.at[at, :]), (slope_s.at[at, :], slope_ref.at[at, :])],
            out_sems,
            2 * p,
        )
    for copy in loads[5:]:
        copy.wait()
    count, block, _ = near_ref.shape
    send = send_pairs(near_s, own_s, near_ref, own_ref, out_sems, 8)

    def one_pair(m, carry):
        product = tn(act_s[:, pair_rows(place_ref, m, 2 * block)], grads_s[...])
        put_pair(place_ref, m, product, near_s, own_s)
        for copy in send(m):
            copy.start()
        return carry

    lax.fori_loop(0, count, one_pair, 0)
    for m in range(count):
        stores += send(m)
    for copy in stores:
        copy.wait()


def hidden_layer(place, parts, w, bias, pairs):
    _, rows, width = parts[0].shape
    units = w.shape[1]
    blocks = (pairs, units // (2 * pairs), width)
    return pl.pallas_call(
        hidden_kernel,
        in_specs=[SMEM] + [ANY] * 5 + [VMEM],
        out_specs=[ANY] * 4,
        out_shape=[shape_of((4 * rows, units))] * 2 + [shape_of(blocks)] * 2,
        scratch_shapes=[pltpu.VMEM((4 * rows, width), BF16)] * 2
        + [pltpu.VMEM(w.shape, BF16)]
        + [pltpu.VMEM((4 * rows, units), BF16)] * 2
        + [pltpu.VMEM(blocks, BF16)] * 2
        + [pltpu.SemaphoreType.DMA((9,)), pltpu.SemaphoreType.DMA((8 + 2 * pairs,))],
        compiler_params=PARAMS,
        cost_estimate=cost(1.2e10, 20 << 20),
        name="hidden",
    )(place, *parts, w, bias)


def unhidden_kernel(
    place_ref,
    a_ref,
    b_ref,
    c_ref,
    d_ref,
    w_ref,
    slope_ref,
    grad_ref,
    near_ref,
    own_ref,
    sum_ref,
    grads_s,
    tokens_s,
    w_s,
    slope_s,
    near_s,
    own_s,
    in_sems,
    out_sems,
):
    rows = a_ref.shape[1]
    parts = (a_ref, b_ref, c_ref, d_ref)
    loads = copies([(w_ref, w_s)], in_sems)
    loads += loaded(parts, grads_s, in_sems, 1, 1)
    loads += copies(
        [
            (slope_ref.at[pl.ds(p * rows, rows), :], slope_s.at[pl.ds(p * rows, rows), :])
            for p in range(4)
        ],
        in_sems,
        5,
    )
    loads += loaded(parts, tokens_s, in_sems, 9, 0)
    loads[0].wait()
    stores = []
    for p in range(4):
        loads[1 + p].wait()
        loads[5 + p].wait()
        at = pl.ds(p * rows, rows)
        grad = (nt(grads_s[at, :], w_s[...]) * slope_s[at, :].astype(F32)).astype(BF16)
        slope_s[at, :] = grad
        part = jnp.sum(grad.astype(F32), axis=0, keepdims=True)
        if p == 0:
            sum_ref[...] = part
        else:
            sum_ref[...] += part
        stores += copies([(slope_s.at[at, :], grad_ref.at[at, :])], out_sems, p)
    for copy in loads[9:]:
        copy.wait()
    count, block, _ = near_ref.shape
    for m in range(count):
        product = tn(tokens_s[:, pair_rows(place_ref, m, 2 * block)], slope_s[...])
        put_pair(place_ref, m, product, near_s, own_s)
        stores += copies(
            [(near_s.at[m], near_ref.at[m]), (own_s.at[m], own_ref.at[m])], out_sems, 4 + 2 * m
        )
    for copy in stores:
        copy.wait()


def unhidden_layer(place, parts, w, slope, pairs):
    _, rows, width = parts[0].shape
    units = w.shape[0]
    blocks = (pairs, width // (2 * pairs), units)
    return pl.pallas_call(
        unhidden_kernel,
        in_specs=[SMEM] + [ANY] * 6,
        out_specs=[ANY] * 3 + [VMEM],
        out_shape=[shape_of((4 * rows, units))]
        + [shape_of(blocks)] * 2
        + [shape_of((1, units), F32)],
        scratch_shapes=[pltpu.VMEM((4 * rows, width), BF16)] * 2
        + [pltpu.VMEM(w.shape, BF16)]
        + [pltpu.VMEM((4 * rows, units), BF16)]
        + [pltpu.VMEM(blocks, BF16)] * 2
        + [pltpu.SemaphoreType.DMA((13,)), pltpu.SemaphoreType.DMA((4 + 2 * pairs,))],
        compiler_params=PARAMS,
        cost_estimate=cost(1.2e10, 22 << 20),
        name="unhidden",
    )(place, *parts, w, slope)


def attention_grads_kernel(
    place_ref,
    a_ref,
    b_ref,
    c_ref,
    d_ref,
    mixed_one_ref,
    pg_one_ref,
    mixed_two_ref,
    pg_two_ref,
    near_ref,
    late_ref,
    own_ref,
    grads_s,
    tokens_s,
    mixed_s,
    pg_s,
    dense_s,
    near_s,
    own_s,
    in_sems,
    out_sems,
):
    parts = (a_ref, b_ref, c_ref, d_ref)
    mixed = [ref.at[p] for ref in (mixed_one_ref, mixed_two_ref) for p in range(2)]
    pg = [ref.at[p] for ref in (pg_one_ref, pg_two_ref) for p in range(2)]
    loads = loaded(parts, grads_s, in_sems, 0, 1)
    loads += loaded(mixed, mixed_s, in_sems, 4)
    loads += loaded(parts, tokens_s, in_sems, 8, 0)
    loads += loaded(pg, pg_s, in_sems, 12)
    for copy in loads[:8]:
        copy.wait()
    count, block, columns = own_ref.shape
    wide = pg_s.shape[1]
    few = block // 4
    dense_s[...] = tn(mixed_s[...], grads_s[...])
    for copy in loads[8:]:
        copy.wait()
    across = columns // 4
    swap = (place_ref[0] & 1) == 1
    stores = []
    for m in (2, 3, 0, 1):
        product = tn(tokens_s[:, pair_rows(place_ref, m, 2 * block)], pg_s[...])
        put_pair(place_ref, m, product, near_s, own_s, slice(0, wide))
        product = dense_s[pair_rows(place_ref, m, 2 * few), :]
        low, high = product[:few], product[few:]
        own = jnp.where(swap, high, low).astype(BF16)
        near = jnp.where(swap, low, high).astype(BF16)
        for j in range(4):
            cols = slice(j * across, (j + 1) * across)
            own_s[m, j * few : (j + 1) * few, wide:] = own[:, cols]
            near_s[m, j * few : (j + 1) * few, wide:] = near[:, cols]
        near_at = near_ref if m >= count // 2 else late_ref
        stores += copies(
            [(near_s.at[m], near_at.at[m % 2]), (own_s.at[m], own_ref.at[m])], out_sems, 2 * m
        )
    for copy in stores:
        copy.wait()


def attention_grads(place, parts, one, two, pairs):
    _, rows, width = parts[0].shape
    heads = one[0].shape[-1]
    wide = one[1].shape[-1]
    blocks = (pairs, width // (2 * pairs), wide + heads)
    return pl.pallas_call(
        attention_grads_kernel,
        in_specs=[SMEM] + [ANY] * 8,
        out_specs=[ANY] * 3,
        out_shape=[shape_of((pairs // 2,) + blocks[1:])] * 2 + [shape_of(blocks)],
        scratch_shapes=[pltpu.VMEM((4 * rows, width), BF16)] * 2
        + [pltpu.VMEM((4 * rows, heads), BF16), pltpu.VMEM((4 * rows, wide), BF16)]
        + [pltpu.VMEM((heads, width), F32)]
        + [pltpu.VMEM(blocks, BF16)] * 2
        + [pltpu.SemaphoreType.DMA((16,)), pltpu.SemaphoreType.DMA((2 * pairs,))],
        compiler_params=PARAMS,
        cost_estimate=cost(7e9, 16 << 20),
        name="attention_grads",
    )(place, *parts, *one, *two)


def results_kernel(
    mixed_ref,
    pg_ref,
    act_ref,
    grad_ref,
    dense_ref,
    shrink_ref,
    project_ref,
    expand_ref,
    mine_ref,
    theirs_ref,
    mixed_s,
    pg_s,
    act_s,
    grad_s,
    dense_s,
    shrink_s,
    project_s,
    expand_s,
    out_s,
    in_sems,
    out_sems,
    *,
    first,
):
    rows = mixed_ref.shape[1]
    theirs = pl.ds((first + 1) * rows, rows)
    mine = pl.ds(first * rows, rows)
    loads = copies(
        [
            (shrink_ref, shrink_s),
            (act_ref.at[theirs, :], act_s.at[1]),
            (mixed_ref, mixed_s),
            (dense_ref, dense_s),
            (expand_ref, expand_s),
            (grad_ref.at[theirs, :], grad_s.at[1]),
            (pg_ref, pg_s),
            (project_ref, project_s),
            (act_ref.at[mine, :], act_s.at[0]),
            (grad_ref.at[mine, :], grad_s.at[0]),
        ],
        in_sems,
    )
    stores = []
    for at, (piece, gradient, waits) in enumerate(
        ((1, 0, loads[:4]), (1, 1, loads[4:8]), (0, 0, loads[8:9]), (0, 1, loads[9:]))
    ):
        for copy in waits:
            copy.wait()
        if gradient:
            total = nt(grad_s[piece], expand_s[...]) + nt(pg_s[piece], project_s[...])
        else:
            total = nn(act_s[piece], shrink_s[...]) + nn(mixed_s[piece], dense_s[...])
        out_s[at] = total.astype(BF16)
        out_ref = theirs_ref if piece else mine_ref
        stores += copies([(out_s.at[at], out_ref.at[gradient])], out_sems, at)
    for copy in stores:
        copy.wait()


def results(mixed, pg, act, grad, dense, shrink, project, expand, first):
    _, rows, heads = mixed.shape
    wide = pg.shape[-1]
    units = act.shape[-1]
    width = dense.shape[1]
    return pl.pallas_call(
        functools.partial(results_kernel, first=first),
        in_specs=[ANY] * 8,
        out_specs=[ANY] * 2,
        out_shape=[shape_of((2, rows, width))] * 2,
        scratch_shapes=[pltpu.VMEM(mixed.shape, BF16), pltpu.VMEM(pg.shape, BF16)]
        + [pltpu.VMEM((2, rows, units), BF16)] * 2
        + [pltpu.VMEM(w.shape, BF16) for w in (dense, shrink, project, expand)]
        + [pltpu.VMEM((4, rows, width), BF16)]
        + [pltpu.SemaphoreType.DMA((10,)), pltpu.SemaphoreType.DMA((4,))],
        compiler_params=PARAMS,
        cost_estimate=cost(8e9, 16 << 20),
        name="results",
    )(mixed, pg, act, grad, dense, shrink, project, expand)


def exchange(value, axis, size, offset):
    return lax.ppermute(value, axis, [(i, i ^ offset) for i in range(size)])


def sum_over(value, axis, size, offset=1):
    while offset < size:
        value = value + exchange(value, axis, size, offset)
        offset *= 2
    return value


def slots(value, index, size):
    row = lax.broadcasted_iota(jnp.int32, (size, 1), 0)
    return jnp.where(row == index, value[None, :], 0.0)


def after(values, *first):
    return lax.optimization_barrier(tuple(values) + first)[: len(values)]


def hop(value, size, offset):
    return exchange(value, "fsdp", size, offset)


class Gather:
    def __init__(self, block, size, near=True):
        self.own, self.size = block, size
        self.far = hop(block, size, 4)
        self.near = hop(block, size, 1) if near else None
        self.far_near = None

    def second(self, *first, near=True):
        own, far = after((self.own, self.far), *first) if first else (self.own, self.far)
        self.pair = hop(jnp.stack([own, far]), self.size, 2)
        if near and self.far_near is None:
            self.far_near = hop(far, self.size, 1)

    def second_near(self):
        self.far_near = hop(self.far, self.size, 1)

    def third(self, *first):
        (pair,) = after((self.pair,), *first) if first else (self.pair,)
        self.pair_near = hop(pair, self.size, 1)

    def blocks(self, *first):
        every = (self.own, self.near, self.far, self.far_near, self.pair, self.pair_near)
        return after(every, *first) if first else every


class Scatter:
    def __init__(self, near, own, size, late=None):
        self.own, self.size = own, size
        self.near = hop(near, size, 1)
        self.late = self.near if late is None else hop(late, size, 1)
        self.start = 2 if late is None else 0

    def second(self, *first):
        near, own = after((self.near, self.own), *first)
        near, own = near[self.start : self.start + 2], own[2:]
        self.pair = hop((own.astype(F32) + near.astype(F32)).astype(BF16), self.size, 2)
        return self.near

    def third(self, *first):
        pair, near = after((self.pair, self.late), *first) if first else (self.pair, self.late)
        total = self.own[1].astype(F32) + near[1].astype(F32) + pair[1].astype(F32)
        self.far = hop(total.astype(BF16), self.size, 4)
        return pair

    def terms(self):
        return self.own, self.late, self.pair, self.far

    def total(self):
        return sum(term.astype(F32) for term in (self.own[0], self.late[0], self.pair[0], self.far))


def row_of(value):
    return jnp.broadcast_to(value, (value.shape[0], 128)).T[:1, :]


def block_total(own_ref, late_ref, pair_ref, far_ref, columns):
    total = own_ref[:, columns].astype(F32) + late_ref[:, columns].astype(F32)
    return total + pair_ref[:, columns].astype(F32) + far_ref[:, columns].astype(F32)


def finish_project_kernel(
    own_ref, late_ref, pair_ref, far_ref, w_ref, sum_ref, vector_ref, grad_ref, dense_ref, part_ref
):
    wide = w_ref.shape[1]
    heads = wide // (3 * HD)
    gain, shift = column(vector_ref[0:1, :]), column(vector_ref[1:2, :])
    first = second = 0.0
    for head in range(heads):
        for part in range(3):
            at = (part * heads + head) * HD
            to = (head * 3 + part) * HD
            total = block_total(own_ref, late_ref, pair_ref, far_ref, slice(at, at + HD))
            weight = w_ref[:, to : to + HD].astype(F32)
            sums = sum_ref[:, at : at + HD]
            grad_ref[:, to : to + HD] = gain * total + shift * sums
            first = first + jnp.sum(weight * total, axis=1, keepdims=True)
            second = second + jnp.sum(weight * sums, axis=1, keepdims=True)
    part_ref[0:1, :] = row_of(first)
    part_ref[1:2, :] = row_of(second)
    rows, width = dense_ref.shape
    across = width // 4
    total = block_total(own_ref, late_ref, pair_ref, far_ref, slice(wide, wide + across))
    for j in range(4):
        dense_ref[:, j * across : (j + 1) * across] = total[j * rows : (j + 1) * rows, :]


def finish_project(terms, weight, sums, vectors, rows):
    width = weight.shape[0] * 8
    lead = pl.BlockSpec((None, weight.shape[0], width), lambda i: (0, 0, 0))
    whole = [
        pl.BlockSpec(shape, lambda i: (0, 0))
        for shape in (terms[3].shape, weight.shape, sums.shape, vectors.shape)
    ]
    outs = (weight.shape, (rows, width), (2, weight.shape[0]))
    return pl.pallas_call(
        finish_project_kernel,
        grid=(1,),
        in_specs=[lead] * 3 + whole,
        out_specs=[pl.BlockSpec(shape, lambda i: (0, 0)) for shape in outs],
        out_shape=[shape_of(shape, F32) for shape in outs],
        compiler_params=PARAMS,
        cost_estimate=cost(0, 4 << 20),
        name="finish_project",
    )(*terms, weight, sums, vectors)


def finish_expand_kernel(
    own_ref, late_ref, pair_ref, far_ref, w_ref, sum_ref, vector_ref, grad_ref, part_ref
):
    gain, shift = column(vector_ref[2:3, :]), column(vector_ref[3:4, :])
    total = block_total(own_ref, late_ref, pair_ref, far_ref, slice(None))
    weight = w_ref[...].astype(F32)
    grad_ref[...] = gain * total + shift * sum_ref[...]
    part_ref[0:1, :] = row_of(jnp.sum(weight * total, axis=1, keepdims=True))
    part_ref[1:2, :] = row_of(jnp.sum(weight * sum_ref[...], axis=1, keepdims=True))


def finish_expand(terms, weight, sums, vectors):
    lead = pl.BlockSpec((None,) + weight.shape, lambda i: (0, 0, 0))
    whole = [
        pl.BlockSpec(shape, lambda i: (0, 0))
        for shape in (terms[3].shape, weight.shape, sums.shape, vectors.shape)
    ]
    outs = (weight.shape, (2, weight.shape[0]))
    return pl.pallas_call(
        finish_expand_kernel,
        grid=(1,),
        in_specs=[lead] * 3 + whole,
        out_specs=[pl.BlockSpec(shape, lambda i: (0, 0)) for shape in outs],
        out_shape=[shape_of(shape, F32) for shape in outs],
        compiler_params=PARAMS,
        cost_estimate=cost(0, 4 << 20),
        name="finish_expand",
    )(*terms, weight, sums, vectors)


def finish_tokens_kernel(
    mine_ref, near_ref, far_ref, inputs_ref, cotangent_ref, keep_ref, bias_ref, out_ref, grad_ref
):
    def total(which):
        return (
            mine_ref[which].astype(F32) + near_ref[which].astype(F32) + far_ref[which].astype(F32)
        )

    features = inputs_ref[...].astype(F32)
    out_ref[...] = (features + total(0) + bias_ref[...]).astype(BF16)
    normed, rate = normalise(features)
    grad = total(1)
    inner = jnp.mean(grad * normed, axis=-1, keepdims=True)
    centre = jnp.mean(grad, axis=-1, keepdims=True)
    upstream = cotangent_ref[...].astype(F32) * keep_ref[...]
    grad_ref[...] = (upstream + rate * (grad - centre - normed * inner)).astype(BF16)


def finish_tokens(mine, near, far, inputs, cotangent, keep, bias):
    rows, width = inputs.shape
    step = rows // 4
    both = pl.BlockSpec((2, step, width), lambda i: (0, i, 0))
    block = pl.BlockSpec((step, width), lambda i: (i, 0))
    return pl.pallas_call(
        finish_tokens_kernel,
        grid=(4,),
        in_specs=[both] * 3
        + [block] * 2
        + [pl.BlockSpec((step, 1), lambda i: (i, 0)), pl.BlockSpec((1, width), lambda i: (0, 0))],
        out_specs=[block] * 2,
        out_shape=[shape_of((rows, width))] * 2,
        compiler_params=PARAMS,
        cost_estimate=cost(0, 12 << 20),
        name="finish_tokens",
    )(mine, near, far, inputs, cotangent, keep, bias)


def by_part(array):
    shape = array.shape
    array = array.reshape(shape[:-1] + (shape[-1] // (3 * HD), 3, HD))
    return jnp.swapaxes(array, -3, -2).reshape(shape)


def by_head(array):
    shape = array.shape
    array = array.reshape(shape[:-1] + (3, shape[-1] // (3 * HD), HD))
    return jnp.swapaxes(array, -3, -2).reshape(shape)


def gathered(weight):
    return lax.all_gather(weight, "fsdp", axis=0, tiled=True)


def folded(weight, gain, shift, offset):
    weight = gathered(weight).astype(F32)
    bias = offset[None, :] + jnp.sum(weight * shift[:, None], axis=0, keepdims=True)
    return (weight * gain[:, None]).astype(BF16), bias


def whole_rows(own, near):
    whole = jnp.stack([own, near], axis=1).astype(F32)[jnp.array([0, 2, 1, 3])]
    return whole.reshape(-1, whole.shape[-1])


def scattered(value):
    return lax.psum_scatter(value, "fsdp", scatter_dimension=0, tiled=True)


def local(
    inputs,
    segments,
    cotangent,
    attention_gain,
    attention_shift,
    feedforward_gain,
    feedforward_shift,
    project_weight,
    project_bias,
    dense_weight,
    dense_bias,
    expand_weight,
    expand_bias,
    shrink_weight,
    shrink_bias,
):
    size = lax.axis_size("fsdp")
    across = lax.axis_size("tensor")
    rows, width = inputs.shape
    assert across == 4 and 2 * rows == SEQ_LEN and segments.shape[0] == 2 * SEQ_LEN
    index = lax.axis_index("fsdp")
    rank = lax.axis_index("tensor")
    core = (rank % 2).astype(jnp.int32)[None]
    chip = rank // 2
    block = width // size
    pairs = 4
    direct = size == 2 * pairs
    place = (index if direct else index * 0).astype(jnp.int32)[None]

    own_labels = lax.dynamic_slice_in_dim(segments, rank * rows, rows, 0)
    keep = (own_labels != 0).astype(F32)[:, None]
    if direct:
        first = Gather(expand_weight, size)
    early = after((inputs,), first.near)[0] if direct else inputs
    own, bias_grad = prepare(early, cotangent, keep)

    small = jnp.concatenate(
        [
            attention_gain,
            attention_shift,
            feedforward_gain,
            feedforward_shift,
            dense_bias + shrink_bias,
        ]
    )
    piece = small.shape[0] // 5
    small = slots(small, rank, across)
    small_far = small + exchange(small, "tensor", across, 2)
    (small_far,) = after((small_far,), own)
    small = small_far + exchange(small_far, "tensor", across, 1)
    own_vectors = jnp.swapaxes(small.reshape(across, 5, piece), 0, 1).reshape(5, block)
    counts = (5 * block, project_bias.shape[0], expand_bias.shape[0])
    packed = jnp.concatenate(
        [own_vectors.reshape(-1), project_bias.astype(F32), expand_bias.astype(F32)]
    )
    packed = slots(packed, index, size)
    packed_near = packed + exchange(packed, "fsdp", size, 1)
    if direct:
        (packed_near,) = after((packed_near,), first.far, first.near, own)
    if direct:
        packed_far = packed_near + exchange(packed_near, "fsdp", size, 4)
        packed = packed_far + exchange(packed_far, "fsdp", size, 2)
    else:
        packed = sum_over(packed_near, "fsdp", size, 2)
    vectors = jnp.swapaxes(packed[:, : counts[0]].reshape(size, 5, block), 0, 1).reshape(5, width)
    project_offset = by_part(packed[:, counts[0] : counts[0] + counts[1]].reshape(-1))
    expand_offset = packed[:, counts[0] + counts[1] :].reshape(-1)

    (own,) = after((own,), small_far)

    def chip_pair(value):
        return exchange(value, "tensor", across, 1)

    def other_chip(value):
        return exchange(value, "tensor", across, 2)

    labels = segments.reshape(2, SEQ_LEN)
    labels = jnp.where(chip == 0, labels, labels[::-1])
    places = jnp.arange(SEQ_LEN, dtype=jnp.int32)[None, :]
    marks = jnp.where(labels != 0, labels, -1 - places)
    across_chip = other_chip(own)
    own_near, _ = after((own, small), packed_far) if direct else (own, small)
    partner = chip_pair(own_near)
    if direct:
        first.second_near()
        (pack_weight,) = after((project_weight,), first.far_near)
        packed_weights, *tables = pack(pack_weight, dense_weight, rotary_turns())
        (near_block,) = after((shrink_weight,), packed_near)
        near_block = hop(near_block, size, 1)
        first.second(packed)
        (far_block,) = after((shrink_weight,), packed)
        second = Gather(far_block, size, False)
        second.near = near_block
        second.second(first.pair, first.far_near, packed_weights, near_block)
        (far_block,) = after((packed_weights,), second.far)
        third = Gather(far_block, size, False)
        first.third(first.far_near, packed_weights)
        expand, expand_row = join_expand(
            place,
            first.blocks(),
            vectors[2][None, :],
            vectors[3][None, :],
            expand_offset[None, :],
        )
        (across_chip,) = after((across_chip,), second.pair, third.far, expand_row)
        (expand,) = after((expand,), second.pair, second.far_near, third.far, partner)
        second.third(expand)
        third.second(second.pair, near=False)
    else:
        _, *tables = pack(project_weight, dense_weight, rotary_turns())
        expand, expand_row = folded(expand_weight, vectors[2], vectors[3], expand_offset)
        project, project_row = folded(
            by_part(project_weight), vectors[0], vectors[1], project_offset
        )
        dense = gathered(dense_weight)
        shrink = gathered(shrink_weight)
    parts = (own, partner, across_chip, chip_pair(across_chip))

    active, slope, shrink_near, shrink_own = hidden_layer(place, parts, expand, expand_row, pairs)
    if direct:
        shrink_sums = Scatter(shrink_near, shrink_own, size)
        near_block, far_block = after((packed_weights, third.far), shrink_own)
        third.near = hop(near_block, size, 1)
        third.far_near = hop(far_block, size, 1)
        third.third(shrink_own)
        shrink = join(place, second.blocks(shrink_own))
    hidden_grad, expand_near, expand_own, expand_offset_grad = unhidden_layer(
        place, parts, shrink, slope, pairs
    )
    if direct:
        expand_sums = Scatter(expand_near, expand_own, size)
        project, dense, project_row = join_project(
            place,
            third.blocks(expand_own),
            vectors[0][None, :],
            vectors[1][None, :],
            project_offset[None, :],
        )
    else:
        (project,) = after((project,), expand_own)

    def attend(sequence):
        at = slice(2 * sequence, 2 * sequence + 2)
        return attention(core, parts[at], project, project_row, dense, marks[sequence], tables)

    two = attend(1)
    weights = (dense, shrink, project, expand)
    act = active
    if direct:
        ready = shrink_sums.second(two[2])
        (act,) = after((active,), ready)
    far_mine, far_theirs = results(two[0], two[1], act, hidden_grad, *weights, first=2)
    far = chip_pair(far_theirs)
    far_sum = (far_mine.astype(F32) + far.astype(F32)).astype(BF16)
    far = other_chip(far_sum)
    if direct:
        ready = shrink_sums.third(far_mine)
        more = expand_sums.second(far_mine)
        (project,) = after((project,), ready, more)
    else:
        (project,) = after((project,), far_mine)
    one = attend(0)
    if direct:
        ready = expand_sums.third(one[2], far_sum)
        (pair_grads,) = after((one[1],), ready, shrink_sums.far, far_sum)
        one = (one[0], pair_grads, one[2])
    both_near, both_late, both_own = attention_grads(place, parts, one[:2], two[:2], pairs)
    project_offset_grad = one[2] + two[2]
    wide = project_offset_grad.shape[1]
    units = expand_offset_grad.shape[1]
    few = dense_weight.shape[0]
    totals = jnp.concatenate([project_offset_grad, expand_offset_grad, bias_grad], axis=1)
    (totals,) = after((totals,), both_own)
    totals = totals_near = totals + exchange(totals, "fsdp", size, 1)
    if direct:
        totals = totals_pair = totals + exchange(totals, "fsdp", size, 2)
        totals = totals + exchange(totals, "fsdp", size, 4)
    else:
        totals = sum_over(totals, "fsdp", size, 2)
    project_totals = totals[:, :wide]
    expand_totals = totals[:, wide : wide + units]
    bias_totals = totals[0, wide + units :]

    act = active
    if direct:
        both_sums = Scatter(both_near, both_own, size, both_late)
        (act,) = after((active,), both_own, expand_sums.far)
    near_mine, near_theirs = results(one[0], one[1], act, hidden_grad, *weights, first=0)
    def mine(vector, count, start):
        return lax.dynamic_slice_in_dim(vector, start * count, count, 0)

    own_rows = own_vectors[:4]
    if direct:
        both_sums.second(near_mine, totals)
        shrink_sum = shrink_sums.total()
        ready = both_sums.third(shrink_sum)
        (expand_totals,) = after((expand_totals,), ready)
        expand_gradient, expand_parts = finish_expand(
            expand_sums.terms(), expand_weight, expand_totals, own_rows
        )
        far, near_mine, near_theirs = after((far, near_mine, near_theirs), ready)
        near = chip_pair(near_theirs)
        output, inputs_gradient = finish_tokens(
            near_mine, near, far, inputs, cotangent, keep, vectors[4][None, :]
        )
        (project_totals,) = after((project_totals,), output, expand_parts)
        project_gradient, dense_sum, project_parts = finish_project(
            both_sums.terms(), project_weight, project_totals, own_rows, few
        )
        partial = [project_parts, expand_parts]
    else:
        near = chip_pair(near_theirs)
        output, inputs_gradient = finish_tokens(
            near_mine, near, far, inputs, cotangent, keep, vectors[4][None, :]
        )
        shrink_sum = scattered(whole_rows(shrink_own, shrink_near))
        expand_sum = scattered(whole_rows(expand_own, expand_near))
        both = whole_rows(both_own, jnp.concatenate([both_late, both_near]))
        project_sum = scattered(both[:, :wide])
        dense_sum = both[:, wide:].reshape(2 * pairs, 4, -1, width // 4)
        dense_sum = scattered(jnp.swapaxes(dense_sum, 1, 2).reshape(-1, width))
        columns = own_rows[:, :, None]
        project_gradient = by_head(columns[0] * project_sum + columns[1] * project_totals)
        expand_gradient = columns[2] * expand_sum + columns[3] * expand_totals
        own_project = by_part(project_weight).astype(F32)
        own_expand = expand_weight.astype(F32)
        partial = [
            jnp.sum(term, axis=1)[None, :]
            for term in (
                own_project * project_sum,
                own_project * project_totals,
                own_expand * expand_sum,
                own_expand * expand_totals,
            )
        ]
    partial = jnp.concatenate(partial + [mine(bias_totals, block, index)[None, :]])
    partial = sum_over(partial, "tensor", across)
    partial = lax.dynamic_slice_in_dim(partial, rank * piece, piece, 1)
    return (
        output,
        inputs_gradient,
        partial[0],
        partial[1],
        partial[2],
        partial[3],
        project_gradient,
        mine(by_head(project_totals[0]), project_bias.shape[0], index),
        dense_sum,
        partial[4],
        expand_gradient,
        mine(expand_totals[0], expand_bias.shape[0], index),
        shrink_sum,
        partial[4],
    )


def solution(mesh):
    in_specs = (
        P(("fsdp", "tensor"), None),
        P("fsdp"),
        P(("fsdp", "tensor"), None),
        P(("fsdp", "tensor")),
        P(("fsdp", "tensor")),
        P(("fsdp", "tensor")),
        P(("fsdp", "tensor")),
        P("fsdp", "tensor"),
        P(("tensor", "fsdp")),
        P(("tensor", "fsdp"), None),
        P(("fsdp", "tensor")),
        P("fsdp", "tensor"),
        P(("tensor", "fsdp")),
        P(("tensor", "fsdp"), None),
        P(("fsdp", "tensor")),
    )
    out_specs = (
        P(("fsdp", "tensor"), None),
        P(("fsdp", "tensor"), None),
        P(("fsdp", "tensor")),
        P(("fsdp", "tensor")),
        P(("fsdp", "tensor")),
        P(("fsdp", "tensor")),
        P("fsdp", "tensor"),
        P(("tensor", "fsdp")),
        P(("tensor", "fsdp"), None),
        P(("fsdp", "tensor")),
        P("fsdp", "tensor"),
        P(("tensor", "fsdp")),
        P(("tensor", "fsdp"), None),
        P(("fsdp", "tensor")),
    )
    return jax.shard_map(local, mesh=mesh, in_specs=in_specs, out_specs=out_specs, check_vma=False)
```
